32 devices in a mesh: dp: 8 (over z, y), tensor: 4 (over x, core).
Axes of the slice: x: 2, y: 2, z: 4, core: 2. Of those that a mesh axis runs over, the one named last changes fastest.
Arguments:
- tokens_in: bfloat16 [5120, 512], P(('dp', 'tensor')), may hold values from -6 to 6
- grad_out: bfloat16 [5120, 512], P(('dp', 'tensor')), may hold values from -6 to 6
- enc_states: bfloat16 [512, 512], P('dp'), may hold values from -6 to 6
- parents: int32 [40], P('dp'), may hold values from -1 to 39, as said below
- tree_ids: int32 [40], P('dp'), may hold values from 0 to 1, as said below
- timesteps: int32 [2], replicated, may hold values from 0 to 49
- time_table: bfloat16 [50, 512], P(None, 'dp'), may hold values from -3 to 3
- norm_self: bfloat16 [512], P('dp'), may hold values from 0.25 to 1.75
- w_query: bfloat16 [512, 512], P('dp', 'tensor'), may hold values from -0.5 to 0.5
- w_key: bfloat16 [512, 512], P('dp', 'tensor'), may hold values from -0.25 to 0.25
- w_value: bfloat16 [512, 512], P('dp', 'tensor'), may hold values from -0.25 to 0.25
- w_out: bfloat16 [512, 512], P('tensor', 'dp'), may hold values from -1 to 1
- norm_cross: bfloat16 [512], P('dp'), may hold values from 0.25 to 1.75
- c_query: bfloat16 [512, 512], P('dp', 'tensor'), may hold values from -0.5 to 0.5
- c_key: bfloat16 [512, 512], P('dp', 'tensor'), may hold values from -0.25 to 0.25
- c_value: bfloat16 [512, 512], P('dp', 'tensor'), may hold values from -0.25 to 0.25
- c_out: bfloat16 [512, 512], P('tensor', 'dp'), may hold values from -0.75 to 0.75
- norm_ffn: bfloat16 [512], P('dp'), may hold values from 0.25 to 1.75
- w_hidden: bfloat16 [512, 2048], P('dp', 'tensor'), may hold values from -0.25 to 0.25
- w_back: bfloat16 [2048, 512], P('tensor', 'dp'), may hold values from -0.1875 to 0.1875
Outputs:
- output: bfloat16 [5120, 512], P(('dp', 'tensor'))
- grad_inp: float32 [5120, 512], P(('dp', 'tensor'))
- grad_enc: float32 [512, 512], P('dp')
- grad_table: float32 [50, 512], P(None, 'dp')
- grad_norm_self: float32 [512], P('dp')
- grad_w_query: float32 [512, 512], P('dp', 'tensor')
- grad_w_key: float32 [512, 512], P('dp', 'tensor')
- grad_w_value: float32 [512, 512], P('dp', 'tensor')
- grad_w_out: float32 [512, 512], P('tensor', 'dp')
- grad_norm_cross: float32 [512], P('dp')
- grad_c_query: float32 [512, 512], P('dp', 'tensor')
- grad_c_key: float32 [512, 512], P('dp', 'tensor')
- grad_c_value: float32 [512, 512], P('dp', 'tensor')
- grad_c_out: float32 [512, 512], P('tensor', 'dp')
- grad_norm_ffn: float32 [512], P('dp')
- grad_w_hidden: float32 [512, 2048], P('dp', 'tensor')
- grad_w_back: float32 [2048, 512], P('tensor', 'dp')
The draws below stay inside these ranges and needn't reach their ends.
Inputs may be any that keep to these rules, and one draw needn't show every extreme that they name: `parents`: tree s fills the 20 blocks (s * 20 + 10 + j) mod 40, j = 0 onward, in that order. Its first 8 blocks are a trunk, each the parent of the next, the first with parent -1; the next 4 blocks are branches whose parent is the last trunk block; the remaining blocks are leaves, each the child of one branch, every branch with 2 leaves. `tree_ids`: all blocks of one tree carry the same id, and the trees carry different ids.
All inputs are finite; a program needn't handle non-finite values.
Results may differ from the reference program's by a relative error of at most 0.023.
Values may be sent and summed in bfloat16 or wider, within the bound.
No kernel may reach another device: no remote copies, remote signals or barrier semaphores. Data moves between devices by JAX's collectives and lax.ppermute only.
A program may use at most 128 MiB of HBM per device.

```python
import jax
import jax.numpy as jnp
from jax import lax

D = 512
HEADS = 8
HD = 64
FF = 2048
ENC = 256
BLOCK = 128
TRUNK_BLKS = 8
BRANCHES = 4
LEAVES = 2
STEPS = 50
TREE_BLKS = 20
LEAD = 10
TREES = 2
NBLK = 40
TOKENS = 5120


def draw_parents(key, part):
    tree_keys = jax.random.split(jax.random.fold_in(key, 7), TREES)

    def one_tree(tree_key):
        trunk_rel = jnp.arange(TRUNK_BLKS, dtype=jnp.int32) - 1
        branch = jnp.full((BRANCHES,), TRUNK_BLKS - 1, jnp.int32)
        leaves = TRUNK_BLKS + jax.random.permutation(tree_key, BRANCHES * LEAVES).astype(jnp.int32) // LEAVES
        return jnp.concatenate([trunk_rel, branch, leaves.astype(jnp.int32)])
    relative = jax.vmap(one_tree)(tree_keys)
    starts = (jnp.arange(TREES, dtype=jnp.int32) * TREE_BLKS)[:, None]
    logical = jnp.where(relative >= 0, (relative + starts + LEAD) % NBLK, -1).reshape(-1).astype(jnp.int32)
    return jnp.roll(logical, LEAD).astype(jnp.int32)


def draw_tree_ids(key, part):
    tree_order = jax.random.permutation(jax.random.fold_in(key, 9), TREES).astype(jnp.int32)
    return jnp.roll(jnp.repeat(tree_order, TREE_BLKS), LEAD).astype(jnp.int32)


def levels(stream_key, shape, shards, smallest, largest):
    level = 1.0
    for dim, shards_of in shards:
        draws = jax.random.uniform(jax.random.fold_in(jax.random.fold_in(stream_key, 6), dim), (shards_of,), jnp.float32, smallest / len(shards), largest / len(shards))
        level = level * jnp.repeat(jnp.exp(draws), shape[dim] // shards_of).reshape((-1,) + (1,) * (len(shape) - 1 - dim))
    return level


def normal_values(own_key, shape, scale, most, cuts=(), kind=jnp.bfloat16):
    drawn = jax.random.normal(own_key, shape, jnp.float32) * scale
    if len(cuts) > 0:
        drawn = levels(own_key, shape, cuts, -0.22, 0.18) * drawn
    return jnp.clip(drawn, min=-most, max=most).astype(kind)


def setup_inputs(seed: int = 0) -> dict:
    keys = jax.random.split(jax.random.key(seed), 21)
    return {
        "tokens_in": normal_values(keys[0], (TOKENS, D), 1.0, 6.0, ((0, 32),)),
        "grad_out": normal_values(keys[1], (TOKENS, D), 1.0, 6.0, ((0, 32),)),
        "enc_states": normal_values(keys[2], (TREES * ENC, D), 1.0, 6.0, ((0, 8),)),
        "parents": draw_parents(jax.random.fold_in(keys[20], 71), 0),
        "tree_ids": draw_tree_ids(jax.random.fold_in(keys[20], 71), 0),
        "timesteps": jax.random.randint(keys[5], (TREES,), 0, STEPS).astype(jnp.int32),
        "time_table": normal_values(keys[6], (STEPS, D), 0.5, 3.0, ((1, 8),)),
        "norm_self": jnp.clip(1.0 + 0.15 * jax.random.normal(keys[7], (D,), jnp.float32), 0.25, 1.75).astype(jnp.bfloat16),
        "w_query": normal_values(keys[8], (D, D), (D // 4) ** -0.5, 0.5, ((0, 8), (1, 4))),
        "w_key": normal_values(keys[9], (D, D), D ** -0.5, 0.25, ((0, 8), (1, 4))),
        "w_value": normal_values(keys[10], (D, D), D ** -0.5, 0.25, ((0, 8), (1, 4))),
        "w_out": normal_values(keys[11], (D, D), (D // 16) ** -0.5, 1.0, ((0, 4), (1, 8))),
        "norm_cross": jnp.clip(1.0 + 0.15 * jax.random.normal(keys[12], (D,), jnp.float32), 0.25, 1.75).astype(jnp.bfloat16),
        "c_query": normal_values(keys[13], (D, D), (D // 4) ** -0.5, 0.5, ((0, 8), (1, 4))),
        "c_key": normal_values(keys[14], (D, D), D ** -0.5, 0.25, ((0, 8), (1, 4))),
        "c_value": normal_values(keys[15], (D, D), D ** -0.5, 0.25, ((0, 8), (1, 4))),
        "c_out": normal_values(keys[16], (D, D), (D // 8) ** -0.5, 0.75, ((0, 4), (1, 8))),
        "norm_ffn": jnp.clip(1.0 + 0.15 * jax.random.normal(keys[17], (D,), jnp.float32), 0.25, 1.75).astype(jnp.bfloat16),
        "w_hidden": normal_values(keys[18], (D, FF), D ** -0.5, 0.25, ((0, 8), (1, 4))),
        "w_back": normal_values(keys[19], (FF, D), (FF // 2) ** -0.5, 0.1875, ((0, 4), (1, 8))),
    }


@jax.custom_vjp
def low(v):
    return lax.optimization_barrier(v.astype(jnp.bfloat16)).astype(jnp.float32)

@jax.custom_vjp
def low_back(v):
    return v

def low_keep(v):
    return (low(v), None)

def low_pass(kept, grad):
    return (grad,)

def back_keep(v):
    return (v, None)

def back_low(kept, grad):
    return (low(grad),)
low.defvjp(low_keep, low_pass)
low_back.defvjp(back_keep, back_low)
highest = lax.Precision.HIGHEST
eps = 1e-05

def matmul_high(left_op, right_op):
    return jnp.dot(left_op, right_op, precision=highest)

def layer_norm(row_vals, gain_vec):
    average = lax.optimization_barrier(jnp.mean(row_vals, axis=-1, keepdims=True))
    centered = row_vals - average
    variance = lax.optimization_barrier(jnp.mean(centered * centered, axis=-1, keepdims=True))
    return centered * lax.rsqrt(variance + eps) * gain_vec

def ancestor_table(parent_rel):
    blocks = jnp.arange(TREE_BLKS, dtype=jnp.int32)

    def one_hop(carry, unused):
        current, table_now = carry
        table_now = table_now | (current[:, None] == blocks[None, :])
        safe_idx = jnp.maximum(current, 0)
        upward = jnp.where(current >= 0, parent_rel[safe_idx], -1).astype(jnp.int32)
        return ((upward, table_now), None)
    start_table = blocks[:, None] + blocks[None, :] < 0
    (final_cur, table_done), unused = lax.scan(one_hop, (parent_rel, start_table), None, length=TREE_BLKS)
    return table_done

def token_mask(parent_rel):
    table_done = ancestor_table(parent_rel)
    positions = jnp.arange(TREE_BLKS * BLOCK, dtype=jnp.int32)
    block_of = positions // BLOCK
    upper = table_done[block_of][:, block_of]
    causal = (block_of[:, None] == block_of[None, :]) & (positions[None, :] <= positions[:, None])
    return (upper | causal).astype(jnp.int32)

def attention(query_t, key_t, val_t, mask_t):
    query_count = query_t.shape[0]
    query_heads = query_t.reshape(query_count, HEADS, HD)
    key_heads = key_t.reshape(key_t.shape[0], HEADS, HD)
    val_heads = val_t.reshape(val_t.shape[0], HEADS, HD)
    scores = jnp.einsum('qhd,khd->hqk', query_heads, key_heads, precision=highest) * HD ** (-0.5)
    scores = low_back(scores)
    if mask_t is not None:
        scores = jnp.where(mask_t[None] > 0, scores, -1e+30)
    probs_low = low(jax.nn.softmax(scores, axis=-1))
    mixed_heads = jnp.einsum('hqk,khd->qhd', probs_low, val_heads, precision=highest)
    return mixed_heads.reshape(query_count, HEADS * HD)

def self_tree(pieces):
    query_t, key_t, val_t, mask_t = pieces
    return attention(query_t, key_t, val_t, mask_t)

def cross_tree(pieces):
    query_t, key_t, val_t = pieces
    return attention(query_t, key_t, val_t, None)

def reference(tokens_in, grad_out, enc_states, parents, tree_ids, timesteps, time_table, norm_self, w_query, w_key, w_value, w_out, norm_cross, c_query, c_key, c_value, c_out, norm_ffn, w_hidden, w_back):
    tree_len = TREE_BLKS * BLOCK
    lead_rows = LEAD * BLOCK
    enc_lead = ENC // 2
    tokens_log = jnp.roll(tokens_in, -lead_rows, axis=0)
    grad_log = jnp.roll(grad_out, -lead_rows, axis=0)
    enc_log = jnp.roll(enc_states, -enc_lead, axis=0)
    parents_roll = jnp.roll(parents, -LEAD).astype(jnp.int32)
    parents_log = jnp.where(parents_roll >= 0, (parents_roll - LEAD) % NBLK, -1).astype(jnp.int32)
    ids_log = jnp.roll(tree_ids, -LEAD).astype(jnp.int32)
    slot_tree = ids_log.reshape(TREES, TREE_BLKS)[:, 0].astype(jnp.int32)
    token_steps = jnp.repeat(jnp.take(timesteps, slot_tree, axis=0), tree_len).astype(jnp.int32)
    starts = (jnp.arange(TREES, dtype=jnp.int32) * TREE_BLKS)[:, None]
    parent_rows = parents_log.reshape(TREES, TREE_BLKS).astype(jnp.int32)
    parent_rel = jnp.where(parent_rows >= 0, parent_rows - starts, -1).astype(jnp.int32)
    masks = jax.vmap(token_mask)(parent_rel)

    def by_tree(row_vals):
        return row_vals.reshape(TREES, tree_len, D)

    def forward(tokens_f, enc_f, table_f, gain_self, query_w, key_w, value_w, out_w, gain_cross, cquery_w, ckey_w, cvalue_w, cout_w, gain_ffn, up_w, down_w):
        resid_in = tokens_f + jnp.take(table_f, token_steps, axis=0)
        act_self = low(layer_norm(resid_in, gain_self))
        queries = low_back(low(matmul_high(act_self, query_w)))
        keys_all = low_back(low(matmul_high(act_self, key_w)))
        values_all = low_back(low(matmul_high(act_self, value_w)))
        mixed_self = lax.map(jax.checkpoint(self_tree), (by_tree(queries), by_tree(keys_all), by_tree(values_all), masks))
        attn_out = low_back(low(mixed_self.reshape(TOKENS, D)))
        resid_mid = resid_in + low_back(matmul_high(attn_out, out_w))
        act_cross = low(layer_norm(resid_mid, gain_cross))
        cross_queries = low_back(low(matmul_high(act_cross, cquery_w)))
        enc_keys = low_back(low(matmul_high(enc_f, ckey_w))).reshape(TREES, ENC, D)
        enc_vals = low_back(low(matmul_high(enc_f, cvalue_w))).reshape(TREES, ENC, D)
        mixed_cross = lax.map(jax.checkpoint(cross_tree), (by_tree(cross_queries), enc_keys, enc_vals))
        cross_out = low_back(low(mixed_cross.reshape(TOKENS, D)))
        resid_ffn = resid_mid + low_back(matmul_high(cross_out, cout_w))
        act_ffn = low(layer_norm(resid_ffn, gain_ffn))
        hidden_pre = low_back(matmul_high(act_ffn, up_w))
        hidden_low = low(jax.nn.gelu(hidden_pre, approximate=False))
        return resid_ffn + low_back(matmul_high(hidden_low, down_w))
    floats = [value_in.astype(jnp.float32) for value_in in (tokens_log, enc_log, time_table, norm_self, w_query, w_key, w_value, w_out, norm_cross, c_query, c_key, c_value, c_out, norm_ffn, w_hidden, w_back)]
    output_f, back_fn = jax.vjp(forward, *floats)
    grads = back_fn(grad_log.astype(jnp.float32))
    output_back = jnp.roll(output_f, lead_rows, axis=0).astype(jnp.bfloat16)
    grad_tokens = jnp.roll(grads[0], lead_rows, axis=0)
    grad_encoder = jnp.roll(grads[1], enc_lead, axis=0)
    return (output_back, grad_tokens, grad_encoder, grads[2], grads[3], grads[4], grads[5], grads[6], grads[7], grads[8], grads[9], grads[10], grads[11], grads[12], grads[13], grads[14], grads[15])
```

```python
import jax
import jax.numpy as jnp
from jax import lax
from jax.sharding import PartitionSpec as P

HEADS = 8
TRUNK_BLKS = 8
BRANCHES = 4
LEAVES = 2
eps = 1e-05
bf16 = jnp.bfloat16
f32 = jnp.float32


def layer_norm(row_vals, gain_vec):
    average = jnp.mean(row_vals, axis=-1, keepdims=True)
    centered = row_vals - average
    variance = jnp.mean(centered * centered, axis=-1, keepdims=True)
    inv = lax.rsqrt(variance + eps)
    return centered * inv * gain_vec, inv, centered * inv


def layer_norm_back(grad_act, normed, inv, gain_vec):
    scaled = grad_act * gain_vec
    mean_g = jnp.mean(scaled, axis=-1, keepdims=True)
    mean_gx = jnp.mean(scaled * normed, axis=-1, keepdims=True)
    return inv * (scaled - mean_g - normed * mean_gx)


def gelu_exact(hidden_vals):
    return jax.nn.gelu(hidden_vals, approximate=False)


def mm(a, b):
    return jnp.dot(a, b, preferred_element_type=f32)


def mm_tn(a, b):
    return lax.dot_general(a, b, (((0,), (0,)), ((), ())), preferred_element_type=f32)


def mm_nt(a, b):
    return lax.dot_general(a, b, (((1,), (1,)), ((), ())), preferred_element_type=f32)


def split_heads(row_vals, local_heads):
    return row_vals.reshape(row_vals.shape[0], local_heads, row_vals.shape[1] // local_heads)


def scores_of(query_heads, key_heads, allowed):
    scaling = query_heads.shape[2] ** (-0.5)
    scores = jnp.einsum("qhd,khd->hqk", query_heads, key_heads, preferred_element_type=f32) * scaling
    if allowed is not None:
        scores = jnp.where(allowed[None], scores, -1e30)
    return scores


def attend(queries, key_rows, val_rows, allowed, local_heads):
    query_heads = split_heads(queries, local_heads)
    key_heads = split_heads(key_rows, local_heads)
    val_heads = split_heads(val_rows, local_heads)
    scores = scores_of(query_heads, key_heads, allowed)
    row_peak = jnp.max(scores, axis=-1, keepdims=True)
    exp_terms = jnp.exp(scores - row_peak)
    row_total = jnp.sum(exp_terms, axis=-1, keepdims=True)
    probs_low = (exp_terms / row_total).astype(bf16)
    mixed_heads = jnp.einsum("hqk,khd->qhd", probs_low, val_heads, preferred_element_type=f32)
    return (mixed_heads.reshape(queries.shape), row_peak + jnp.log(row_total))


def attend_back(queries, key_rows, val_rows, allowed, local_heads, log_total, grad_mixed):
    query_heads = split_heads(queries, local_heads)
    key_heads = split_heads(key_rows, local_heads)
    val_heads = split_heads(val_rows, local_heads)
    scaling = query_heads.shape[2] ** (-0.5)
    scores = scores_of(query_heads, key_heads, allowed)
    probs_all = jnp.exp(scores - log_total)
    probs_low = probs_all.astype(bf16)
    grad_heads = split_heads(grad_mixed, local_heads)
    grad_vals = jnp.einsum("hqk,qhd->khd", probs_low, grad_heads, preferred_element_type=f32)
    grad_probs = jnp.einsum("qhd,khd->hqk", grad_heads, val_heads, preferred_element_type=f32)
    inner_sum = jnp.sum(grad_probs * probs_all, axis=-1, keepdims=True)
    grad_scores = (probs_all * (grad_probs - inner_sum)).astype(bf16)
    grad_query = jnp.einsum("hqk,khd->qhd", grad_scores, key_heads, preferred_element_type=f32) * scaling
    grad_keys = jnp.einsum("hqk,qhd->khd", grad_scores, query_heads, preferred_element_type=f32) * scaling
    return (
        grad_query.astype(bf16).reshape(queries.shape),
        grad_keys.reshape(key_rows.shape),
        grad_vals.reshape(val_rows.shape),
    )


def tree_mask(parents, block_len, hops_back, logical_dev):
    blocks_dev = parents.shape[0]
    group = hops_back + 1
    tree_blocks = TRUNK_BLKS + BRANCHES * (1 + LEAVES)
    total_blocks = lax.axis_size("dp") * blocks_dev
    lead_blocks = group // 2 * blocks_dev
    parent_log = jnp.where(parents >= 0, (parents - lead_blocks) % total_blocks, -1)
    query_block = logical_dev * blocks_dev + jnp.arange(blocks_dev, dtype=jnp.int32)
    key_block = (logical_dev - hops_back) * blocks_dev + jnp.arange((hops_back + 1) * blocks_dev, dtype=jnp.int32)
    tree_start = (query_block // tree_blocks * tree_blocks)[:, None]
    query_col = query_block[:, None]
    key_row = key_block[None, :]
    earlier = (
        (key_row >= tree_start)
        & (key_row < query_col)
        & ((key_row - tree_start < TRUNK_BLKS) | (key_row == parent_log[:, None]))
    )
    same_block = key_row == query_col
    positions = jnp.arange(block_len, dtype=jnp.int32)
    causal = positions[None, :] <= positions[:, None]
    allowed = earlier[:, None, :, None] | same_block[:, None, :, None] & causal[None, :, None, :]
    return allowed.reshape(blocks_dev * block_len, (hops_back + 1) * blocks_dev * block_len)


def xor_route(axis, bit):
    return [(i, i ^ bit) for i in range(lax.axis_size(axis))]


def sibling(x):
    return lax.ppermute(x, "tensor", xor_route("tensor", 1))


def across(x):
    return lax.ppermute(x, "tensor", xor_route("tensor", 2))


def pick(x, index, axis):
    return lax.dynamic_index_in_dim(x, index, axis, False)


def halve(partial, low_bit):
    rows = partial.shape[0] // 4
    parts = partial.reshape(2, 2, rows, partial.shape[1])
    kept = pick(parts, low_bit, 1)
    sent = pick(parts, 1 - low_bit, 1).astype(bf16)
    return kept + sibling(sent).astype(f32)


def reduce_half(partial, low_bit):
    chip = halve(partial, low_bit).astype(bf16)
    return chip.astype(f32) + across(chip).astype(f32)


def reduce_own(partial, low_bit, high_bit):
    chip = halve(partial, low_bit)
    sent = pick(chip, 1 - high_bit, 0).astype(bf16)
    return pick(chip, high_bit, 0) + across(sent).astype(f32)


def spread_half(half, low_bit):
    other = sibling(half)
    even = jnp.where(low_bit == 0, half, other)
    odd = jnp.where(low_bit == 0, other, half)
    return jnp.stack([even, odd], axis=1).reshape(-1, half.shape[-1])


def gather_dp(x, groups=None):
    count = lax.axis_size("dp") if groups is None else len(groups[0])
    copies = jnp.broadcast_to(x[None], (count,) + x.shape)
    return lax.all_to_all(copies, "dp", 0, 0, axis_index_groups=groups)


def scatter_dp(full):
    count = lax.axis_size("dp")
    parts = full.astype(bf16).reshape(count, full.shape[0] // count, full.shape[1])
    return jnp.sum(lax.all_to_all(parts, "dp", 0, 0).astype(f32), axis=0)


def on_device(
    tokens_in, grad_out, enc_states, parents, tree_ids, timesteps, time_table, norm_self,
    w_query, w_key, w_value, w_out, norm_cross, c_query, c_key, c_value, c_out, norm_ffn,
    w_hidden, w_back,
):
    count = lax.axis_size("dp")
    tensor = lax.axis_size("tensor")
    local_heads = HEADS // tensor
    blocks_dev = parents.shape[0]
    group = (TRUNK_BLKS + BRANCHES * (1 + LEAVES)) // blocks_dev
    hops_back = group - 1
    me = lax.axis_index("tensor")
    low_bit, high_bit = me % 2, me // 2
    logical_dev = (lax.axis_index("dp") - group // 2) % count
    trees = timesteps.shape[0]
    width = tokens_in.shape[1]
    shard = norm_self.shape[0]
    groups = [
        [(tree * group + member + group // 2) % count for member in range(group)]
        for tree in range(count // group)
    ]
    steps_hot = (jnp.arange(time_table.shape[0], dtype=jnp.int32)[None, :] == timesteps[:, None]).astype(bf16)
    table_rows = mm(steps_hot, time_table).astype(bf16)
    small = jnp.concatenate([norm_self[None], norm_cross[None], norm_ffn[None], table_rows], axis=0)
    qkv_cols = 3 * w_query.shape[1]
    small_rows = -(-small.shape[0] // 16) * 16
    small = jnp.pad(small, ((0, small_rows - small.shape[0]), (0, qkv_cols - shard)))
    first = gather_dp(jnp.concatenate([w_query, w_key, w_value], axis=1))
    small_all = gather_dp(small)
    both = lax.all_gather(jnp.stack([tokens_in, grad_out]), "tensor", axis=1)
    enc_tree = gather_dp(enc_states, groups).reshape(-1, width)
    second = gather_dp(jnp.concatenate([w_out.T, c_query, c_key, c_value, c_out.T], axis=1)).reshape(width, -1)
    third = gather_dp(jnp.concatenate([w_hidden, w_back.T], axis=1)).reshape(width, -1)
    head_cols = w_query.shape[1]
    qkv_full = first.reshape(width, qkv_cols)
    rows_all = small_all[:, :, :shard].transpose(1, 0, 2).reshape(small_rows, width).astype(f32)
    gain_self, gain_cross, gain_ffn = rows_all[0:1], rows_all[1:2], rows_all[2:3]
    tree_index = tree_ids[0]
    tree_hot = jnp.arange(trees, dtype=jnp.int32) == tree_index
    step_id = jnp.sum(jnp.where(tree_hot, timesteps, 0))
    time_row = jnp.sum(jnp.where(tree_hot[:, None], rows_all[3 : 3 + trees], 0.0), axis=0, keepdims=True)
    out_t, cq, ck, cv, co_t = [second[:, i * head_cols : (i + 1) * head_cols] for i in range(5)]
    hidden_cols = w_hidden.shape[1]
    up, down_t = third[:, :hidden_cols], third[:, hidden_cols:]
    resid_all = both[0].astype(f32) + time_row
    act_self, inv_self, normed_self = layer_norm(resid_all, gain_self)
    act_self = act_self.astype(bf16).reshape(-1, width)
    rows_own = tokens_in.shape[0]
    resid_half = pick(resid_all.reshape(2, 2, rows_own, width), low_bit, 1)
    projected = mm(act_self, qkv_full).astype(bf16)
    queries = projected[:, :head_cols]
    local_kv = projected[:, head_cols:]
    token_rows = act_self.shape[0]

    def later(distance):
        return [
            ((l + group // 2) % count, (l + distance + group // 2) % count)
            for l in range(count)
            if l % group + distance < group
        ]

    earlier = [lax.ppermute(local_kv, "dp", later(distance)) for distance in range(hops_back, 0, -1)]
    kv_all = jnp.concatenate(earlier + [local_kv], axis=0)
    key_all, val_all = kv_all[:, :head_cols], kv_all[:, head_cols:]
    allowed = tree_mask(parents, token_rows // blocks_dev, hops_back, logical_dev)
    attn_mixed, lse_self = attend(queries, key_all, val_all, allowed, local_heads)
    attn_low = attn_mixed.astype(bf16)
    resid_mid = resid_half + reduce_half(mm_nt(attn_low, out_t), low_bit)
    act_half, inv_cross, normed_cross = layer_norm(resid_mid, gain_cross)
    act_cross = spread_half(act_half.astype(bf16), low_bit)
    cross_queries = mm(act_cross, cq).astype(bf16)
    enc_keys = mm(enc_tree, ck).astype(bf16)
    enc_vals = mm(enc_tree, cv).astype(bf16)
    cross_mixed, lse_cross = attend(cross_queries, enc_keys, enc_vals, None, local_heads)
    cross_low = cross_mixed.astype(bf16)
    resid_ffn = resid_mid + reduce_half(mm_nt(cross_low, co_t), low_bit)
    act_half, inv_ffn, normed_ffn = layer_norm(resid_ffn, gain_ffn)
    act_ffn = spread_half(act_half.astype(bf16), low_bit)
    hidden_pre = mm(act_ffn, up)
    hidden_act, gelu_back = jax.vjp(gelu_exact, hidden_pre)
    hidden_low = hidden_act.astype(bf16)
    grad_top = both[1].reshape(-1, width)
    grad_hidden = mm(grad_top, down_t)
    grad_pre = gelu_back(grad_hidden)[0].astype(bf16)
    grad_act_ffn = reduce_half(mm_nt(grad_pre, up), low_bit)
    output = (
        pick(resid_ffn, high_bit, 0) + reduce_own(mm_nt(hidden_low, down_t), low_bit, high_bit)
    ).astype(bf16)
    ffn_sums = scatter_dp(jnp.concatenate([mm_tn(act_ffn, grad_pre), mm_tn(grad_top, hidden_low)], axis=1))
    grad_gain_ffn = jnp.sum(pick(grad_act_ffn * normed_ffn, high_bit, 0), axis=0)
    grad_half = pick(both[1].reshape(2, 2, rows_own, width), low_bit, 1).astype(f32)
    grad_resid_ffn = grad_half + layer_norm_back(grad_act_ffn, normed_ffn, inv_ffn, gain_ffn)
    grad_cross_top = spread_half(grad_resid_ffn.astype(bf16), low_bit)
    grad_cross_mixed = mm(grad_cross_top, co_t).astype(bf16)
    grad_cq, grad_enc_keys, grad_enc_vals = attend_back(
        cross_queries, enc_keys, enc_vals, None, local_heads, lse_cross, grad_cross_mixed
    )
    grad_act_cross = reduce_half(mm_nt(grad_cq, cq), low_bit)
    grad_gain_cross = jnp.sum(pick(grad_act_cross * normed_cross, high_bit, 0), axis=0)
    grad_resid_mid = grad_resid_ffn + layer_norm_back(grad_act_cross, normed_cross, inv_cross, gain_cross)
    enc_parts = jnp.concatenate([grad_enc_keys, grad_enc_vals], axis=1).astype(bf16)
    enc_parts = enc_parts.reshape(group, -1, 2 * head_cols)
    enc_sum = jnp.sum(
        lax.all_to_all(enc_parts, "dp", 0, 0, axis_index_groups=groups).astype(f32), axis=0
    ).astype(bf16)
    grad_kv_enc = mm_tn(enc_states, enc_sum)
    enc_part = (mm_nt(enc_sum[:, :head_cols], ck) + mm_nt(enc_sum[:, head_cols:], cv)).astype(bf16)
    enc_part = enc_part.astype(f32) + sibling(enc_part).astype(f32)
    enc_chip = enc_part.astype(bf16)
    grad_enc = enc_chip.astype(f32) + across(enc_chip).astype(f32)
    cross_sums = scatter_dp(
        jnp.concatenate([mm_tn(act_cross, grad_cq), grad_kv_enc, mm_tn(grad_cross_top, cross_low)], axis=1)
    )
    grad_self_top = spread_half(grad_resid_mid.astype(bf16), low_bit)
    grad_attn = mm(grad_self_top, out_t).astype(bf16)
    grad_query, grad_keys, grad_vals = attend_back(
        queries, key_all, val_all, allowed, local_heads, lse_self, grad_attn
    )
    grad_kv = jnp.concatenate([grad_keys, grad_vals], axis=1).reshape(group, token_rows, 2 * head_cols)
    total_kv = grad_kv[hops_back]
    for distance in range(hops_back, 0, -1):
        back = [(b, a) for a, b in later(distance)]
        total_kv = total_kv + lax.ppermute(
            grad_kv[hops_back - distance].astype(bf16), "dp", back
        ).astype(f32)
    grad_qkv = jnp.concatenate([grad_query, total_kv.astype(bf16)], axis=1)
    self_sums = scatter_dp(jnp.concatenate([mm_tn(act_self, grad_qkv), mm_tn(grad_self_top, attn_low)], axis=1))
    grad_act_self = reduce_own(mm_nt(grad_qkv, qkv_full), low_bit, high_bit)
    own_normed, own_inv = pick(normed_self, me, 0), pick(inv_self, me, 0)
    grad_gain_self = jnp.sum(grad_act_self * own_normed, axis=0)
    grad_in = pick(grad_resid_mid, high_bit, 0) + layer_norm_back(grad_act_self, own_normed, own_inv, gain_self)
    vectors = jnp.stack(
        [
            grad_gain_self, grad_gain_cross, grad_gain_ffn, jnp.sum(grad_in, axis=0),
            jnp.full((width,), step_id.astype(f32)),
        ]
    )
    vectors = vectors.reshape(5, count, 1, shard).transpose(1, 2, 0, 3)
    vectors = jnp.broadcast_to(vectors, (count, tensor, 5, shard)).reshape(count * tensor, 5, shard)
    received = lax.all_to_all(vectors, ("dp", "tensor"), 0, 0)
    gain_sums = jnp.sum(received[:, :3], axis=0)
    table_hot = jnp.arange(time_table.shape[0], dtype=jnp.int32)[:, None, None] == received[:, 4].astype(jnp.int32)[None]
    grad_table = jnp.sum(jnp.where(table_hot, received[:, 3][None], 0.0), axis=1)
    gq, gk, gv, go = [self_sums[:, i * head_cols : (i + 1) * head_cols] for i in range(4)]
    gcq, gck, gcv, gco = [cross_sums[:, i * head_cols : (i + 1) * head_cols] for i in range(4)]
    return (
        output, grad_in, grad_enc, grad_table, gain_sums[0], gq, gk, gv, go.T, gain_sums[1],
        gcq, gck, gcv, gco.T, gain_sums[2], ffn_sums[:, :hidden_cols], ffn_sums[:, hidden_cols:].T,
    )


def solution(mesh):
    rows, cols, repl = P(("dp", "tensor"), None), P("dp", "tensor"), P("tensor", "dp")
    in_specs = (
        rows, rows, P("dp", None), P("dp"), P("dp"), P(), P(None, "dp"), P("dp"), cols, cols, cols, repl,
        P("dp"), cols, cols, cols, repl, P("dp"), cols, repl,
    )
    out_specs = (
        rows, rows, P("dp", None), P(None, "dp"), P("dp"), cols, cols, cols, repl, P("dp"), cols, cols, cols,
        repl, P("dp"), cols, repl,
    )
    return jax.shard_map(on_device, mesh=mesh, in_specs=in_specs, out_specs=out_specs, check_vma=False)
```

```python
import jax
import jax.numpy as jnp
from jax import lax
from jax.experimental import pallas as pl
from jax.experimental.pallas import tpu as pltpu
from jax.sharding import PartitionSpec as P

HEADS = 8
TRUNK_BLKS = 8
BRANCHES = 4
LEAVES = 2
eps = 1e-05
bf16 = jnp.bfloat16
f32 = jnp.float32
i32 = jnp.int32
NEG = -1e30


def mm(a, b):
    return lax.dot_general(a, b, (((1,), (0,)), ((), ())), preferred_element_type=f32)


def mm_tn(a, b):
    return lax.dot_general(a, b, (((0,), (0,)), ((), ())), preferred_element_type=f32)


def mm_nt(a, b):
    return lax.dot_general(a, b, (((1,), (1,)), ((), ())), preferred_element_type=f32)


def normalize(v):
    centered = v - jnp.mean(v, axis=-1, keepdims=True)
    inv = lax.rsqrt(jnp.mean(centered * centered, axis=-1, keepdims=True) + eps)
    return centered * inv, inv


def norm_back(grad_act, resid, gain):
    normed, inv = normalize(resid)
    scaled = grad_act * gain
    mean_g = jnp.mean(scaled, axis=-1, keepdims=True)
    mean_gx = jnp.mean(scaled * normed, axis=-1, keepdims=True)
    return inv * (scaled - mean_g - normed * mean_gx), jnp.sum(grad_act * normed, axis=0, keepdims=True)


def shaped(shape, dtype):
    return jax.ShapeDtypeStruct(shape, dtype)


def part(array, width, index):
    return (array, (array.shape[0], width), index)


def run(body, outs, ins, scratch=()):
    arrays, specs = [], []
    for item in ins:
        if isinstance(item, tuple):
            array, block, index = item
            specs.append(pl.BlockSpec(block, lambda i, index=index: (0, index)))
        else:
            array = item
            if array.dtype == i32:
                specs.append(pl.BlockSpec(memory_space=pltpu.SMEM))
            else:
                specs.append(pl.BlockSpec(array.shape, lambda i, r=array.ndim: (0,) * r))
        arrays.append(array)
    out_specs = [pl.BlockSpec(o.shape, lambda i, r=len(o.shape): (0,) * r) for o in outs]
    return pl.pallas_call(
        body,
        grid=(1,),
        out_shape=outs,
        in_specs=specs,
        out_specs=out_specs,
        scratch_shapes=list(scratch),
        compiler_params=pltpu.CompilerParams(vmem_limit_bytes=56 * 1024 * 1024),
    )(*arrays)


def project_body(sc, half, other, w, small, act, q, kv, rows):
    turned = small[...].astype(f32).T
    ids = lax.broadcasted_iota(i32, turned.shape, 0)
    time_row = jnp.sum(jnp.where(ids == 3 + sc[4], turned, 0.0), axis=0, keepdims=True)
    rows[0:3, :] = turned[0:3]
    rows[3:4, :] = time_row
    gain = turned[0:1]
    own_rows = half.shape[1]
    for k in range(4):
        src = half[k] if k < 2 else other[k - 2]
        normed, _ = normalize(src.astype(f32) + time_row)
        act[pl.ds(pl.multiple_of(sc[k], 16), own_rows), :] = (normed * gain).astype(bf16)
    cols = q.shape[1]
    result = mm(act[...], w[...]).astype(bf16)
    q[...] = result[:, :cols]
    kv[...] = result[:, cols:]


def scores_t(keys, queries):
    return mm_nt(keys, queries)


def fill_kv(buffer, parts):
    rows = parts[0].shape[0]
    for index, one in enumerate(parts):
        buffer[index * rows : (index + 1) * rows, :] = one[...]
    done = len(parts) * rows
    if buffer.shape[0] > done:
        buffer[done:, :] = jnp.zeros((buffer.shape[0] - done, buffer.shape[1]), buffer.dtype)


def self_scores(sc, buffer, own, qh, h, hd, block):
    count = qh.shape[0] // block
    col = h * hd
    start = pl.multiple_of(sc[5], block)
    trunk_rows = TRUNK_BLKS * block
    keys = buffer[pl.ds(start, trunk_rows), col : col + hd]
    trunk = mm_nt(keys, qh)
    query_block = lax.broadcasted_iota(i32, (1, qh.shape[0]), 1) // block + sc[6]
    pieces = []
    for j in range(TRUNK_BLKS):
        bias = jnp.where(query_block > j, 0.0, NEG)
        pieces.append(trunk[j * block : (j + 1) * block] + bias)
    key_pos = lax.broadcasted_iota(i32, (block, block), 0)
    query_pos = lax.broadcasted_iota(i32, (block, block), 1)
    own_s, par_s = [], []
    for i in range(count):
        q_i = qh[i * block : (i + 1) * block]
        o = mm_nt(own[i * block : (i + 1) * block, col : col + hd], q_i)
        own_s.append(jnp.where(key_pos <= query_pos, o, NEG))
        par = buffer[pl.ds(pl.multiple_of(sc[8 + i], block), block), col : col + hd]
        leaf = (lax.broadcasted_iota(i32, (1, block), 1) * 0 + sc[8 + count + i]) > 0
        par_s.append(mm_nt(par, q_i) + jnp.where(leaf, 0.0, NEG))
    pieces.append(jnp.concatenate(own_s, axis=1))
    pieces.append(jnp.concatenate(par_s, axis=1))
    return pieces, keys


def out_partial(sc, source, w, kept, sent):
    own_rows = kept.shape[1]
    for k in range(4):
        p = mm_nt(source[pl.ds(pl.multiple_of(sc[k], 16), own_rows), :], w[...])
        if k < 2:
            kept[k] = p
        else:
            sent[k - 2] = p.astype(bf16)


def self_body(block, heads, n_parts, sc, q, *refs):
    parts = refs[:n_parts]
    w = refs[n_parts]
    attn, lse, kept, sent, buffer = refs[n_parts + 1 :]
    own = parts[-1]
    fill_kv(buffer, parts)
    cols = q.shape[1]
    hd = cols // heads
    count = q.shape[0] // block
    trunk_rows = TRUNK_BLKS * block
    start = pl.multiple_of(sc[5], block)
    for h in range(heads):
        col = h * hd
        qh = q[:, col : col + hd] * jnp.asarray(hd**-0.5, bf16)
        pieces, _ = self_scores(sc, buffer, own, qh, h, hd, block)
        peak = pieces[0]
        for s in pieces[1:]:
            peak = jnp.maximum(peak, s)
        peak = jnp.max(peak, axis=0, keepdims=True)
        exps = [jnp.exp(s - peak) for s in pieces]
        total = exps[0]
        for e in exps[1:]:
            total = total + e
        total = jnp.sum(total, axis=0, keepdims=True)
        inv = 1.0 / total
        lse[h : h + 1, :] = peak + jnp.log(total)
        low = [(e * inv).astype(bf16) for e in exps]
        vals = buffer[pl.ds(start, trunk_rows), cols + col : cols + col + hd]
        mixed = mm_tn(jnp.concatenate(low[:TRUNK_BLKS], axis=0), vals)
        for i in range(count):
            rows = slice(i * block, (i + 1) * block)
            par = buffer[pl.ds(pl.multiple_of(sc[8 + i], block), block), cols + col : cols + col + hd]
            both = jnp.concatenate([low[TRUNK_BLKS][:, rows], low[TRUNK_BLKS + 1][:, rows]], axis=0)
            two = jnp.concatenate([own[rows, cols + col : cols + col + hd], par], axis=0)
            attn[rows, col : col + hd] = (mixed[rows] + mm_tn(both, two)).astype(bf16)
    out_partial(sc, attn, w, kept, sent)


def norm_body(first, time_at, gain_at, resid, chip, far, rows, resid_out, act):
    for k in range(2):
        base = resid[k].astype(f32)
        if first:
            base = base + rows[time_at : time_at + 1, :]
        v = base + (chip[k].astype(f32) + far[1 - k].astype(f32))
        resid_out[k] = v
        normed, _ = normalize(v)
        act[k] = (normed * rows[gain_at : gain_at + 1, :]).astype(bf16)


def both_halves(own, other):
    r, d = own.shape[1], own.shape[2]
    return jnp.concatenate([own[...].reshape(2 * r, d), other[...].reshape(2 * r, d)], axis=0)


def split_store(p, kept, sent):
    r = kept.shape[1]
    for k in range(2):
        kept[k] = p[k * r : (k + 1) * r]
        sent[k] = p[(2 + k) * r : (3 + k) * r].astype(bf16)


def cross_body(heads, own, other, enc, wq, wk, wv, wo, q, kv, low_out, lse, kept, sent):
    act = both_halves(own, other)
    queries = mm(act, wq[...]).astype(bf16)
    q[...] = queries
    cols = queries.shape[1]
    hd = cols // heads
    keys = mm(enc[...], wk[...]).astype(bf16)
    vals = mm(enc[...], wv[...]).astype(bf16)
    kv[:, :cols] = keys
    kv[:, cols:] = vals
    for h in range(heads):
        sl = slice(h * hd, (h + 1) * hd)
        s = mm_nt(keys[:, sl], queries[:, sl] * jnp.asarray(hd**-0.5, bf16))
        peak = jnp.max(s, axis=0, keepdims=True)
        e = jnp.exp(s - peak)
        total = jnp.sum(e, axis=0, keepdims=True)
        lse[h : h + 1, :] = peak + jnp.log(total)
        low_out[:, sl] = mm_tn((e * (1.0 / total)).astype(bf16), vals[:, sl]).astype(bf16)
    split_store(mm_nt(low_out[...], wo[...]), kept, sent)


def ffn_body(own, other, g_own, g_other, up, down_t, hidden, grad_pre, kept, sent):
    r = own.shape[1]
    for k in range(4):
        act = own[k] if k < 2 else other[k - 2]
        top = g_own[k] if k < 2 else g_other[k - 2]
        pre = mm(act, up[...])
        cdf = 0.5 * (1.0 + lax.erf(pre * 0.7071067811865476))
        hidden[k * r : (k + 1) * r, :] = (pre * cdf).astype(bf16)
        slope = cdf + pre * (jnp.exp(-0.5 * pre * pre) * 0.3989422804014327)
        gp = (mm(top, down_t[...]) * slope).astype(bf16)
        grad_pre[k * r : (k + 1) * r, :] = gp
        p = mm_nt(gp, up[...])
        if k < 2:
            kept[k] = p
        else:
            sent[k - 2] = p.astype(bf16)


def ffn_rest_body(own, other, g_own, g_other, hidden, grad_pre, down_t, kept, sent, sums):
    split_store(mm_nt(hidden[...], down_t[...]), kept, sent)
    cols = hidden.shape[1]
    sums[:, :cols] = mm_tn(both_halves(own, other), grad_pre[...]).astype(bf16)
    sums[:, cols:] = mm_tn(both_halves(g_own, g_other), hidden[...]).astype(bf16)


def back_body(gain_at, base, chip, far, resid, rows, grad, low, dgain):
    for k in range(2):
        g = chip[k].astype(f32) + far[1 - k].astype(f32)
        back, sums = norm_back(g, resid[k], rows[gain_at : gain_at + 1, :])
        v = base[k].astype(f32) + back
        grad[k] = v
        low[k] = v.astype(bf16)
        if k == 0:
            dgain[...] = sums


def inner_rows(grad, out):
    return (grad.astype(f32) * out.astype(f32)).T


def cross_back_body(heads, g_own, g_other, q, kv, low_in, lse, wq, wo, grad_q, grad_kv, kept, sent):
    top = both_halves(g_own, g_other)
    grad_mixed = mm(top, wo[...]).astype(bf16)
    cols = q.shape[1]
    hd = cols // heads
    inner = inner_rows(grad_mixed, low_in[...])
    for h in range(heads):
        sl = slice(h * hd, (h + 1) * hd)
        vl = slice(cols + h * hd, cols + (h + 1) * hd)
        qh = q[:, sl] * jnp.asarray(hd**-0.5, bf16)
        gh = grad_mixed[:, sl]
        probs = jnp.exp(mm_nt(kv[:, sl], qh) - lse[h : h + 1, :])
        grad_kv[:, vl] = mm(probs.astype(bf16), gh).astype(bf16)
        delta = jnp.sum(inner[sl], axis=0, keepdims=True)
        ds = (probs * (mm_nt(kv[:, vl], gh) - delta)).astype(bf16)
        grad_kv[:, sl] = mm(ds, qh).astype(bf16)
        grad_q[:, sl] = (mm_tn(ds, kv[:, sl]) * hd**-0.5).astype(bf16)
    split_store(mm_nt(grad_q[...], wq[...]), kept, sent)


def cross_rest_body(own, other, g_own, g_other, grad_q, low_in, sums):
    cols = grad_q.shape[1]
    sums[:, :cols] = mm_tn(both_halves(own, other), grad_q[...]).astype(bf16)
    sums[:, cols:] = mm_tn(both_halves(g_own, g_other), low_in[...]).astype(bf16)


def self_back_body(block, heads, n_parts, sc, g_own, g_other, q, attn, lse, *refs):
    parts = refs[:n_parts]
    w = refs[n_parts]
    outs = refs[n_parts + 1 :]
    top, grad_q, grad_own = outs[0], outs[1], outs[2]
    remote = outs[3 : 3 + n_parts - 1]
    buffer, sums = outs[3 + n_parts - 1 :]
    own = parts[-1]
    fill_kv(buffer, parts)
    sums[...] = jnp.zeros(sums.shape, f32)
    own_rows = g_own.shape[1]
    for k in range(4):
        src = g_own[k] if k < 2 else g_other[k - 2]
        top[pl.ds(pl.multiple_of(sc[k], 16), own_rows), :] = src
    cols = q.shape[1]
    hd = cols // heads
    count = q.shape[0] // block
    trunk_rows = TRUNK_BLKS * block
    start = pl.multiple_of(sc[5], block)
    grad_attn = mm(top[...], w[...]).astype(bf16)
    inner = inner_rows(grad_attn, attn[...])
    rows_all = own.shape[0]
    for h in range(heads):
        col = h * hd
        sl, vl = slice(col, col + hd), slice(cols + col, cols + col + hd)
        qh = q[:, sl] * jnp.asarray(hd**-0.5, bf16)
        gh = grad_attn[:, sl]
        pieces, keys = self_scores(sc, buffer, own, qh, h, hd, block)
        delta = jnp.sum(inner[sl], axis=0, keepdims=True)
        level = lse[h : h + 1, :]
        vals = buffer[pl.ds(start, trunk_rows), vl]
        probs = jnp.exp(jnp.concatenate(pieces[:TRUNK_BLKS], axis=0) - level)
        ds = (probs * (mm_nt(vals, gh) - delta)).astype(bf16)
        sums[pl.ds(start, trunk_rows), sl] += mm(ds, qh)
        sums[pl.ds(start, trunk_rows), vl] += mm(probs.astype(bf16), gh)
        grad_trunk = mm_tn(ds, keys)
        base = (n_parts - 1) * rows_all
        for i in range(count):
            rows = slice(i * block, (i + 1) * block)
            par_at = pl.ds(pl.multiple_of(sc[8 + i], block), block)
            own_at = slice(base + i * block, base + (i + 1) * block)
            q_i, g_i = qh[rows], gh[rows]
            grad_i = grad_trunk[rows]
            for piece, at in ((pieces[TRUNK_BLKS], own_at), (pieces[TRUNK_BLKS + 1], par_at)):
                p = jnp.exp(piece[:, rows] - level[:, rows])
                d = (p * (mm_nt(buffer[at, vl], g_i) - delta[:, rows])).astype(bf16)
                sums[at, sl] += mm(d, q_i)
                sums[at, vl] += mm(p.astype(bf16), g_i)
                grad_i = grad_i + mm_tn(d, buffer[at, sl])
            grad_q[rows, sl] = (grad_i * hd**-0.5).astype(bf16)
    for index, one in enumerate(remote):
        one[...] = sums[index * rows_all : (index + 1) * rows_all, :].astype(bf16)
    grad_own[...] = sums[base : base + rows_all, :]


def self_rest_body(act, top, attn, grad_q, wq, sum_q, sum_o, grad_act):
    sum_q[...] = mm_tn(act[...], grad_q[...]).astype(bf16)
    sum_o[...] = mm_tn(top[...], attn[...]).astype(bf16)
    grad_act[...] = mm_nt(grad_q[...], wq[...])


def self_end_body(n_parts, sc, act, grad_own, *refs):
    remote = refs[: n_parts - 1]
    wk, wv, sum_q, sum_o, grad_act, sums, kept, sent, total = refs[n_parts - 1 :]
    t = grad_own[...]
    for one in remote:
        t = t + one[...].astype(f32)
    total[...] = t.astype(bf16)
    cols = sum_q.shape[1]
    own_rows = kept.shape[1]
    for k in range(4):
        at = pl.ds(pl.multiple_of(sc[k], 16), own_rows)
        p = grad_act[at, :] + mm_nt(total[at, :cols], wk[...]) + mm_nt(total[at, cols:], wv[...])
        if k < 2:
            kept[k] = p
        else:
            sent[k - 2] = p.astype(bf16)
    sums[:, :cols] = sum_q[...]
    sums[:, cols : 3 * cols] = mm_tn(act[...], total[...]).astype(bf16)
    sums[:, 3 * cols :] = sum_o[...]


def last_body(sc, chip, far, tokens, grad_mid, rows, dgain_cross, dgain_ffn, grad_in, vectors):
    g = chip[...].astype(f32) + far[...].astype(f32)
    resid = tokens[...].astype(f32) + rows[3:4, :]
    back, dgain = norm_back(g, resid, rows[0:1, :])
    v = grad_mid[0] + back
    grad_in[...] = v
    vectors[0:1, :] = dgain
    vectors[1:2, :] = dgain_cross[...]
    vectors[2:3, :] = dgain_ffn[...]
    vectors[3:4, :] = jnp.sum(v, axis=0, keepdims=True)
    vectors[4:8, :] = jnp.zeros((4, v.shape[1]), f32) + sc[7].astype(f32)


def xor_route(axis, bit):
    return [(i, i ^ bit) for i in range(lax.axis_size(axis))]


def sibling(x):
    return lax.ppermute(x, "tensor", xor_route("tensor", 1))


def across(x):
    return lax.ppermute(x, "tensor", xor_route("tensor", 2))


def chip_sum(kept, sent):
    return kept + sibling(sent).astype(f32)


def gather_dp(x, groups=None):
    count = lax.axis_size("dp") if groups is None else len(groups[0])
    copies = jnp.broadcast_to(x[None], (count,) + x.shape)
    return lax.all_to_all(copies, "dp", 0, 0, axis_index_groups=groups).reshape(-1, x.shape[-1])


def scatter_dp(full):
    count = lax.axis_size("dp")
    parts = full.reshape(count, full.shape[0] // count, full.shape[1])
    return jnp.sum(lax.all_to_all(parts, "dp", 0, 0).astype(f32), axis=0)


def on_device(
    tokens_in, grad_out, enc_states, parents, tree_ids, timesteps, time_table, norm_self,
    w_query, w_key, w_value, w_out, norm_cross, c_query, c_key, c_value, c_out, norm_ffn,
    w_hidden, w_back,
):
    count = lax.axis_size("dp")
    tensor = lax.axis_size("tensor")
    heads = HEADS // tensor
    blocks_dev = parents.shape[0]
    tree_blocks = TRUNK_BLKS + BRANCHES * (1 + LEAVES)
    group = tree_blocks // blocks_dev
    hops_back = group - 1
    me = lax.axis_index("tensor")
    logical_dev = (lax.axis_index("dp") - group // 2) % count
    trees = timesteps.shape[0]
    width = tokens_in.shape[1]
    own_rows = tokens_in.shape[0]
    token_rows = own_rows * tensor
    block = token_rows // blocks_dev
    shard = norm_self.shape[0]
    cols = w_query.shape[1]
    hidden_cols = w_hidden.shape[1]
    groups = [
        [(tree * group + member + group // 2) % count for member in range(group)]
        for tree in range(count // group)
    ]
    steps_hot = (jnp.arange(time_table.shape[0], dtype=i32)[:, None] == timesteps[None, :]).astype(bf16)
    table_cols = mm_tn(time_table, steps_hot).astype(bf16)
    small = jnp.concatenate([norm_self[:, None], norm_cross[:, None], norm_ffn[:, None], table_cols], axis=1)
    small = jnp.pad(small, ((0, 0), (0, 128 - small.shape[1])))
    first = gather_dp(jnp.concatenate([w_query, w_key, w_value, small], axis=1))
    tokens_half = jnp.stack([tokens_in, across(tokens_in)])
    tokens_other = sibling(tokens_half)
    grad_half = jnp.stack([grad_out, across(grad_out)])
    grad_other = sibling(grad_half)
    enc_tree = gather_dp(enc_states, groups)
    second = gather_dp(jnp.concatenate([w_out.T, c_query, c_key, c_value, c_out.T], axis=1))
    third = gather_dp(jnp.concatenate([w_hidden, w_back.T], axis=1))
    position = logical_dev % group
    lead_blocks = group // 2 * blocks_dev
    parent_log = (parents - lead_blocks) % (count * blocks_dev)
    parent_rel = parent_log - logical_dev // group * tree_blocks
    query_block = position * blocks_dev + jnp.arange(blocks_dev, dtype=i32)
    is_leaf = query_block >= TRUNK_BLKS + BRANCHES
    shift = (hops_back - position) * blocks_dev
    parent_at = jnp.where(is_leaf, parent_rel, query_block) + shift
    step_id = jnp.sum(jnp.where(jnp.arange(trees, dtype=i32) == tree_ids[0], timesteps, 0))
    scalars = jnp.concatenate(
        [
            (me ^ jnp.array([0, 2, 1, 3], i32)) * own_rows,
            jnp.stack([tree_ids[0], shift * block, position * blocks_dev, step_id]),
            parent_at * block,
            is_leaf.astype(i32),
        ]
    ).astype(i32)
    half = (2, own_rows, width)
    act_self, q, kv, rows = run(
        project_body,
        [
            shaped((token_rows, width), bf16), shaped((token_rows, cols), bf16),
            shaped((token_rows, 2 * cols), bf16), shaped((4, width), f32),
        ],
        [scalars, tokens_half, tokens_other, part(first, 3 * cols, 0), part(first, 128, 3 * cols // 128)],
    )

    def later(distance):
        return [
            ((l + group // 2) % count, (l + distance + group // 2) % count)
            for l in range(count)
            if l % group + distance < group
        ]

    parts = [lax.ppermute(kv, "dp", later(d)) for d in range(hops_back, 0, -1)] + [kv]
    buffer_rows = group * token_rows + max(0, TRUNK_BLKS - blocks_dev) * block
    attn, lse, kept, sent = run(
        lambda *refs: self_body(block, heads, group, *refs),
        [shaped((token_rows, cols), bf16), shaped((8, token_rows), f32), shaped(half, f32), shaped(half, bf16)],
        [scalars, q, *parts, part(second, cols, 0)],
        [pltpu.VMEM((buffer_rows, 2 * cols), bf16)],
    )
    chip = chip_sum(kept, sent).astype(bf16)
    resid_mid, act_own = run(
        lambda *refs: norm_body(True, 3, 1, *refs),
        [shaped(half, f32), shaped(half, bf16)],
        [tokens_half, chip, across(chip), rows],
    )
    act_other = sibling(act_own)
    enc_rows = enc_tree.shape[0]
    cross_q, cross_kv, cross_low, cross_lse, kept, sent = run(
        lambda *refs: cross_body(heads, *refs),
        [
            shaped((token_rows, cols), bf16), shaped((enc_rows, 2 * cols), bf16), shaped((token_rows, cols), bf16),
            shaped((8, token_rows), f32), shaped(half, f32), shaped(half, bf16),
        ],
        [act_own, act_other, enc_tree, *[part(second, cols, i) for i in (1, 2, 3, 4)]],
    )
    chip = chip_sum(kept, sent).astype(bf16)
    resid_ffn, ffn_own = run(
        lambda *refs: norm_body(False, 3, 2, *refs),
        [shaped(half, f32), shaped(half, bf16)],
        [resid_mid, chip, across(chip), rows],
    )
    ffn_other = sibling(ffn_own)
    hidden, grad_pre, kept, sent = run(
        ffn_body,
        [
            shaped((token_rows, hidden_cols), bf16), shaped((token_rows, hidden_cols), bf16),
            shaped(half, f32), shaped(half, bf16),
        ],
        [ffn_own, ffn_other, grad_half, grad_other, part(third, hidden_cols, 0), part(third, hidden_cols, 1)],
    )
    chip = chip_sum(kept, sent).astype(bf16)
    out_kept, out_sent, ffn_sums = run(
        ffn_rest_body,
        [shaped(half, f32), shaped(half, bf16), shaped((width, 2 * hidden_cols), bf16)],
        [ffn_own, ffn_other, grad_half, grad_other, hidden, grad_pre, part(third, hidden_cols, 1)],
    )
    grad_resid_ffn, top_own, dgain_ffn = run(
        lambda *refs: back_body(2, *refs),
        [shaped(half, f32), shaped(half, bf16), shaped((1, width), f32)],
        [grad_half, chip, across(chip), resid_ffn, rows],
    )
    ffn_sums = scatter_dp(ffn_sums)
    out_chip = chip_sum(out_kept, out_sent)
    output = (resid_ffn[0] + (out_chip[0] + across(out_chip[1].astype(bf16)).astype(f32))).astype(bf16)
    top_other = sibling(top_own)
    grad_cq, grad_cross_kv, kept, sent = run(
        lambda *refs: cross_back_body(heads, *refs),
        [
            shaped((token_rows, cols), bf16), shaped((enc_rows, 2 * cols), bf16),
            shaped(half, f32), shaped(half, bf16),
        ],
        [top_own, top_other, cross_q, cross_kv, cross_low, cross_lse, part(second, cols, 1), part(second, cols, 4)],
    )
    chip = chip_sum(kept, sent).astype(bf16)
    (cross_part,) = run(
        cross_rest_body,
        [shaped((width, 2 * cols), bf16)],
        [act_own, act_other, top_own, top_other, grad_cq, cross_low],
    )
    enc_sum = jnp.sum(
        lax.all_to_all(grad_cross_kv.reshape(group, -1, 2 * cols), "dp", 0, 0, axis_index_groups=groups).astype(f32),
        axis=0,
    ).astype(bf16)
    enc_part = mm_nt(enc_sum, second[:, 2 * cols : 4 * cols])
    enc_chip = (enc_part + sibling(enc_part.astype(bf16)).astype(f32)).astype(bf16)
    grad_enc = enc_chip.astype(f32) + across(enc_chip).astype(f32)
    cross_sums = scatter_dp(jnp.concatenate([cross_part, mm_tn(enc_states, enc_sum).astype(bf16)], axis=1))
    grad_resid_mid, self_own, dgain_cross = run(
        lambda *refs: back_body(1, *refs),
        [shaped(half, f32), shaped(half, bf16), shaped((1, width), f32)],
        [grad_resid_ffn, chip, across(chip), resid_mid, rows],
    )
    self_other = sibling(self_own)
    kv_shape = (token_rows, 2 * cols)
    top, grad_q, grad_own, *remote = run(
        lambda *refs: self_back_body(block, heads, group, *refs),
        [shaped((token_rows, width), bf16), shaped((token_rows, cols), bf16), shaped(kv_shape, f32)]
        + [shaped(kv_shape, bf16)] * hops_back,
        [scalars, self_own, self_other, q, attn, lse, *parts, part(second, cols, 0)],
        [pltpu.VMEM((buffer_rows, 2 * cols), bf16), pltpu.VMEM((buffer_rows, 2 * cols), f32)],
    )
    back = [
        lax.ppermute(one, "dp", [(b, a) for a, b in later(d)]) for one, d in zip(remote, range(hops_back, 0, -1))
    ]
    sum_q, sum_o, grad_act = run(
        self_rest_body,
        [shaped((width, cols), bf16), shaped((width, cols), bf16), shaped((token_rows, width), f32)],
        [act_self, top, attn, grad_q, part(first, cols, 0)],
    )
    self_sums, kept, sent = run(
        lambda *refs: self_end_body(group, *refs),
        [shaped((width, 4 * cols), bf16), shaped(half, f32), shaped(half, bf16)],
        [scalars, act_self, grad_own, *back, part(first, cols, 1), part(first, cols, 2), sum_q, sum_o, grad_act],
        [pltpu.VMEM(kv_shape, bf16)],
    )
    chip = chip_sum(kept, sent)
    self_sums = scatter_dp(self_sums)
    grad_in, vectors = run(
        last_body,
        [shaped((own_rows, width), f32), shaped((8, width), f32)],
        [scalars, chip[0], across(chip[1].astype(bf16)), tokens_in, grad_resid_mid, rows, dgain_cross, dgain_ffn],
    )
    vectors = vectors.reshape(8, count, 1, shard).transpose(1, 2, 0, 3)
    vectors = jnp.broadcast_to(vectors, (count, tensor, 8, shard)).reshape(count * tensor, 8, shard)
    received = lax.all_to_all(vectors, ("dp", "tensor"), 0, 0)
    gain_sums = jnp.sum(received[:, :3], axis=0)
    table_hot = jnp.arange(time_table.shape[0], dtype=i32)[:, None, None] == received[:, 4].astype(i32)[None]
    grad_table = jnp.sum(jnp.where(table_hot, received[:, 3][None], 0.0), axis=1)
    gq, gk, gv, go = [self_sums[:, i * cols : (i + 1) * cols] for i in range(4)]
    gcq, gco, gck, gcv = [cross_sums[:, i * cols : (i + 1) * cols] for i in range(4)]
    return (
        output, grad_in, grad_enc, grad_table, gain_sums[0], gq, gk, gv, go.T, gain_sums[1],
        gcq, gck, gcv, gco.T, gain_sums[2], ffn_sums[:, :hidden_cols], ffn_sums[:, hidden_cols:].T,
    )


def solution(mesh):
    rows, cols, repl = P(("dp", "tensor"), None), P("dp", "tensor"), P("tensor", "dp")
    in_specs = (
        rows, rows, P("dp", None), P("dp"), P("dp"), P(), P(None, "dp"), P("dp"), cols, cols, cols, repl,
        P("dp"), cols, cols, cols, repl, P("dp"), cols, repl,
    )
    out_specs = (
        rows, rows, P("dp", None), P(None, "dp"), P("dp"), cols, cols, cols, repl, P("dp"), cols, cols, cols,
        repl, P("dp"), cols, repl,
    )
    return jax.shard_map(on_device, mesh=mesh, in_specs=in_specs, out_specs=out_specs, check_vma=False)
```

```python
import jax
import jax.numpy as jnp
from jax import lax
from jax.experimental import pallas as pl
from jax.experimental.pallas import tpu as pltpu
from jax.sharding import PartitionSpec as P

HEADS = 8
TRUNK_BLKS = 8
BRANCHES = 4
LEAVES = 2
eps = 1e-05
bf16 = jnp.bfloat16
f32 = jnp.float32
i32 = jnp.int32
NEG = -1e30


def mm(a, b):
    return lax.dot_general(a, b, (((1,), (0,)), ((), ())), preferred_element_type=f32)


def mm_tn(a, b):
    return lax.dot_general(a, b, (((0,), (0,)), ((), ())), preferred_element_type=f32)


def mm_nt(a, b):
    return lax.dot_general(a, b, (((1,), (1,)), ((), ())), preferred_element_type=f32)


def normalize(v):
    centered = v - jnp.mean(v, axis=-1, keepdims=True)
    inv = lax.rsqrt(jnp.mean(centered * centered, axis=-1, keepdims=True) + eps)
    return centered * inv, inv


def norm_back(grad_act, resid, gain):
    normed, inv = normalize(resid)
    scaled = grad_act * gain
    mean_g = jnp.mean(scaled, axis=-1, keepdims=True)
    mean_gx = jnp.mean(scaled * normed, axis=-1, keepdims=True)
    return inv * (scaled - mean_g - normed * mean_gx), jnp.sum(grad_act * normed, axis=0, keepdims=True)


def shaped(shape, dtype):
    return jax.ShapeDtypeStruct(shape, dtype)


class Cols:
    def __init__(self, ref, start, width):
        self.ref, self.cols, self.dtype = ref, slice(start, start + width), ref.dtype
        self.shape = (ref.shape[0], width)

    def __getitem__(self, key):
        return self.ref[:, self.cols]


def part(array, width, index):
    return (array, width * index, width)


def loading(body, n_scalars, n_loads, n_ins):
    def wrapped(*refs):
        sources = refs[n_scalars : n_scalars + n_loads]
        held = refs[len(refs) - n_loads - 1 : len(refs) - 1]
        sems = refs[-1]
        copies = [pltpu.make_async_copy(src, dst, sems.at[i]) for i, (src, dst) in enumerate(zip(sources, held))]
        for one in copies:
            one.start()
        for one in copies:
            one.wait()
        body(*refs[:n_scalars], *held, *refs[n_ins : len(refs) - n_loads - 1])

    return wrapped


def run(body, outs, ins, scratch=(), us=2, load=False, limit=24):
    arrays = [item[0] if isinstance(item, tuple) else item for item in ins]
    spaces = [pltpu.SMEM if array.dtype == i32 else (pltpu.HBM if load else pltpu.VMEM) for array in arrays]
    scratch = list(scratch)

    def wrapped(*refs):
        seen = [Cols(ref, item[1], item[2]) if isinstance(item, tuple) else ref for ref, item in zip(refs, ins)]
        body(*seen, *refs[len(ins) :])

    if load:
        loads = [array for array in arrays if array.dtype != i32]
        wrapped = loading(body, len(arrays) - len(loads), len(loads), len(arrays))
        scratch += [pltpu.VMEM(array.shape, array.dtype) for array in loads]
        scratch.append(pltpu.SemaphoreType.DMA((len(loads),)))
    return pl.pallas_call(
        wrapped,
        out_shape=outs,
        in_specs=[pl.BlockSpec(memory_space=space) for space in spaces],
        out_specs=[pl.BlockSpec(memory_space=pltpu.VMEM) for _ in outs],
        scratch_shapes=scratch,
        cost_estimate=pl.CostEstimate(flops=us * 3 * 10**9, bytes_accessed=10**6, transcendentals=0),
        compiler_params=pltpu.CompilerParams(vmem_limit_bytes=limit * 1024 * 1024),
    )(*arrays)


def pack_body(trees, n_first, steps, table, n_self, n_cross, n_ffn, *refs):
    weights, later, out, rest = refs[:n_first], refs[n_first:-2], refs[-2], refs[-1]
    at = 0
    for one in later:
        rest[:, at : at + one.shape[1]] = one[...]
        at += one.shape[1]
    lines = lax.broadcasted_iota(i32, table.shape, 0)
    full = table[...].astype(f32)
    small = [n_self[...].astype(f32), n_cross[...].astype(f32), n_ffn[...].astype(f32)]
    for i in range(trees):
        small.append(jnp.sum(jnp.where(lines == steps[i], full, 0.0), axis=0, keepdims=True))
    shard = table.shape[1]
    small.append(jnp.zeros((1, out.shape[2] - len(small) * shard), f32))
    tail = jnp.broadcast_to(jnp.concatenate(small, axis=1), (8, out.shape[2])).astype(bf16)
    for d in range(out.shape[0]):
        at = 0
        for one in weights:
            out[d, :shard, at : at + one.shape[1]] = one[...]
            at += one.shape[1]
        out[d, shard:, :] = tail


def assemble_body(slots, base, near, far, out):
    for i, ref in enumerate((near, far)):
        for k in range(ref.shape[0]):
            out[slots[base + i * ref.shape[0] + k]] = ref[k]


def project_body(sc, half, other, first, act, q, kv, rows, w):
    shard = first.shape[1] - 8
    count = first.shape[0]
    for d in range(count):
        w[d * shard : (d + 1) * shard, :] = first[d, :shard, :]
    tails = [first[d, shard:, :].astype(f32)[0:1] for d in range(count)]

    def line(k):
        return jnp.concatenate([one[:, k * shard : (k + 1) * shard] for one in tails], axis=1)

    trees = (first.shape[2] // shard) - 3
    time_row = jnp.zeros((1, count * shard), f32)
    for i in range(min(trees, rows.shape[0] - 4)):
        time_row = time_row + jnp.where(sc[4] == i, line(3 + i), 0.0)
    gain = line(0)
    rows[0:1, :] = gain
    rows[1:2, :] = line(1)
    rows[2:3, :] = line(2)
    rows[3:4, :] = time_row
    own_rows = half.shape[1]
    for k in range(4):
        src = half[k] if k < 2 else other[k - 2]
        normed, _ = normalize(src.astype(f32) + time_row)
        act[pl.ds(pl.multiple_of(sc[k], 16), own_rows), :] = (normed * gain).astype(bf16)
    cols = q.shape[1]
    result = mm(act[...], w[...]).astype(bf16)
    q[...] = result[:, :cols]
    kv[...] = result[:, cols:]


def fill_kv(buffer, parts):
    rows = parts[0].shape[0]
    for index, one in enumerate(parts):
        buffer[index * rows : (index + 1) * rows, :] = one[...]
    done = len(parts) * rows
    if buffer.shape[0] > done:
        buffer[done:, :] = jnp.zeros((buffer.shape[0] - done, buffer.shape[1]), buffer.dtype)


def self_scores(sc, buffer, own, qh, h, hd, block):
    count = qh.shape[0] // block
    col = h * hd
    start = pl.multiple_of(sc[5], block)
    trunk_rows = TRUNK_BLKS * block
    keys = buffer[pl.ds(start, trunk_rows), col : col + hd]
    trunk = mm_nt(keys, qh)
    query_block = lax.broadcasted_iota(i32, (1, qh.shape[0]), 1) // block + sc[6]
    pieces = []
    for j in range(TRUNK_BLKS):
        bias = jnp.where(query_block > j, 0.0, NEG)
        pieces.append(trunk[j * block : (j + 1) * block] + bias)
    key_pos = lax.broadcasted_iota(i32, (block, block), 0)
    query_pos = lax.broadcasted_iota(i32, (block, block), 1)
    own_s, par_s = [], []
    for i in range(count):
        q_i = qh[i * block : (i + 1) * block]
        o = mm_nt(own[i * block : (i + 1) * block, col : col + hd], q_i)
        own_s.append(jnp.where(key_pos <= query_pos, o, NEG))
        par = buffer[pl.ds(pl.multiple_of(sc[8 + i], block), block), col : col + hd]
        leaf = (lax.broadcasted_iota(i32, (1, block), 1) * 0 + sc[8 + count + i]) > 0
        par_s.append(mm_nt(par, q_i) + jnp.where(leaf, 0.0, NEG))
    pieces.append(jnp.concatenate(own_s, axis=1))
    pieces.append(jnp.concatenate(par_s, axis=1))
    return pieces, keys


def out_partial(sc, source, w, kept, sent):
    own_rows = kept.shape[1]
    for k in range(4):
        p = mm_nt(source[pl.ds(pl.multiple_of(sc[k], 16), own_rows), :], w[...])
        if k < 2:
            kept[k] = p
        else:
            sent[k - 2] = p.astype(bf16)


def self_body(block, heads, n_parts, sc, q, *refs):
    parts = refs[:n_parts]
    w = refs[n_parts]
    attn, lse, kept, sent, buffer = refs[n_parts + 1 :]
    own = parts[-1]
    fill_kv(buffer, parts)
    cols = q.shape[1]
    hd = cols // heads
    count = q.shape[0] // block
    trunk_rows = TRUNK_BLKS * block
    start = pl.multiple_of(sc[5], block)
    for h in range(heads):
        col = h * hd
        qh = q[:, col : col + hd] * jnp.asarray(hd**-0.5, bf16)
        pieces, _ = self_scores(sc, buffer, own, qh, h, hd, block)
        peak = pieces[0]
        for s in pieces[1:]:
            peak = jnp.maximum(peak, s)
        peak = jnp.max(peak, axis=0, keepdims=True)
        exps = [jnp.exp(s - peak) for s in pieces]
        total = exps[0]
        for e in exps[1:]:
            total = total + e
        total = jnp.sum(total, axis=0, keepdims=True)
        inv = 1.0 / total
        lse[h : h + 1, :] = peak + jnp.log(total)
        low = [(e * inv).astype(bf16) for e in exps]
        vals = buffer[pl.ds(start, trunk_rows), cols + col : cols + col + hd]
        mixed = mm_tn(jnp.concatenate(low[:TRUNK_BLKS], axis=0), vals)
        for i in range(count):
            rows = slice(i * block, (i + 1) * block)
            par = buffer[pl.ds(pl.multiple_of(sc[8 + i], block), block), cols + col : cols + col + hd]
            both = jnp.concatenate([low[TRUNK_BLKS][:, rows], low[TRUNK_BLKS + 1][:, rows]], axis=0)
            two = jnp.concatenate([own[rows, cols + col : cols + col + hd], par], axis=0)
            attn[rows, col : col + hd] = (mixed[rows] + mm_tn(both, two)).astype(bf16)
    out_partial(sc, attn, w, kept, sent)


def norm_body(first, time_at, gain_at, resid, chip, far, rows, resid_out, act):
    for k in range(2):
        base = resid[k].astype(f32)
        if first:
            base = base + rows[time_at : time_at + 1, :]
        v = base + (chip[k].astype(f32) + far[1 - k].astype(f32))
        resid_out[k] = v
        normed, _ = normalize(v)
        act[k] = (normed * rows[gain_at : gain_at + 1, :]).astype(bf16)


def both_halves(own, other):
    r, d = own.shape[1], own.shape[2]
    return jnp.concatenate([own[...].reshape(2 * r, d), other[...].reshape(2 * r, d)], axis=0)


def split_store(p, kept, sent):
    r = kept.shape[1]
    for k in range(2):
        kept[k] = p[k * r : (k + 1) * r]
        sent[k] = p[(2 + k) * r : (3 + k) * r].astype(bf16)


def cross_body(heads, n_enc, own, other, *refs):
    encs = refs[:n_enc]
    w, q, kv, low_out, lse, kept, sent = refs[n_enc:]
    act = both_halves(own, other)
    cols = q.shape[1]
    hd = cols // heads
    queries = mm(act, w[:, :cols]).astype(bf16)
    q[...] = queries
    pairs = mm(jnp.concatenate([enc[...] for enc in encs], axis=0), w[:, cols : 3 * cols]).astype(bf16)
    kv[...] = pairs
    for h in range(heads):
        sl = slice(h * hd, (h + 1) * hd)
        s = mm_nt(pairs[:, sl], queries[:, sl] * jnp.asarray(hd**-0.5, bf16))
        peak = jnp.max(s, axis=0, keepdims=True)
        e = jnp.exp(s - peak)
        total = jnp.sum(e, axis=0, keepdims=True)
        lse[h : h + 1, :] = peak + jnp.log(total)
        vals = pairs[:, cols + h * hd : cols + (h + 1) * hd]
        low_out[:, sl] = mm_tn((e * (1.0 / total)).astype(bf16), vals).astype(bf16)
    split_store(mm_nt(low_out[...], w[:, 3 * cols : 4 * cols]), kept, sent)


def ffn_body(own, other, g_own, g_other, up, down_t, hidden, grad_pre, kept, sent):
    r = own.shape[1]
    for k in range(4):
        act = own[k] if k < 2 else other[k - 2]
        top = g_own[k] if k < 2 else g_other[k - 2]
        pre = mm(act, up[...])
        cdf = 0.5 * (1.0 + lax.erf(pre * 0.7071067811865476))
        hidden[k * r : (k + 1) * r, :] = (pre * cdf).astype(bf16)
        slope = cdf + pre * (jnp.exp(-0.5 * pre * pre) * 0.3989422804014327)
        gp = (mm(top, down_t[...]) * slope).astype(bf16)
        grad_pre[k * r : (k + 1) * r, :] = gp
        p = mm_nt(gp, up[...])
        if k < 2:
            kept[k] = p
        else:
            sent[k - 2] = p.astype(bf16)


def relative(slots, base, scratch, value, kept, sent):
    scratch[...] = value.reshape(scratch.shape).astype(bf16)
    for i, ref in enumerate((kept, sent)):
        for k in range(ref.shape[0]):
            ref[k] = scratch[slots[base + i * ref.shape[0] + k]]


def grads_body(n_enc, slots, *refs):
    own, other, top_own, top_other, grad_q, low_in = refs[:6]
    encs, grad_encs = refs[6 : 6 + n_enc], refs[6 + n_enc : 6 + 2 * n_enc]
    ffn_own, ffn_other, g_own, g_other, hidden, grad_pre, near, far, scratch = refs[6 + 2 * n_enc :]
    sums = [
        mm_tn(both_halves(own, other), grad_q[...]),
        mm_tn(
            jnp.concatenate([one[...] for one in encs], axis=0), jnp.concatenate([one[...] for one in grad_encs], axis=0)
        ),
        mm_tn(both_halves(top_own, top_other), low_in[...]),
        mm_tn(both_halves(ffn_own, ffn_other), grad_pre[...]),
        mm_tn(both_halves(g_own, g_other), hidden[...]),
    ]
    relative(slots, 2 * near.shape[0], scratch, jnp.concatenate(sums, axis=1), near, far)


def out_body(hidden, down_t, kept, sent):
    split_store(mm_nt(hidden[...], down_t[...]), kept, sent)


def back_body(gain_at, base, chip, far, resid, rows, grad, low, dgain):
    for k in range(2):
        g = chip[k].astype(f32) + far[1 - k].astype(f32)
        back, sums = norm_back(g, resid[k], rows[gain_at : gain_at + 1, :])
        v = base[k].astype(f32) + back
        grad[k] = v
        low[k] = v.astype(bf16)
        if k == 0:
            dgain[...] = sums


def inner_rows(grad, out):
    return (grad.astype(f32) * out.astype(f32)).T


def cross_back_body(heads, g_own, g_other, q, kv, low_in, lse, w, grad_q, kept, sent, *grad_encs):
    top = both_halves(g_own, g_other)
    cols = q.shape[1]
    hd = cols // heads
    grad_mixed = mm(top, w[:, 3 * cols : 4 * cols]).astype(bf16)
    inner = inner_rows(grad_mixed, low_in[...])
    enc_rows = grad_encs[0].shape[0]
    for h in range(heads):
        sl = slice(h * hd, (h + 1) * hd)
        vl = slice(cols + h * hd, cols + (h + 1) * hd)
        qh = q[:, sl] * jnp.asarray(hd**-0.5, bf16)
        gh = grad_mixed[:, sl]
        probs = jnp.exp(mm_nt(kv[:, sl], qh) - lse[h : h + 1, :])
        grad_v = mm(probs.astype(bf16), gh).astype(bf16)
        delta = jnp.sum(inner[sl], axis=0, keepdims=True)
        ds = (probs * (mm_nt(kv[:, vl], gh) - delta)).astype(bf16)
        grad_k = mm(ds, qh).astype(bf16)
        for i, one in enumerate(grad_encs):
            one[:, sl] = grad_k[i * enc_rows : (i + 1) * enc_rows]
            one[:, vl] = grad_v[i * enc_rows : (i + 1) * enc_rows]
        grad_q[:, sl] = (mm_tn(ds, kv[:, sl]) * hd**-0.5).astype(bf16)
    split_store(mm_nt(grad_q[...], w[:, :cols]), kept, sent)


def enc_body(n_enc, w, *refs):
    parts, out = refs[:n_enc], refs[n_enc]
    total = parts[0][...].astype(f32)
    for one in parts[1:]:
        total = total + one[...].astype(f32)
    cols = total.shape[1] // 2
    out[...] = mm_nt(total.astype(bf16), w[:, cols : 3 * cols]).astype(bf16)


def self_back_body(block, heads, n_parts, sc, g_own, g_other, q, attn, lse, *refs):
    parts = refs[:n_parts]
    w = refs[n_parts]
    outs = refs[n_parts + 1 :]
    top, ds_trunk, ds_near, grad_own = outs[:4]
    remote = outs[4 : 4 + n_parts - 1]
    buffer, sums = outs[4 + n_parts - 1 :]
    own = parts[-1]
    fill_kv(buffer, parts)
    sums[...] = jnp.zeros(sums.shape, f32)
    own_rows = g_own.shape[1]
    for k in range(4):
        src = g_own[k] if k < 2 else g_other[k - 2]
        top[pl.ds(pl.multiple_of(sc[k], 16), own_rows), :] = src
    cols = q.shape[1]
    hd = cols // heads
    count = q.shape[0] // block
    trunk_rows = TRUNK_BLKS * block
    start = pl.multiple_of(sc[5], block)
    grad_attn = mm(top[...], w[...]).astype(bf16)
    inner = inner_rows(grad_attn, attn[...])
    rows_all = own.shape[0]
    base = (n_parts - 1) * rows_all
    for h in range(heads):
        col = h * hd
        sl, vl = slice(col, col + hd), slice(cols + col, cols + col + hd)
        qh = q[:, sl] * jnp.asarray(hd**-0.5, bf16)
        gh = grad_attn[:, sl]
        pieces, keys = self_scores(sc, buffer, own, qh, h, hd, block)
        delta = jnp.sum(inner[sl], axis=0, keepdims=True)
        level = lse[h : h + 1, :]
        vals = buffer[pl.ds(start, trunk_rows), vl]
        probs = jnp.exp(jnp.concatenate(pieces[:TRUNK_BLKS], axis=0) - level)
        ds = (probs * (mm_nt(vals, gh) - delta)).astype(bf16)
        ds_trunk[h] = ds
        sums[pl.ds(start, trunk_rows), sl] += mm(ds, qh)
        sums[pl.ds(start, trunk_rows), vl] += mm(probs.astype(bf16), gh)
        for i in range(count):
            rows = slice(i * block, (i + 1) * block)
            par_at = pl.ds(pl.multiple_of(sc[8 + i], block), block)
            own_at = slice(base + i * block, base + (i + 1) * block)
            q_i, g_i = qh[rows], gh[rows]
            near = ((pieces[TRUNK_BLKS], own_at), (pieces[TRUNK_BLKS + 1], par_at))
            for j, (piece, at) in enumerate(near):
                p = jnp.exp(piece[:, rows] - level[:, rows])
                d = (p * (mm_nt(buffer[at, vl], g_i) - delta[:, rows])).astype(bf16)
                ds_near[h, j, :, rows] = d
                sums[at, sl] += mm(d, q_i)
                sums[at, vl] += mm(p.astype(bf16), g_i)
    for index, one in enumerate(remote):
        one[...] = sums[index * rows_all : (index + 1) * rows_all, :].astype(bf16)
    grad_own[...] = sums[base : base + rows_all, :]


def self_rest_body(block, heads, n_parts, sc, act, top, attn, ds_trunk, ds_near, *refs):
    parts = refs[:n_parts]
    wq, sum_q, sum_o, grad_act, grad_q, buffer = refs[n_parts:]
    fill_kv(buffer, parts)
    own = parts[-1]
    cols = grad_q.shape[1]
    hd = cols // heads
    trunk_rows = TRUNK_BLKS * block
    start = pl.multiple_of(sc[5], block)
    for h in range(heads):
        sl = slice(h * hd, (h + 1) * hd)
        trunk = mm_tn(ds_trunk[h], buffer[pl.ds(start, trunk_rows), sl])
        for i in range(grad_q.shape[0] // block):
            rows = slice(i * block, (i + 1) * block)
            par = buffer[pl.ds(pl.multiple_of(sc[8 + i], block), block), sl]
            both = jnp.concatenate([ds_near[h, 0, :, rows], ds_near[h, 1, :, rows]], axis=0)
            near = mm_tn(both, jnp.concatenate([own[rows, sl], par], axis=0))
            grad_q[rows, sl] = ((trunk[rows] + near) * hd**-0.5).astype(bf16)
    sum_q[...] = mm_tn(act[...], grad_q[...])
    sum_o[...] = mm_tn(top[...], attn[...])
    grad_act[...] = mm_nt(grad_q[...], wq[...])


def self_end_body(n_parts, sc, slots, act, grad_own, *refs):
    remote = refs[: n_parts - 1]
    wk, wv, sum_q, sum_o, grad_act, near, far, kept, sent, total, scratch = refs[n_parts - 1 :]
    t = grad_own[...]
    for one in remote:
        t = t + one[...].astype(f32)
    total[...] = t.astype(bf16)
    cols = sum_q.shape[1]
    own_rows = kept.shape[1]
    for k in range(4):
        at = pl.ds(pl.multiple_of(sc[k], 16), own_rows)
        p = grad_act[at, :] + mm_nt(total[at, :cols], wk[...]) + mm_nt(total[at, cols:], wv[...])
        if k < 2:
            kept[k] = p
        else:
            sent[k - 2] = p.astype(bf16)
    weights = jnp.concatenate([sum_q[...], mm_tn(act[...], total[...]), sum_o[...]], axis=1)
    relative(slots, 2 * near.shape[0], scratch, weights, near, far)


def vector_body(trees, sc, kept, sent, half, other, grad_mid, rows, dgain_cross, dgain_ffn, out):
    gain = rows[0:1, :]
    dgain = jnp.zeros(gain.shape, f32)
    column = jnp.sum(grad_mid[0], axis=0, keepdims=True)
    for k in range(4):
        g = kept[k] if k < 2 else sent[k - 2].astype(f32)
        src = half[k] if k < 2 else other[k - 2]
        back, one = norm_back(g, src.astype(f32) + rows[3:4, :], gain)
        dgain = dgain + one
        column = column + jnp.sum(back, axis=0, keepdims=True)
    lines = lax.broadcasted_iota(i32, (out.shape[1], gain.shape[1]), 0)
    block = jnp.where(lines == 3 + sc[4], column, 0.0)
    for i, one in enumerate((dgain, dgain_cross[...], dgain_ffn[...])):
        block = jnp.where(lines == i, one, block)
    shard = out.shape[2]
    for d in range(out.shape[0]):
        out[d] = block[:, d * shard : (d + 1) * shard]


def last_body(chip, far, tokens, grad_mid, rows, grad_in):
    g = chip[0] + far[...].astype(f32)
    back, _ = norm_back(g, tokens[...].astype(f32) + rows[3:4, :], rows[0:1, :])
    grad_in[...] = grad_mid[0] + back


def small_body(trees, steps, slots, near, far, gains, table):
    me = slots[slots.shape[0] - 1]
    total = near[me] + far[me]
    gains[...] = total[:8]
    lines = lax.broadcasted_iota(i32, table.shape, 0)
    sums = jnp.zeros(table.shape, f32)
    for i in range(trees):
        sums = sums + jnp.where(lines == steps[i], total[3 + i : 4 + i], 0.0)
    table[...] = sums


def finish_pair_body(near, far, *outs):
    total = near[0].astype(f32) + far[0].astype(f32)
    at = 0
    for one in outs:
        one[...] = total[:, at : at + one.shape[1]]
        at += one.shape[1]


def xor_route(axis, bit):
    return [(i, i ^ bit) for i in range(lax.axis_size(axis))]


def sibling(x):
    return lax.ppermute(x, "tensor", xor_route("tensor", 1))


def across(x):
    return lax.ppermute(x, "tensor", xor_route("tensor", 2))


def chip_sum(kept, sent):
    return kept + sibling(sent).astype(f32)


def tie(x, *others):
    return lax.optimization_barrier((x, *others))[0]


def doubling(x):
    held = x[None]
    bit = lax.axis_size("dp") // 2
    while bit > 1:
        held = jnp.concatenate([held, lax.ppermute(held, "dp", xor_route("dp", bit))], axis=0)
        bit //= 2
    return held


def neighbour(x):
    return lax.ppermute(x, "dp", xor_route("dp", 1))


class Halving:
    def __init__(self, near, far):
        self.bit = 2
        self.near, self.received = near, neighbour(far)

    def step(self, *dues):
        self.received = tie(self.received, *dues)
        if self.bit >= lax.axis_size("dp"):
            return self.received
        total = (self.near.astype(f32) + self.received.astype(f32)).astype(bf16)
        middle = total.shape[0] // 2
        self.near = total[:middle]
        self.received = lax.ppermute(total[middle:], "dp", xor_route("dp", self.bit))
        self.bit *= 2
        return self.near

    def end(self, *dues):
        while self.bit < lax.axis_size("dp"):
            self.step(*dues)
        return self.near, tie(self.received, *dues)


def on_device(
    tokens_in, grad_out, enc_states, parents, tree_ids, timesteps, time_table, norm_self,
    w_query, w_key, w_value, w_out, norm_cross, c_query, c_key, c_value, c_out, norm_ffn,
    w_hidden, w_back,
):
    count = lax.axis_size("dp")
    tensor = lax.axis_size("tensor")
    heads = HEADS // tensor
    blocks_dev = parents.shape[0]
    tree_blocks = TRUNK_BLKS + BRANCHES * (1 + LEAVES)
    group = tree_blocks // blocks_dev
    hops_back = group - 1
    me = lax.axis_index("tensor")
    dp_index = lax.axis_index("dp")
    logical_dev = (dp_index - group // 2) % count
    trees = timesteps.shape[0]
    width = tokens_in.shape[1]
    own_rows = tokens_in.shape[0]
    token_rows = own_rows * tensor
    block = token_rows // blocks_dev
    shard = norm_self.shape[0]
    cols = w_query.shape[1]
    hidden_cols = w_hidden.shape[1]
    packed, rest = run(
        lambda *refs: pack_body(trees, 3, *refs),
        [shaped((count, shard + 8, 3 * cols), bf16), shaped((shard, 4 * cols + 2 * hidden_cols), bf16)],
        [
            timesteps, time_table, norm_self[None], norm_cross[None], norm_ffn[None],
            w_query, w_key, w_value, c_query, c_key, c_value, c_out.T, w_hidden, w_back.T,
        ],
        load=True,
        limit=60,
    )
    first = lax.all_to_all(packed, "dp", 0, 0)
    tokens_half = jnp.stack([tokens_in, across(tokens_in)])
    tokens_other = sibling(tokens_half)
    grad_half = jnp.stack([grad_out, across(grad_out)])
    grad_other = sibling(grad_half)
    rest_near = doubling(rest)

    def turn(distance):
        return [
            ((l + group // 2) % count, (l - l % group + (l + distance) % group + group // 2) % count)
            for l in range(count)
        ]

    position = logical_dev % group
    lead_blocks = group // 2 * blocks_dev
    parent_log = (parents - lead_blocks) % (count * blocks_dev)
    parent_rel = parent_log - logical_dev // group * tree_blocks
    query_block = position * blocks_dev + jnp.arange(blocks_dev, dtype=i32)
    is_leaf = query_block >= TRUNK_BLKS + BRANCHES
    shift = (hops_back - position) * blocks_dev
    parent_at = jnp.where(is_leaf, parent_rel, query_block) + shift
    step_id = jnp.sum(jnp.where(jnp.arange(trees, dtype=i32) == tree_ids[0], timesteps, 0))
    scalars = jnp.concatenate(
        [
            (me ^ jnp.array([0, 2, 1, 3], i32)) * own_rows,
            jnp.stack([tree_ids[0], shift * block, position * blocks_dev, step_id]),
            parent_at * block,
            is_leaf.astype(i32),
        ]
    ).astype(i32)
    bits = count.bit_length() - 1
    near_masks = [sum(((k >> j) & 1) * (count >> (j + 1)) for j in range(bits - 1)) for k in range(count // 2)]
    half_masks = [sum(((k >> j) & 1) * (count >> (j + 1)) for j in range(bits - 1)) for k in range(count // 2)]
    masks = near_masks + [m | 1 for m in near_masks] + half_masks + [m | 1 for m in half_masks] + [0]
    slots = (dp_index ^ jnp.array(masks, i32)).astype(i32)

    def assemble(near, far):
        far = far if far is not None else neighbour(near)
        (full,) = run(
            lambda *refs: assemble_body(refs[0], 0, *refs[1:]),
            [shaped((count,) + near.shape[1:], bf16)],
            [slots, near, far],
            us=1,
        )
        return full.reshape(width, near.shape[2])

    half = (2, own_rows, width)
    act_self, q, kv, rows, qkv_w = run(
        project_body,
        [
            shaped((token_rows, width), bf16), shaped((token_rows, cols), bf16),
            shaped((token_rows, 2 * cols), bf16), shaped((4 + trees, width), f32),
            shaped((width, 3 * cols), bf16),
        ],
        [scalars, tokens_half, tokens_other, first],
    )
    out_near = doubling(w_out.T)
    w_o = assemble(out_near, neighbour(out_near))

    def later(distance):
        return [
            ((l + group // 2) % count, (l + distance + group // 2) % count)
            for l in range(count)
            if l % group + distance < group
        ]

    parts = [lax.ppermute(kv, "dp", later(d)) for d in range(hops_back, 0, -1)] + [kv]
    buffer_rows = group * token_rows + max(0, TRUNK_BLKS - blocks_dev) * block
    cross_near, ffn_near = rest_near[:, :, : 4 * cols], rest_near[:, :, 4 * cols :]
    cross_far = neighbour(cross_near)
    q = tie(q, cross_far, grad_other)
    ffn_far = neighbour(ffn_near)
    attn, lse, kept, sent = run(
        lambda *refs: self_body(block, heads, group, *refs),
        [shaped((token_rows, cols), bf16), shaped((8, token_rows), f32), shaped(half, f32), shaped(half, bf16)],
        [scalars, q, *parts, w_o],
        [pltpu.VMEM((buffer_rows, 2 * cols), bf16)],
        us=5,
    )
    chip = chip_sum(kept, sent).astype(bf16)
    enc_rows = enc_states.shape[0]
    enc_sent = tie(enc_states, attn)
    enc_parts = [enc_states] + [lax.ppermute(enc_sent, "dp", turn(d)) for d in range(1, group)]
    resid_mid, act_own = run(
        lambda *refs: norm_body(True, 3, 1, *refs),
        [shaped(half, f32), shaped(half, bf16)],
        [tokens_half, chip, tie(across(chip), ffn_far, *enc_parts), rows],
        us=1,
    )
    act_other = sibling(act_own)
    rest_w = assemble(cross_near, cross_far)
    ffn_w = assemble(ffn_near, ffn_far)
    cross_q, cross_kv, cross_low, cross_lse, kept, sent = run(
        lambda *refs: cross_body(heads, group, *refs),
        [
            shaped((token_rows, cols), bf16), shaped((group * enc_rows, 2 * cols), bf16),
            shaped((token_rows, cols), bf16), shaped((8, token_rows), f32), shaped(half, f32), shaped(half, bf16),
        ],
        [act_own, act_other, *enc_parts, rest_w],
    )
    chip = chip_sum(kept, sent).astype(bf16)
    resid_ffn, ffn_own = run(
        lambda *refs: norm_body(False, 3, 2, *refs),
        [shaped(half, f32), shaped(half, bf16)],
        [resid_mid, chip, across(chip), rows],
        us=1,
    )
    ffn_other = sibling(ffn_own)
    hidden, grad_pre, kept, sent = run(
        ffn_body,
        [
            shaped((token_rows, hidden_cols), bf16), shaped((token_rows, hidden_cols), bf16),
            shaped(half, f32), shaped(half, bf16),
        ],
        [ffn_own, ffn_other, grad_half, grad_other, part(ffn_w, hidden_cols, 0), part(ffn_w, hidden_cols, 1)],
        us=3,
    )
    chip = chip_sum(kept, sent).astype(bf16)
    out_kept, out_sent = run(
        out_body, [shaped(half, f32), shaped(half, bf16)], [hidden, part(ffn_w, hidden_cols, 1)]
    )
    grad_resid_ffn, top_own, dgain_ffn = run(
        lambda *refs: back_body(2, *refs),
        [shaped(half, f32), shaped(half, bf16), shaped((1, width), f32)],
        [grad_half, chip, tie(across(chip), out_sent), resid_ffn, rows],
        us=1,
    )
    top_other = sibling(top_own)
    grad_cq, kept, sent, *grad_encs = run(
        lambda *refs: cross_back_body(heads, *refs),
        [shaped((token_rows, cols), bf16), shaped(half, f32), shaped(half, bf16)]
        + [shaped((enc_rows, 2 * cols), bf16)] * group,
        [top_own, top_other, cross_q, cross_kv, cross_low, cross_lse, rest_w],
        us=3,
    )
    chip = chip_sum(kept, sent).astype(bf16)
    split = (count // 2, shard, 4 * cols + 2 * hidden_cols)
    rest_kept, rest_sent = run(
        lambda *refs: grads_body(group, *refs),
        [shaped(split, bf16), shaped(split, bf16)],
        [
            slots, act_own, act_other, top_own, top_other, grad_cq, cross_low, *enc_parts, *grad_encs,
            ffn_own, ffn_other, grad_half, grad_other, hidden, grad_pre,
        ],
        [pltpu.VMEM((count, shard, split[2]), bf16)],
        us=4,
    )
    rest_chain = Halving(rest_kept, rest_sent)
    grad_encs = [grad_encs[0]] + [
        lax.ppermute(grad_encs[d], "dp", [(b, a) for a, b in turn(d)]) for d in range(1, group)
    ]
    grad_resid_mid, self_own, dgain_cross = run(
        lambda *refs: back_body(1, *refs),
        [shaped(half, f32), shaped(half, bf16), shaped((1, width), f32)],
        [grad_resid_ffn, chip, tie(across(chip), rest_sent), resid_mid, rows],
        us=1,
    )
    self_other = sibling(self_own)
    kv_shape = (token_rows, 2 * cols)
    top, ds_trunk, ds_near, grad_own, *remote = run(
        lambda *refs: self_back_body(block, heads, group, *refs),
        [
            shaped((token_rows, width), bf16), shaped((heads, TRUNK_BLKS * block, token_rows), bf16),
            shaped((heads, 2, block, token_rows), bf16), shaped(kv_shape, f32),
        ]
        + [shaped(kv_shape, bf16)] * hops_back,
        [scalars, self_own, self_other, q, attn, lse, *parts, w_o],
        [pltpu.VMEM((buffer_rows, 2 * cols), bf16), pltpu.VMEM((buffer_rows, 2 * cols), f32)],
        us=8,
    )
    back = [
        lax.ppermute(one, "dp", [(b, a) for a, b in later(d)]) for one, d in zip(remote, range(hops_back, 0, -1))
    ]
    sum_q, sum_o, grad_act = run(
        lambda *refs: self_rest_body(block, heads, group, *refs),
        [shaped((width, cols), f32), shaped((width, cols), f32), shaped((token_rows, width), f32)],
        [scalars, act_self, top, attn, ds_trunk, ds_near, *parts, part(qkv_w, cols, 0)],
        [pltpu.VMEM((token_rows, cols), bf16), pltpu.VMEM((buffer_rows, 2 * cols), bf16)],
        us=4,
    )
    held = rest_chain.step(grad_act)
    (enc_part,) = run(
        lambda *refs: enc_body(group, *refs),
        [shaped((enc_rows, width), bf16)],
        [rest_w, tie(grad_encs[0], ds_trunk), *grad_encs[1:]],
        us=1,
    )
    out_chip = chip_sum(out_kept, tie(out_sent, ds_trunk))
    output = (resid_ffn[0] + (out_chip[0] + across(out_chip[1].astype(bf16)).astype(f32))).astype(bf16)
    enc_chip = (enc_part.astype(f32) + sibling(enc_part).astype(f32)).astype(bf16)
    grad_enc = enc_chip.astype(f32) + across(enc_chip).astype(f32)
    grad_own = tie(grad_own, output, grad_enc, held)
    split = (count // 2, shard, 4 * cols)
    self_kept, self_sent, kept, sent = run(
        lambda *refs: self_end_body(group, *refs),
        [shaped(split, bf16), shaped(split, bf16), shaped(half, f32), shaped(half, bf16)],
        [
            scalars, slots, act_self, grad_own, *back, part(qkv_w, cols, 1), part(qkv_w, cols, 2), sum_q, sum_o, grad_act,
        ],
        [pltpu.VMEM(kv_shape, bf16), pltpu.VMEM((count, shard, 4 * cols), bf16)],
        us=3,
    )
    self_chain = Halving(self_kept, self_sent)
    rest_chain.step(sent)
    (vectors,) = run(
        lambda *refs: vector_body(trees, *refs),
        [shaped((count, -(-(3 + trees) // 8) * 8, shard), f32)],
        [scalars, kept, sent, tokens_half, tokens_other, grad_resid_mid, rows, dgain_cross, dgain_ffn],
    )
    chip = chip_sum(kept, sent)
    vectors = vectors + sibling(vectors)
    vectors = vectors + across(vectors)
    (grad_in,) = run(
        last_body,
        [shaped((own_rows, width), f32)],
        [chip, across(chip[1].astype(bf16)), tokens_in, grad_resid_mid, rows],
        us=1,
    )
    bit = 1
    vectors = tie(vectors, grad_in, self_chain.step(vectors))
    while bit < count // 2:
        vectors = vectors + lax.ppermute(vectors, "dp", xor_route("dp", bit))
        bit *= 2
        vectors = tie(vectors, self_chain.step(vectors))
    received = lax.ppermute(vectors, "dp", xor_route("dp", bit))
    self_sums, rest_sums = self_chain.end(), rest_chain.end()
    gains, grad_table = run(
        lambda *refs: small_body(trees, *refs),
        [shaped((8, shard), f32), shaped((time_table.shape[0], shard), f32)],
        [timesteps, slots, vectors, received],
        us=1,
    )
    square = shaped((shard, cols), f32)
    gq, gk, gv, go = run(finish_pair_body, [square] * 4, [*self_sums], us=1)
    wide = shaped((shard, hidden_cols), f32)
    gcq, gck, gcv, gco, gup, gdown = run(finish_pair_body, [square] * 4 + [wide] * 2, [*rest_sums], us=1)
    return (
        output, grad_in, grad_enc, grad_table, gains[0], gq, gk, gv, go.T, gains[1],
        gcq, gck, gcv, gco.T, gains[2], gup, gdown.T,
    )


def solution(mesh):
    rows, cols, repl = P(("dp", "tensor"), None), P("dp", "tensor"), P("tensor", "dp")
    in_specs = (
        rows, rows, P("dp", None), P("dp"), P("dp"), P(), P(None, "dp"), P("dp"), cols, cols, cols, repl,
        P("dp"), cols, cols, cols, repl, P("dp"), cols, repl,
    )
    out_specs = (
        rows, rows, P("dp", None), P(None, "dp"), P("dp"), cols, cols, cols, repl, P("dp"), cols, cols, cols,
        repl, P("dp"), cols, repl,
    )
    return jax.shard_map(on_device, mesh=mesh, in_specs=in_specs, out_specs=out_specs, check_vma=False)
```

```python
import jax
import jax.numpy as jnp
from jax import lax
from jax.experimental import pallas as pl
from jax.experimental.pallas import tpu as pltpu
from jax.sharding import PartitionSpec as P

HEADS = 8
TRUNK_BLKS = 8
BRANCHES = 4
LEAVES = 2
eps = 1e-05
bf16 = jnp.bfloat16
f32 = jnp.float32
i32 = jnp.int32
NEG = -1e30


def mm(a, b):
    return lax.dot_general(a, b, (((1,), (0,)), ((), ())), preferred_element_type=f32)


def mm_tn(a, b):
    return lax.dot_general(a, b, (((0,), (0,)), ((), ())), preferred_element_type=f32)


def mm_nt(a, b):
    return lax.dot_general(a, b, (((1,), (1,)), ((), ())), preferred_element_type=f32)


def normalize(v):
    centered = v - jnp.mean(v, axis=-1, keepdims=True)
    inv = lax.rsqrt(jnp.mean(centered * centered, axis=-1, keepdims=True) + eps)
    return centered * inv, inv


def norm_back(grad_act, resid, gain):
    normed, inv = normalize(resid)
    scaled = grad_act * gain
    mean_g = jnp.mean(scaled, axis=-1, keepdims=True)
    mean_gx = jnp.mean(scaled * normed, axis=-1, keepdims=True)
    return inv * (scaled - mean_g - normed * mean_gx), jnp.sum(grad_act * normed, axis=0, keepdims=True)


def shaped(shape, dtype):
    return jax.ShapeDtypeStruct(shape, dtype)


class Cols:
    def __init__(self, ref, start, width):
        self.ref, self.cols, self.dtype = ref, slice(start, start + width), ref.dtype
        self.shape = (ref.shape[0], width)

    def __getitem__(self, key):
        return self.ref[:, self.cols]


def part(array, width, index):
    return (array, width * index, width)


def loading(body, n_scalars, n_loads, n_ins):
    def wrapped(*refs):
        sources = refs[n_scalars : n_scalars + n_loads]
        held = refs[len(refs) - n_loads - 1 : len(refs) - 1]
        sems = refs[-1]
        copies = [pltpu.make_async_copy(src, dst, sems.at[i]) for i, (src, dst) in enumerate(zip(sources, held))]
        for one in copies:
            one.start()
        for one in copies:
            one.wait()
        body(*refs[:n_scalars], *held, *refs[n_ins : len(refs) - n_loads - 1])

    return wrapped


def run(body, outs, ins, scratch=(), us=2, load=False, limit=24):
    arrays = [item[0] if isinstance(item, tuple) else item for item in ins]
    spaces = [pltpu.SMEM if array.dtype == i32 else (pltpu.HBM if load else pltpu.VMEM) for array in arrays]
    scratch = list(scratch)

    def wrapped(*refs):
        seen = [Cols(ref, item[1], item[2]) if isinstance(item, tuple) else ref for ref, item in zip(refs, ins)]
        body(*seen, *refs[len(ins) :])

    if load:
        loads = [array for array in arrays if array.dtype != i32]
        wrapped = loading(body, len(arrays) - len(loads), len(loads), len(arrays))
        scratch += [pltpu.VMEM(array.shape, array.dtype) for array in loads]
        scratch.append(pltpu.SemaphoreType.DMA((len(loads),)))
    return pl.pallas_call(
        wrapped,
        out_shape=outs,
        in_specs=[pl.BlockSpec(memory_space=space) for space in spaces],
        out_specs=[pl.BlockSpec(memory_space=pltpu.VMEM) for _ in outs],
        scratch_shapes=scratch,
        cost_estimate=pl.CostEstimate(flops=us * 50 * 10**6, bytes_accessed=10**6, transcendentals=0),
        compiler_params=pltpu.CompilerParams(vmem_limit_bytes=limit * 1024 * 1024),
    )(*arrays)


def pack_body(trees, n_first, steps, table, n_self, n_cross, n_ffn, *refs):
    weights, later, out, outs = refs[:n_first], refs[n_first:-3], refs[-3], refs[-2:]
    for group, one in ((later[:5], outs[0]), (later[5:], outs[1])):
        at = 0
        for piece in group:
            one[:, at : at + piece.shape[1]] = piece[...]
            at += piece.shape[1]
    lines = lax.broadcasted_iota(i32, table.shape, 0)
    full = table[...].astype(f32)
    small = [n_self[...].astype(f32), n_cross[...].astype(f32), n_ffn[...].astype(f32)]
    for i in range(trees):
        small.append(jnp.sum(jnp.where(lines == steps[i], full, 0.0), axis=0, keepdims=True))
    shard = table.shape[1]
    small.append(jnp.zeros((1, out.shape[2] - len(small) * shard), f32))
    tail = jnp.broadcast_to(jnp.concatenate(small, axis=1), (8, out.shape[2])).astype(bf16)
    for d in range(out.shape[0]):
        at = 0
        for one in weights:
            out[d, :shard, at : at + one.shape[1]] = one[...]
            at += one.shape[1]
        out[d, shard:, :] = tail


def assemble_body(slots, base, near, far, out):
    for i, ref in enumerate((near, far)):
        for k in range(ref.shape[0]):
            out[slots[base + i * ref.shape[0] + k]] = ref[k]


def project_body(sc, half, other, first, act, q, kv, rows, w):
    shard = first.shape[1] - 8
    count = first.shape[0]
    for d in range(count):
        w[d * shard : (d + 1) * shard, :] = first[d, :shard, :]
    tails = [first[d, shard:, :].astype(f32)[0:1] for d in range(count)]

    def line(k):
        return jnp.concatenate([one[:, k * shard : (k + 1) * shard] for one in tails], axis=1)

    trees = (first.shape[2] // shard) - 3
    time_row = jnp.zeros((1, count * shard), f32)
    for i in range(min(trees, rows.shape[0] - 4)):
        time_row = time_row + jnp.where(sc[4] == i, line(3 + i), 0.0)
    gain = line(0)
    rows[0:1, :] = gain
    rows[1:2, :] = line(1)
    rows[2:3, :] = line(2)
    rows[3:4, :] = time_row
    own_rows = half.shape[1]
    for k in range(4):
        src = half[k] if k < 2 else other[k - 2]
        normed, _ = normalize(src.astype(f32) + time_row)
        act[pl.ds(pl.multiple_of(sc[k], 16), own_rows), :] = (normed * gain).astype(bf16)
    cols = q.shape[1]
    result = mm(act[...], w[...]).astype(bf16)
    q[...] = result[:, :cols]
    kv[...] = result[:, cols:]


def fill_kv(buffer, parts):
    rows = parts[0].shape[0]
    for index, one in enumerate(parts):
        buffer[index * rows : (index + 1) * rows, :] = one[...]
    done = len(parts) * rows
    if buffer.shape[0] > done:
        buffer[done:, :] = jnp.zeros((buffer.shape[0] - done, buffer.shape[1]), buffer.dtype)


def self_scores(sc, buffer, own, qh, h, hd, block):
    count = qh.shape[0] // block
    col = h * hd
    start = pl.multiple_of(sc[5], block)
    trunk_rows = TRUNK_BLKS * block
    keys = buffer[pl.ds(start, trunk_rows), col : col + hd]
    trunk = mm_nt(keys, qh)
    query_block = lax.broadcasted_iota(i32, (1, qh.shape[0]), 1) // block + sc[6]
    pieces = []
    for j in range(TRUNK_BLKS):
        bias = jnp.where(query_block > j, 0.0, NEG)
        pieces.append(trunk[j * block : (j + 1) * block] + bias)
    key_pos = lax.broadcasted_iota(i32, (block, block), 0)
    query_pos = lax.broadcasted_iota(i32, (block, block), 1)
    own_s, par_s = [], []
    for i in range(count):
        q_i = qh[i * block : (i + 1) * block]
        o = mm_nt(own[i * block : (i + 1) * block, col : col + hd], q_i)
        own_s.append(jnp.where(key_pos <= query_pos, o, NEG))
        par = buffer[pl.ds(pl.multiple_of(sc[8 + i], block), block), col : col + hd]
        leaf = (lax.broadcasted_iota(i32, (1, block), 1) * 0 + sc[8 + count + i]) > 0
        par_s.append(mm_nt(par, q_i) + jnp.where(leaf, 0.0, NEG))
    pieces.append(jnp.concatenate(own_s, axis=1))
    pieces.append(jnp.concatenate(par_s, axis=1))
    return pieces, keys


def out_partial(sc, source, w, kept, sent):
    own_rows = kept.shape[1]
    for k in range(4):
        p = mm_nt(source[pl.ds(pl.multiple_of(sc[k], 16), own_rows), :], w[...])
        if k < 2:
            kept[k] = p
        else:
            sent[k - 2] = p.astype(bf16)


def self_body(block, heads, n_parts, sc, q, *refs):
    parts = refs[:n_parts]
    w = refs[n_parts]
    attn, lse, kept, sent, buffer = refs[n_parts + 1 :]
    own = parts[-1]
    fill_kv(buffer, parts)
    cols = q.shape[1]
    hd = cols // heads
    count = q.shape[0] // block
    trunk_rows = TRUNK_BLKS * block
    start = pl.multiple_of(sc[5], block)
    for h in range(heads):
        col = h * hd
        qh = q[:, col : col + hd] * jnp.asarray(hd**-0.5, bf16)
        pieces, _ = self_scores(sc, buffer, own, qh, h, hd, block)
        peak = pieces[0]
        for s in pieces[1:]:
            peak = jnp.maximum(peak, s)
        peak = jnp.max(peak, axis=0, keepdims=True)
        exps = [jnp.exp(s - peak) for s in pieces]
        total = exps[0]
        for e in exps[1:]:
            total = total + e
        total = jnp.sum(total, axis=0, keepdims=True)
        inv = 1.0 / total
        lse[h : h + 1, :] = peak + jnp.log(total)
        low = [(e * inv).astype(bf16) for e in exps]
        vals = buffer[pl.ds(start, trunk_rows), cols + col : cols + col + hd]
        mixed = mm_tn(jnp.concatenate(low[:TRUNK_BLKS], axis=0), vals)
        for i in range(count):
            rows = slice(i * block, (i + 1) * block)
            par = buffer[pl.ds(pl.multiple_of(sc[8 + i], block), block), cols + col : cols + col + hd]
            both = jnp.concatenate([low[TRUNK_BLKS][:, rows], low[TRUNK_BLKS + 1][:, rows]], axis=0)
            two = jnp.concatenate([own[rows, cols + col : cols + col + hd], par], axis=0)
            attn[rows, col : col + hd] = (mixed[rows] + mm_tn(both, two)).astype(bf16)
    out_partial(sc, attn, w, kept, sent)


def norm_body(first, time_at, gain_at, resid, chip, far, rows, resid_out, act):
    for k in range(2):
        base = resid[k].astype(f32)
        if first:
            base = base + rows[time_at : time_at + 1, :]
        v = base + (chip[k].astype(f32) + far[1 - k].astype(f32))
        resid_out[k] = v
        normed, _ = normalize(v)
        act[k] = (normed * rows[gain_at : gain_at + 1, :]).astype(bf16)


def both_halves(own, other):
    r, d = own.shape[1], own.shape[2]
    return jnp.concatenate([own[...].reshape(2 * r, d), other[...].reshape(2 * r, d)], axis=0)


def split_store(p, kept, sent):
    r = kept.shape[1]
    for k in range(2):
        kept[k] = p[k * r : (k + 1) * r]
        sent[k] = p[(2 + k) * r : (3 + k) * r].astype(bf16)


def cross_body(heads, n_enc, own, other, *refs):
    encs = refs[:n_enc]
    w, q, kv, low_out, lse, kept, sent = refs[n_enc:]
    act = both_halves(own, other)
    cols = q.shape[1]
    hd = cols // heads
    queries = mm(act, w[:, :cols]).astype(bf16)
    q[...] = queries
    pairs = mm(jnp.concatenate([enc[...] for enc in encs], axis=0), w[:, cols : 3 * cols]).astype(bf16)
    kv[...] = pairs
    for h in range(heads):
        sl = slice(h * hd, (h + 1) * hd)
        s = mm_nt(pairs[:, sl], queries[:, sl] * jnp.asarray(hd**-0.5, bf16))
        peak = jnp.max(s, axis=0, keepdims=True)
        e = jnp.exp(s - peak)
        total = jnp.sum(e, axis=0, keepdims=True)
        lse[h : h + 1, :] = peak + jnp.log(total)
        vals = pairs[:, cols + h * hd : cols + (h + 1) * hd]
        low_out[:, sl] = mm_tn((e * (1.0 / total)).astype(bf16), vals).astype(bf16)
    split_store(mm_nt(low_out[...], w[:, 3 * cols : 4 * cols]), kept, sent)


def ffn_body(own, other, g_own, g_other, up, down_t, hidden, grad_pre, kept, sent):
    r = own.shape[1]
    for k in range(4):
        act = own[k] if k < 2 else other[k - 2]
        top = g_own[k] if k < 2 else g_other[k - 2]
        pre = mm(act, up[...])
        cdf = 0.5 * (1.0 + lax.erf(pre * 0.7071067811865476))
        hidden[k * r : (k + 1) * r, :] = (pre * cdf).astype(bf16)
        slope = cdf + pre * (jnp.exp(-0.5 * pre * pre) * 0.3989422804014327)
        gp = (mm(top, down_t[...]) * slope).astype(bf16)
        grad_pre[k * r : (k + 1) * r, :] = gp
        p = mm_nt(gp, up[...])
        if k < 2:
            kept[k] = p
        else:
            sent[k - 2] = p.astype(bf16)


def relative(slots, base, scratch, value, kept, sent):
    scratch[...] = value.reshape(scratch.shape).astype(bf16)
    for i, ref in enumerate((kept, sent)):
        for k in range(ref.shape[0]):
            ref[k] = scratch[slots[base + i * ref.shape[0] + k]]


def grads_body(n_enc, slots, *refs):
    own, other, top_own, top_other, grad_q, low_in = refs[:6]
    encs, grad_encs = refs[6 : 6 + n_enc], refs[6 + n_enc : 6 + 2 * n_enc]
    ffn_own, ffn_other, g_own, g_other, hidden, grad_pre, near, far, scratch = refs[6 + 2 * n_enc :]
    sums = [
        mm_tn(both_halves(own, other), grad_q[...]),
        mm_tn(
            jnp.concatenate([one[...] for one in encs], axis=0), jnp.concatenate([one[...] for one in grad_encs], axis=0)
        ),
        mm_tn(both_halves(top_own, top_other), low_in[...]),
        mm_tn(both_halves(ffn_own, ffn_other), grad_pre[...]),
        mm_tn(both_halves(g_own, g_other), hidden[...]),
    ]
    relative(slots, 2 * near.shape[0], scratch, jnp.concatenate(sums, axis=1), near, far)


def out_body(hidden, down_t, kept, sent):
    split_store(mm_nt(hidden[...], down_t[...]), kept, sent)


def back_body(gain_at, base, chip, far, resid, rows, grad, low, dgain):
    for k in range(2):
        g = chip[k].astype(f32) + far[1 - k].astype(f32)
        back, sums = norm_back(g, resid[k], rows[gain_at : gain_at + 1, :])
        v = base[k].astype(f32) + back
        grad[k] = v
        low[k] = v.astype(bf16)
        if k == 0:
            dgain[...] = sums


def inner_rows(grad, out):
    return (grad.astype(f32) * out.astype(f32)).T


def cross_back_body(heads, g_own, g_other, q, kv, low_in, lse, w, grad_q, kept, sent, *grad_encs):
    top = both_halves(g_own, g_other)
    cols = q.shape[1]
    hd = cols // heads
    grad_mixed = mm(top, w[:, 3 * cols : 4 * cols]).astype(bf16)
    inner = inner_rows(grad_mixed, low_in[...])
    enc_rows = grad_encs[0].shape[0]
    for h in range(heads):
        sl = slice(h * hd, (h + 1) * hd)
        vl = slice(cols + h * hd, cols + (h + 1) * hd)
        qh = q[:, sl] * jnp.asarray(hd**-0.5, bf16)
        gh = grad_mixed[:, sl]
        probs = jnp.exp(mm_nt(kv[:, sl], qh) - lse[h : h + 1, :])
        grad_v = mm(probs.astype(bf16), gh).astype(bf16)
        delta = jnp.sum(inner[sl], axis=0, keepdims=True)
        ds = (probs * (mm_nt(kv[:, vl], gh) - delta)).astype(bf16)
        grad_k = mm(ds, qh).astype(bf16)
        for i, one in enumerate(grad_encs):
            one[:, sl] = grad_k[i * enc_rows : (i + 1) * enc_rows]
            one[:, vl] = grad_v[i * enc_rows : (i + 1) * enc_rows]
        grad_q[:, sl] = (mm_tn(ds, kv[:, sl]) * hd**-0.5).astype(bf16)
    split_store(mm_nt(grad_q[...], w[:, :cols]), kept, sent)


def enc_body(n_enc, w, *refs):
    parts, out = refs[:n_enc], refs[n_enc]
    total = parts[0][...].astype(f32)
    for one in parts[1:]:
        total = total + one[...].astype(f32)
    cols = total.shape[1] // 2
    out[...] = mm_nt(total.astype(bf16), w[:, cols : 3 * cols]).astype(bf16)


def self_back_body(block, heads, n_parts, sc, g_own, g_other, q, attn, lse, *refs):
    parts = refs[:n_parts]
    w = refs[n_parts]
    outs = refs[n_parts + 1 :]
    top, ds_trunk, ds_near, grad_own = outs[:4]
    remote = outs[4 : 4 + n_parts - 1]
    buffer, sums = outs[4 + n_parts - 1 :]
    own = parts[-1]
    fill_kv(buffer, parts)
    sums[...] = jnp.zeros(sums.shape, f32)
    own_rows = g_own.shape[1]
    for k in range(4):
        src = g_own[k] if k < 2 else g_other[k - 2]
        top[pl.ds(pl.multiple_of(sc[k], 16), own_rows), :] = src
    cols = q.shape[1]
    hd = cols // heads
    count = q.shape[0] // block
    trunk_rows = TRUNK_BLKS * block
    start = pl.multiple_of(sc[5], block)
    grad_attn = mm(top[...], w[...]).astype(bf16)
    inner = inner_rows(grad_attn, attn[...])
    rows_all = own.shape[0]
    base = (n_parts - 1) * rows_all
    for h in range(heads):
        col = h * hd
        sl, vl = slice(col, col + hd), slice(cols + col, cols + col + hd)
        qh = q[:, sl] * jnp.asarray(hd**-0.5, bf16)
        gh = grad_attn[:, sl]
        pieces, keys = self_scores(sc, buffer, own, qh, h, hd, block)
        delta = jnp.sum(inner[sl], axis=0, keepdims=True)
        level = lse[h : h + 1, :]
        vals = buffer[pl.ds(start, trunk_rows), vl]
        probs = jnp.exp(jnp.concatenate(pieces[:TRUNK_BLKS], axis=0) - level)
        ds = (probs * (mm_nt(vals, gh) - delta)).astype(bf16)
        ds_trunk[h] = ds
        sums[pl.ds(start, trunk_rows), sl] += mm(ds, qh)
        sums[pl.ds(start, trunk_rows), vl] += mm(probs.astype(bf16), gh)
        for i in range(count):
            rows = slice(i * block, (i + 1) * block)
            par_at = pl.ds(pl.multiple_of(sc[8 + i], block), block)
            own_at = slice(base + i * block, base + (i + 1) * block)
            q_i, g_i = qh[rows], gh[rows]
            near = ((pieces[TRUNK_BLKS], own_at), (pieces[TRUNK_BLKS + 1], par_at))
            for j, (piece, at) in enumerate(near):
                p = jnp.exp(piece[:, rows] - level[:, rows])
                d = (p * (mm_nt(buffer[at, vl], g_i) - delta[:, rows])).astype(bf16)
                ds_near[h, j, :, rows] = d
                sums[at, sl] += mm(d, q_i)
                sums[at, vl] += mm(p.astype(bf16), g_i)
    for index, one in enumerate(remote):
        one[...] = sums[index * rows_all : (index + 1) * rows_all, :].astype(bf16)
    grad_own[...] = sums[base : base + rows_all, :]


def self_rest_body(block, heads, n_parts, sc, act, top, attn, ds_trunk, ds_near, *refs):
    parts = refs[:n_parts]
    wq, sum_q, sum_o, grad_act, grad_q, buffer = refs[n_parts:]
    fill_kv(buffer, parts)
    own = parts[-1]
    cols = grad_q.shape[1]
    hd = cols // heads
    trunk_rows = TRUNK_BLKS * block
    start = pl.multiple_of(sc[5], block)
    for h in range(heads):
        sl = slice(h * hd, (h + 1) * hd)
        trunk = mm_tn(ds_trunk[h], buffer[pl.ds(start, trunk_rows), sl])
        for i in range(grad_q.shape[0] // block):
            rows = slice(i * block, (i + 1) * block)
            par = buffer[pl.ds(pl.multiple_of(sc[8 + i], block), block), sl]
            both = jnp.concatenate([ds_near[h, 0, :, rows], ds_near[h, 1, :, rows]], axis=0)
            near = mm_tn(both, jnp.concatenate([own[rows, sl], par], axis=0))
            grad_q[rows, sl] = ((trunk[rows] + near) * hd**-0.5).astype(bf16)
    sum_q[...] = mm_tn(act[...], grad_q[...])
    sum_o[...] = mm_tn(top[...], attn[...])
    grad_act[...] = mm_nt(grad_q[...], wq[...])


def self_end_body(n_parts, sc, slots, act, grad_own, *refs):
    remote = refs[: n_parts - 1]
    wk, wv, sum_q, sum_o, grad_act, near, far, kept, sent, total, scratch = refs[n_parts - 1 :]
    t = grad_own[...]
    for one in remote:
        t = t + one[...].astype(f32)
    total[...] = t.astype(bf16)
    cols = sum_q.shape[1]
    own_rows = kept.shape[1]
    for k in range(4):
        at = pl.ds(pl.multiple_of(sc[k], 16), own_rows)
        p = grad_act[at, :] + mm_nt(total[at, :cols], wk[...]) + mm_nt(total[at, cols:], wv[...])
        if k < 2:
            kept[k] = p
        else:
            sent[k - 2] = p.astype(bf16)
    weights = jnp.concatenate([sum_q[...], mm_tn(act[...], total[...]), sum_o[...]], axis=1)
    relative(slots, 2 * near.shape[0], scratch, weights, near, far)


def vector_body(tensor, trees, sc, kept, sent, half, other, grad_mid, rows, dgain_cross, dgain_ffn, out):
    gain = rows[0:1, :]
    dgain = jnp.zeros(gain.shape, f32)
    column = jnp.sum(grad_mid[0], axis=0, keepdims=True)
    for k in range(4):
        g = kept[k] if k < 2 else sent[k - 2].astype(f32)
        src = half[k] if k < 2 else other[k - 2]
        back, one = norm_back(g, src.astype(f32) + rows[3:4, :], gain)
        dgain = dgain + one
        column = column + jnp.sum(back, axis=0, keepdims=True)
    lines = lax.broadcasted_iota(i32, (out.shape[1], gain.shape[1]), 0)
    block = jnp.where(lines == 3 + sc[4], column, 0.0)
    for i, one in enumerate((dgain, dgain_cross[...], dgain_ffn[...])):
        block = jnp.where(lines == i, one, block)
    shard = out.shape[2]
    for d in range(out.shape[0] // tensor):
        for t in range(tensor):
            out[d * tensor + t] = block[:, d * shard : (d + 1) * shard]


def last_body(chip, far, tokens, grad_mid, rows, grad_in):
    g = chip[0] + far[...].astype(f32)
    back, _ = norm_back(g, tokens[...].astype(f32) + rows[3:4, :], rows[0:1, :])
    grad_in[...] = grad_mid[0] + back


def small_body(trees, steps, received, gains, table):
    total = received[0]
    for k in range(1, received.shape[0]):
        total = total + received[k]
    gains[...] = total[:8]
    lines = lax.broadcasted_iota(i32, table.shape, 0)
    sums = jnp.zeros(table.shape, f32)
    for i in range(trees):
        sums = sums + jnp.where(lines == steps[i], total[3 + i : 4 + i], 0.0)
    table[...] = sums


def finish_pair_body(near, far, *outs):
    total = near[0].astype(f32) + far[0].astype(f32)
    at = 0
    for one in outs:
        one[...] = total[:, at : at + one.shape[1]]
        at += one.shape[1]


def xor_route(axis, bit):
    return [(i, i ^ bit) for i in range(lax.axis_size(axis))]


def sibling(x):
    return lax.ppermute(x, "tensor", xor_route("tensor", 1))


def across(x):
    return lax.ppermute(x, "tensor", xor_route("tensor", 2))


def chip_sum(kept, sent):
    return kept + sibling(sent).astype(f32)


def tie(x, *others):
    return lax.optimization_barrier((x, *others))[0]


class Doubling:
    def __init__(self, x):
        self.held = x[None]
        self.bit = lax.axis_size("dp") // 2
        self.received = None
        self.send()

    def send(self):
        if self.bit > 1:
            self.received = lax.ppermute(self.held, "dp", xor_route("dp", self.bit))

    def step(self, *dues):
        if self.bit > 1:
            self.held = jnp.concatenate([self.held, tie(self.received, *dues)], axis=0)
            self.bit //= 2
            self.send()
        return self.held

    def end(self, *dues):
        while self.bit > 1:
            self.step(*dues)
        return self.held


def neighbour(x):
    return lax.ppermute(x, "dp", xor_route("dp", 1))


class Halving:
    def __init__(self, near, far):
        self.bit = 2
        self.near, self.received = near, neighbour(far)

    def step(self, *dues):
        self.received = tie(self.received, *dues)
        if self.bit >= lax.axis_size("dp"):
            return self.received
        total = (self.near.astype(f32) + self.received.astype(f32)).astype(bf16)
        middle = total.shape[0] // 2
        self.near = total[:middle]
        self.received = lax.ppermute(total[middle:], "dp", xor_route("dp", self.bit))
        self.bit *= 2
        return self.near

    def end(self, *dues):
        while self.bit < lax.axis_size("dp"):
            self.step(*dues)
        return self.near, tie(self.received, *dues)


def on_device(
    tokens_in, grad_out, enc_states, parents, tree_ids, timesteps, time_table, norm_self,
    w_query, w_key, w_value, w_out, norm_cross, c_query, c_key, c_value, c_out, norm_ffn,
    w_hidden, w_back,
):
    count = lax.axis_size("dp")
    tensor = lax.axis_size("tensor")
    heads = HEADS // tensor
    blocks_dev = parents.shape[0]
    tree_blocks = TRUNK_BLKS + BRANCHES * (1 + LEAVES)
    group = tree_blocks // blocks_dev
    hops_back = group - 1
    me = lax.axis_index("tensor")
    dp_index = lax.axis_index("dp")
    logical_dev = (dp_index - group // 2) % count
    trees = timesteps.shape[0]
    width = tokens_in.shape[1]
    own_rows = tokens_in.shape[0]
    token_rows = own_rows * tensor
    block = token_rows // blocks_dev
    shard = norm_self.shape[0]
    cols = w_query.shape[1]
    hidden_cols = w_hidden.shape[1]
    packed, cross_pack, ffn_pack = run(
        lambda *refs: pack_body(trees, 3, *refs),
        [shaped((count, shard + 8, 3 * cols), bf16), shaped((shard, 5 * cols), bf16), shaped((shard, 2 * hidden_cols), bf16)],
        [
            timesteps, time_table, norm_self[None], norm_cross[None], norm_ffn[None],
            w_query, w_key, w_value, c_query, c_key, c_value, c_out.T, w_out.T, w_hidden, w_back.T,
        ],
        load=True,
        limit=60,
    )
    first = lax.all_to_all(packed, "dp", 0, 0)
    tokens_half = jnp.stack([tokens_in, across(tie(tokens_in, packed))])
    tokens_other = sibling(tokens_half)
    grad_half = jnp.stack([grad_out, across(tie(grad_out, packed))])
    grad_other = sibling(grad_half)
    cross_chain = Doubling(cross_pack)
    ffn_chain = Doubling(ffn_pack)

    def turn(distance):
        return [
            ((l + group // 2) % count, (l - l % group + (l + distance) % group + group // 2) % count)
            for l in range(count)
        ]

    position = logical_dev % group
    lead_blocks = group // 2 * blocks_dev
    parent_log = (parents - lead_blocks) % (count * blocks_dev)
    parent_rel = parent_log - logical_dev // group * tree_blocks
    query_block = position * blocks_dev + jnp.arange(blocks_dev, dtype=i32)
    is_leaf = query_block >= TRUNK_BLKS + BRANCHES
    shift = (hops_back - position) * blocks_dev
    parent_at = jnp.where(is_leaf, parent_rel, query_block) + shift
    step_id = jnp.sum(jnp.where(jnp.arange(trees, dtype=i32) == tree_ids[0], timesteps, 0))
    scalars = jnp.concatenate(
        [
            (me ^ jnp.array([0, 2, 1, 3], i32)) * own_rows,
            jnp.stack([tree_ids[0], shift * block, position * blocks_dev, step_id]),
            parent_at * block,
            is_leaf.astype(i32),
        ]
    ).astype(i32)
    bits = count.bit_length() - 1
    near_masks = [sum(((k >> j) & 1) * (count >> (j + 1)) for j in range(bits - 1)) for k in range(count // 2)]
    half_masks = [sum(((k >> j) & 1) * (count >> (j + 1)) for j in range(bits - 1)) for k in range(count // 2)]
    masks = near_masks + [m | 1 for m in near_masks] + half_masks + [m | 1 for m in half_masks] + [0]
    slots = (dp_index ^ jnp.array(masks, i32)).astype(i32)

    def assemble(near, far):
        far = far if far is not None else neighbour(near)
        (full,) = run(
            lambda *refs: assemble_body(refs[0], 0, *refs[1:]),
            [shaped((count,) + near.shape[1:], bf16)],
            [slots, near, far],
            us=1,
        )
        return full.reshape(width, near.shape[2])

    half = (2, own_rows, width)
    act_self, q, kv, rows, qkv_w = run(
        project_body,
        [
            shaped((token_rows, width), bf16), shaped((token_rows, cols), bf16),
            shaped((token_rows, 2 * cols), bf16), shaped((4 + trees, width), f32),
            shaped((width, 3 * cols), bf16),
        ],
        [scalars, tokens_half, tokens_other, first],
    )
    cross_chain.step(kv)
    cross_near = cross_chain.end()
    rest_w = assemble(cross_near, neighbour(cross_near))
    w_o = part(rest_w, cols, 4)

    def later(distance):
        return [
            ((l + group // 2) % count, (l + distance + group // 2) % count)
            for l in range(count)
            if l % group + distance < group
        ]

    parts = [lax.ppermute(kv, "dp", later(d)) for d in range(hops_back, 0, -1)] + [kv]
    buffer_rows = group * token_rows + max(0, TRUNK_BLKS - blocks_dev) * block
    ffn_chain.step(kv)
    ffn_near = ffn_chain.end()
    q = tie(q, grad_other)
    attn, lse, kept, sent = run(
        lambda *refs: self_body(block, heads, group, *refs),
        [shaped((token_rows, cols), bf16), shaped((8, token_rows), f32), shaped(half, f32), shaped(half, bf16)],
        [scalars, q, *parts, w_o],
        [pltpu.VMEM((buffer_rows, 2 * cols), bf16)],
        us=5,
    )
    enc_rows = enc_states.shape[0]
    enc_sent = tie(enc_states, attn)
    enc_parts = [enc_states] + [lax.ppermute(enc_sent, "dp", turn(d)) for d in range(1, group)]
    chip = chip_sum(kept, sent).astype(bf16)
    ffn_far = neighbour(tie(ffn_near, attn))
    resid_mid, act_own = run(
        lambda *refs: norm_body(True, 3, 1, *refs),
        [shaped(half, f32), shaped(half, bf16)],
        [tokens_half, chip, tie(across(chip), ffn_far, *enc_parts), rows],
        us=1,
    )
    act_other = sibling(act_own)
    ffn_w = assemble(ffn_near, ffn_far)
    up_w, down_w = part(ffn_w, hidden_cols, 0), part(ffn_w, hidden_cols, 1)
    cross_q, cross_kv, cross_low, cross_lse, kept, sent = run(
        lambda *refs: cross_body(heads, group, *refs),
        [
            shaped((token_rows, cols), bf16), shaped((group * enc_rows, 2 * cols), bf16),
            shaped((token_rows, cols), bf16), shaped((8, token_rows), f32), shaped(half, f32), shaped(half, bf16),
        ],
        [act_own, act_other, *enc_parts, rest_w],
    )
    chip = chip_sum(kept, sent).astype(bf16)
    resid_ffn, ffn_own = run(
        lambda *refs: norm_body(False, 3, 2, *refs),
        [shaped(half, f32), shaped(half, bf16)],
        [resid_mid, chip, tie(across(chip)), rows],
        us=1,
    )
    ffn_other = sibling(ffn_own)
    hidden, grad_pre, kept, sent = run(
        ffn_body,
        [
            shaped((token_rows, hidden_cols), bf16), shaped((token_rows, hidden_cols), bf16),
            shaped(half, f32), shaped(half, bf16),
        ],
        [ffn_own, ffn_other, grad_half, grad_other, up_w, down_w],
        us=3,
    )
    chip = chip_sum(kept, sent).astype(bf16)
    out_kept, out_sent = run(
        out_body, [shaped(half, f32), shaped(half, bf16)], [hidden, down_w]
    )
    grad_resid_ffn, top_own, dgain_ffn = run(
        lambda *refs: back_body(2, *refs),
        [shaped(half, f32), shaped(half, bf16), shaped((1, width), f32)],
        [grad_half, chip, tie(across(chip), out_sent), resid_ffn, rows],
        us=1,
    )
    top_other = sibling(top_own)
    grad_cq, kept, sent, *grad_encs = run(
        lambda *refs: cross_back_body(heads, *refs),
        [shaped((token_rows, cols), bf16), shaped(half, f32), shaped(half, bf16)]
        + [shaped((enc_rows, 2 * cols), bf16)] * group,
        [top_own, top_other, cross_q, cross_kv, cross_low, cross_lse, rest_w],
        us=3,
    )
    chip = chip_sum(kept, sent).astype(bf16)
    split = (count // 2, shard, 4 * cols + 2 * hidden_cols)
    rest_kept, rest_sent = run(
        lambda *refs: grads_body(group, *refs),
        [shaped(split, bf16), shaped(split, bf16)],
        [
            slots, tie(act_own, chip), act_other, top_own, top_other, grad_cq, cross_low, *enc_parts, *grad_encs,
            ffn_own, ffn_other, grad_half, grad_other, hidden, grad_pre,
        ],
        [pltpu.VMEM((count, shard, split[2]), bf16)],
        us=4,
    )
    rest_chain = Halving(rest_kept, rest_sent)
    out_chip = out_kept + sibling(tie(out_sent, chip)).astype(f32)
    grad_encs = [grad_encs[0]] + [
        lax.ppermute(tie(grad_encs[d], rest_sent), "dp", [(b, a) for a, b in turn(d)]) for d in range(1, group)
    ]
    grad_resid_mid, self_own, dgain_cross = run(
        lambda *refs: back_body(1, *refs),
        [shaped(half, f32), shaped(half, bf16), shaped((1, width), f32)],
        [grad_resid_ffn, chip, tie(across(chip), rest_sent, out_chip), resid_mid, rows],
        us=1,
    )
    (enc_part,) = run(
        lambda *refs: enc_body(group, *refs),
        [shaped((enc_rows, width), bf16)],
        [rest_w, grad_encs[0], *grad_encs[1:]],
        us=1,
    )
    enc_chip = (enc_part.astype(f32) + sibling(enc_part).astype(f32)).astype(bf16)
    enc_far = across(enc_chip)
    self_other = sibling(self_own)
    out_far = across(tie(out_chip[1].astype(bf16), self_own))
    kv_shape = (token_rows, 2 * cols)
    top, ds_trunk, ds_near, grad_own, *remote = run(
        lambda *refs: self_back_body(block, heads, group, *refs),
        [
            shaped((token_rows, width), bf16), shaped((heads, TRUNK_BLKS * block, token_rows), bf16),
            shaped((heads, 2, block, token_rows), bf16), shaped(kv_shape, f32),
        ]
        + [shaped(kv_shape, bf16)] * hops_back,
        [scalars, self_own, self_other, q, attn, lse, *parts, w_o],
        [pltpu.VMEM((buffer_rows, 2 * cols), bf16), pltpu.VMEM((buffer_rows, 2 * cols), f32)],
        us=8,
    )
    back = [
        lax.ppermute(one, "dp", [(b, a) for a, b in later(d)]) for one, d in zip(remote, range(hops_back, 0, -1))
    ]
    sum_q, sum_o, grad_act = run(
        lambda *refs: self_rest_body(block, heads, group, *refs),
        [shaped((width, cols), f32), shaped((width, cols), f32), shaped((token_rows, width), f32)],
        [scalars, act_self, top, attn, ds_trunk, ds_near, *parts, part(qkv_w, cols, 0)],
        [pltpu.VMEM((token_rows, cols), bf16), pltpu.VMEM((buffer_rows, 2 * cols), bf16)],
        us=4,
    )
    held = rest_chain.step(grad_act)
    grad_own = tie(grad_own, held)
    split = (count // 2, shard, 4 * cols)
    self_kept, self_sent, kept, sent = run(
        lambda *refs: self_end_body(group, *refs),
        [shaped(split, bf16), shaped(split, bf16), shaped(half, f32), shaped(half, bf16)],
        [
            scalars, slots, act_self, grad_own, *back, part(qkv_w, cols, 1), part(qkv_w, cols, 2), sum_q, sum_o, grad_act,
        ],
        [pltpu.VMEM(kv_shape, bf16), pltpu.VMEM((count, shard, 4 * cols), bf16)],
        us=3,
    )
    self_chain = Halving(self_kept, self_sent)
    chip = chip_sum(kept, sent)
    (vectors,) = run(
        lambda *refs: vector_body(tensor, trees, *refs),
        [shaped((count * tensor, -(-(3 + trees) // 8) * 8, shard), f32)],
        [scalars, tie(kept, chip), sent, tokens_half, tokens_other, grad_resid_mid, rows, dgain_cross, dgain_ffn],
    )
    received = lax.all_to_all(vectors, ("dp", "tensor"), 0, 0)
    (grad_in,) = run(
        last_body,
        [shaped((own_rows, width), f32)],
        [chip, across(chip[1].astype(bf16)), tokens_in, grad_resid_mid, rows],
        us=1,
    )
    self_chain.step()
    rest_chain.step(sent)
    output = (resid_ffn[0] + (out_chip[0] + out_far.astype(f32))).astype(bf16)
    grad_enc = enc_chip.astype(f32) + enc_far.astype(f32)
    self_sums, rest_sums = self_chain.end(), rest_chain.end()
    gains, grad_table = run(
        lambda *refs: small_body(trees, *refs),
        [shaped((8, shard), f32), shaped((time_table.shape[0], shard), f32)],
        [timesteps, received],
        us=1,
    )
    square = shaped((shard, cols), f32)
    gq, gk, gv, go = run(finish_pair_body, [square] * 4, [*self_sums], us=1)
    wide = shaped((shard, hidden_cols), f32)
    gcq, gck, gcv, gco, gup, gdown = run(finish_pair_body, [square] * 4 + [wide] * 2, [*rest_sums], us=1)
    return (
        output, grad_in, grad_enc, grad_table, gains[0], gq, gk, gv, go.T, gains[1],
        gcq, gck, gcv, gco.T, gains[2], gup, gdown.T,
    )


def solution(mesh):
    rows, cols, repl = P(("dp", "tensor"), None), P("dp", "tensor"), P("tensor", "dp")
    in_specs = (
        rows, rows, P("dp", None), P("dp"), P("dp"), P(), P(None, "dp"), P("dp"), cols, cols, cols, repl,
        P("dp"), cols, cols, cols, repl, P("dp"), cols, repl,
    )
    out_specs = (
        rows, rows, P("dp", None), P(None, "dp"), P("dp"), cols, cols, cols, repl, P("dp"), cols, cols, cols,
        repl, P("dp"), cols, repl,
    )
    return jax.shard_map(on_device, mesh=mesh, in_specs=in_specs, out_specs=out_specs, check_vma=False)
```

```python
import jax
import jax.numpy as jnp
from jax import lax
from jax.experimental import pallas as pl
from jax.experimental.pallas import tpu as pltpu
from jax.sharding import PartitionSpec as P

HEADS = 8
TRUNK_BLKS = 8
BRANCHES = 4
LEAVES = 2
eps = 1e-05
bf16 = jnp.bfloat16
f32 = jnp.float32
i32 = jnp.int32
NEG = -1e30


def mm(a, b):
    return lax.dot_general(a, b, (((1,), (0,)), ((), ())), preferred_element_type=f32)


def mm_tn(a, b):
    return lax.dot_general(a, b, (((0,), (0,)), ((), ())), preferred_element_type=f32)


def mm_nt(a, b):
    return lax.dot_general(a, b, (((1,), (1,)), ((), ())), preferred_element_type=f32)


def normalize(v):
    centered = v - jnp.mean(v, axis=-1, keepdims=True)
    inv = lax.rsqrt(jnp.mean(centered * centered, axis=-1, keepdims=True) + eps)
    return centered * inv, inv


def norm_back(grad_act, resid, gain):
    normed, inv = normalize(resid)
    scaled = grad_act * gain
    mean_g = jnp.mean(scaled, axis=-1, keepdims=True)
    mean_gx = jnp.mean(scaled * normed, axis=-1, keepdims=True)
    return inv * (scaled - mean_g - normed * mean_gx), jnp.sum(grad_act * normed, axis=0, keepdims=True)


def shaped(shape, dtype):
    return jax.ShapeDtypeStruct(shape, dtype)


class Cols:
    def __init__(self, ref, start, width):
        self.ref, self.cols, self.dtype = ref, slice(start, start + width), ref.dtype
        self.shape = (ref.shape[0], width)

    def __getitem__(self, key):
        return self.ref[:, self.cols]


def part(array, width, index):
    return (array, width * index, width)


def loading(body, n_scalars, n_loads, n_ins):
    def wrapped(*refs):
        sources = refs[n_scalars : n_scalars + n_loads]
        held = refs[len(refs) - n_loads - 1 : len(refs) - 1]
        sems = refs[-1]
        copies = [pltpu.make_async_copy(src, dst, sems.at[i]) for i, (src, dst) in enumerate(zip(sources, held))]
        for one in copies:
            one.start()
        for one in copies:
            one.wait()
        body(*refs[:n_scalars], *held, *refs[n_ins : len(refs) - n_loads - 1])

    return wrapped


def run(body, outs, ins, scratch=(), us=2, load=False, limit=24):
    arrays = [item[0] if isinstance(item, tuple) else item for item in ins]
    spaces = [pltpu.SMEM if array.dtype == i32 else (pltpu.HBM if load else pltpu.VMEM) for array in arrays]
    scratch = list(scratch)

    def wrapped(*refs):
        seen = [Cols(ref, item[1], item[2]) if isinstance(item, tuple) else ref for ref, item in zip(refs, ins)]
        body(*seen, *refs[len(ins) :])

    if load:
        loads = [array for array in arrays if array.dtype != i32]
        wrapped = loading(body, len(arrays) - len(loads), len(loads), len(arrays))
        scratch += [pltpu.VMEM(array.shape, array.dtype) for array in loads]
        scratch.append(pltpu.SemaphoreType.DMA((len(loads),)))
    return pl.pallas_call(
        wrapped,
        out_shape=outs,
        in_specs=[pl.BlockSpec(memory_space=space) for space in spaces],
        out_specs=[pl.BlockSpec(memory_space=pltpu.VMEM) for _ in outs],
        scratch_shapes=scratch,
        cost_estimate=pl.CostEstimate(flops=us * 100 * 10**6, bytes_accessed=10**6, transcendentals=0),
        compiler_params=pltpu.CompilerParams(vmem_limit_bytes=limit * 1024 * 1024),
    )(*arrays)


def side_body(n_first, *refs):
    ins, outs = refs[:-2], refs[-2:]
    for group, one in ((ins[:n_first], outs[0]), (ins[n_first:], outs[1])):
        at = 0
        for piece in group:
            one[:, at : at + piece.shape[1]] = piece[...]
            at += piece.shape[1]


def pack_body(trees, steps, table, n_self, n_cross, n_ffn, *refs):
    weights, out = refs[:-1], refs[-1]
    lines = lax.broadcasted_iota(i32, table.shape, 0)
    full = table[...].astype(f32)
    small = [n_self[...].astype(f32), n_cross[...].astype(f32), n_ffn[...].astype(f32)]
    for i in range(trees):
        small.append(jnp.sum(jnp.where(lines == steps[i], full, 0.0), axis=0, keepdims=True))
    shard = table.shape[1]
    small.append(jnp.zeros((1, out.shape[2] - len(small) * shard), f32))
    tail = jnp.broadcast_to(jnp.concatenate(small, axis=1), (8, out.shape[2])).astype(bf16)
    for d in range(out.shape[0]):
        at = 0
        for one in weights:
            out[d, :shard, at : at + one.shape[1]] = one[...]
            at += one.shape[1]
        out[d, shard:, :] = tail


def assemble_body(slots, base, near, far, out):
    for i, ref in enumerate((near, far)):
        for k in range(ref.shape[0]):
            out[slots[base + i * ref.shape[0] + k]] = ref[k]


def project_body(sc, half, other, first, act, q, kv, rows, w):
    shard = first.shape[1] - 8
    count = first.shape[0]
    for d in range(count):
        w[d * shard : (d + 1) * shard, :] = first[d, :shard, :]
    tails = [first[d, shard:, :].astype(f32)[0:1] for d in range(count)]

    def line(k):
        return jnp.concatenate([one[:, k * shard : (k + 1) * shard] for one in tails], axis=1)

    trees = (first.shape[2] // shard) - 3
    time_row = jnp.zeros((1, count * shard), f32)
    for i in range(min(trees, rows.shape[0] - 4)):
        time_row = time_row + jnp.where(sc[4] == i, line(3 + i), 0.0)
    gain = line(0)
    rows[0:1, :] = gain
    rows[1:2, :] = line(1)
    rows[2:3, :] = line(2)
    rows[3:4, :] = time_row
    own_rows = half.shape[1]
    for k in range(4):
        src = half[k] if k < 2 else other[k - 2]
        normed, _ = normalize(src.astype(f32) + time_row)
        act[pl.ds(pl.multiple_of(sc[k], 16), own_rows), :] = (normed * gain).astype(bf16)
    cols = q.shape[1]
    result = mm(act[...], w[...]).astype(bf16)
    q[...] = result[:, :cols]
    kv[...] = result[:, cols:]


def fill_kv(buffer, parts):
    rows = parts[0].shape[0]
    for index, one in enumerate(parts):
        buffer[index * rows : (index + 1) * rows, :] = one[...]
    done = len(parts) * rows
    if buffer.shape[0] > done:
        buffer[done:, :] = jnp.zeros((buffer.shape[0] - done, buffer.shape[1]), buffer.dtype)


def self_scores(sc, buffer, own, qh, h, hd, block):
    count = qh.shape[0] // block
    col = h * hd
    start = pl.multiple_of(sc[5], block)
    trunk_rows = TRUNK_BLKS * block
    keys = buffer[pl.ds(start, trunk_rows), col : col + hd]
    trunk = mm_nt(keys, qh)
    query_block = lax.broadcasted_iota(i32, (1, qh.shape[0]), 1) // block + sc[6]
    pieces = []
    for j in range(TRUNK_BLKS):
        bias = jnp.where(query_block > j, 0.0, NEG)
        pieces.append(trunk[j * block : (j + 1) * block] + bias)
    key_pos = lax.broadcasted_iota(i32, (block, block), 0)
    query_pos = lax.broadcasted_iota(i32, (block, block), 1)
    own_s, par_s = [], []
    for i in range(count):
        q_i = qh[i * block : (i + 1) * block]
        o = mm_nt(own[i * block : (i + 1) * block, col : col + hd], q_i)
        own_s.append(jnp.where(key_pos <= query_pos, o, NEG))
        par = buffer[pl.ds(pl.multiple_of(sc[8 + i], block), block), col : col + hd]
        leaf = (lax.broadcasted_iota(i32, (1, block), 1) * 0 + sc[8 + count + i]) > 0
        par_s.append(mm_nt(par, q_i) + jnp.where(leaf, 0.0, NEG))
    pieces.append(jnp.concatenate(own_s, axis=1))
    pieces.append(jnp.concatenate(par_s, axis=1))
    return pieces, keys


def out_partial(sc, source, w, kept, sent):
    own_rows = kept.shape[1]
    for k in range(4):
        p = mm_nt(source[pl.ds(pl.multiple_of(sc[k], 16), own_rows), :], w[...])
        if k < 2:
            kept[k] = p
        else:
            sent[k - 2] = p.astype(bf16)


def self_body(block, heads, n_parts, sc, q, *refs):
    parts = refs[:n_parts]
    w = refs[n_parts]
    attn, lse, kept, sent, buffer = refs[n_parts + 1 :]
    own = parts[-1]
    fill_kv(buffer, parts)
    cols = q.shape[1]
    hd = cols // heads
    count = q.shape[0] // block
    trunk_rows = TRUNK_BLKS * block
    start = pl.multiple_of(sc[5], block)
    for h in range(heads):
        col = h * hd
        qh = q[:, col : col + hd] * jnp.asarray(hd**-0.5, bf16)
        pieces, _ = self_scores(sc, buffer, own, qh, h, hd, block)
        peak = pieces[0]
        for s in pieces[1:]:
            peak = jnp.maximum(peak, s)
        peak = jnp.max(peak, axis=0, keepdims=True)
        exps = [jnp.exp(s - peak) for s in pieces]
        total = exps[0]
        for e in exps[1:]:
            total = total + e
        total = jnp.sum(total, axis=0, keepdims=True)
        inv = 1.0 / total
        lse[h : h + 1, :] = peak + jnp.log(total)
        low = [(e * inv).astype(bf16) for e in exps]
        vals = buffer[pl.ds(start, trunk_rows), cols + col : cols + col + hd]
        mixed = mm_tn(jnp.concatenate(low[:TRUNK_BLKS], axis=0), vals)
        for i in range(count):
            rows = slice(i * block, (i + 1) * block)
            par = buffer[pl.ds(pl.multiple_of(sc[8 + i], block), block), cols + col : cols + col + hd]
            both = jnp.concatenate([low[TRUNK_BLKS][:, rows], low[TRUNK_BLKS + 1][:, rows]], axis=0)
            two = jnp.concatenate([own[rows, cols + col : cols + col + hd], par], axis=0)
            attn[rows, col : col + hd] = (mixed[rows] + mm_tn(both, two)).astype(bf16)
    out_partial(sc, attn, w, kept, sent)


def norm_body(first, time_at, gain_at, resid, chip, far, rows, resid_out, act):
    for k in range(2):
        base = resid[k].astype(f32)
        if first:
            base = base + rows[time_at : time_at + 1, :]
        v = base + (chip[k].astype(f32) + far[1 - k].astype(f32))
        resid_out[k] = v
        normed, _ = normalize(v)
        act[k] = (normed * rows[gain_at : gain_at + 1, :]).astype(bf16)


def both_halves(own, other):
    r, d = own.shape[1], own.shape[2]
    return jnp.concatenate([own[...].reshape(2 * r, d), other[...].reshape(2 * r, d)], axis=0)


def split_store(p, kept, sent):
    r = kept.shape[1]
    for k in range(2):
        kept[k] = p[k * r : (k + 1) * r]
        sent[k] = p[(2 + k) * r : (3 + k) * r].astype(bf16)


def cross_body(heads, n_enc, own, other, *refs):
    encs = refs[:n_enc]
    w, q, kv, low_out, lse, kept, sent = refs[n_enc:]
    act = both_halves(own, other)
    cols = q.shape[1]
    hd = cols // heads
    queries = mm(act, w[:, :cols]).astype(bf16)
    q[...] = queries
    pairs = mm(jnp.concatenate([enc[...] for enc in encs], axis=0), w[:, cols : 3 * cols]).astype(bf16)
    kv[...] = pairs
    for h in range(heads):
        sl = slice(h * hd, (h + 1) * hd)
        s = mm_nt(pairs[:, sl], queries[:, sl] * jnp.asarray(hd**-0.5, bf16))
        peak = jnp.max(s, axis=0, keepdims=True)
        e = jnp.exp(s - peak)
        total = jnp.sum(e, axis=0, keepdims=True)
        lse[h : h + 1, :] = peak + jnp.log(total)
        vals = pairs[:, cols + h * hd : cols + (h + 1) * hd]
        low_out[:, sl] = mm_tn((e * (1.0 / total)).astype(bf16), vals).astype(bf16)
    split_store(mm_nt(low_out[...], w[:, 3 * cols : 4 * cols]), kept, sent)


def ffn_body(own, other, g_own, g_other, up, down_t, hidden, grad_pre, kept, sent):
    r = own.shape[1]
    for k in range(4):
        act = own[k] if k < 2 else other[k - 2]
        top = g_own[k] if k < 2 else g_other[k - 2]
        pre = mm(act, up[...])
        cdf = 0.5 * (1.0 + lax.erf(pre * 0.7071067811865476))
        hidden[k * r : (k + 1) * r, :] = (pre * cdf).astype(bf16)
        slope = cdf + pre * (jnp.exp(-0.5 * pre * pre) * 0.3989422804014327)
        gp = (mm(top, down_t[...]) * slope).astype(bf16)
        grad_pre[k * r : (k + 1) * r, :] = gp
        p = mm_nt(gp, up[...])
        if k < 2:
            kept[k] = p
        else:
            sent[k - 2] = p.astype(bf16)


def relative(slots, base, scratch, value, kept, sent):
    scratch[...] = value.reshape(scratch.shape).astype(bf16)
    for i, ref in enumerate((kept, sent)):
        for k in range(ref.shape[0]):
            ref[k] = scratch[slots[base + i * ref.shape[0] + k]]


def grads_body(n_enc, slots, *refs):
    own, other, top_own, top_other, grad_q, low_in = refs[:6]
    encs, grad_encs = refs[6 : 6 + n_enc], refs[6 + n_enc : 6 + 2 * n_enc]
    ffn_own, ffn_other, g_own, g_other, hidden, grad_pre, near, far, scratch = refs[6 + 2 * n_enc :]
    sums = [
        mm_tn(both_halves(own, other), grad_q[...]),
        mm_tn(
            jnp.concatenate([one[...] for one in encs], axis=0), jnp.concatenate([one[...] for one in grad_encs], axis=0)
        ),
        mm_tn(both_halves(top_own, top_other), low_in[...]),
        mm_tn(both_halves(ffn_own, ffn_other), grad_pre[...]),
        mm_tn(both_halves(g_own, g_other), hidden[...]),
    ]
    relative(slots, 2 * near.shape[0], scratch, jnp.concatenate(sums, axis=1), near, far)


def out_body(hidden, down_t, kept, sent):
    split_store(mm_nt(hidden[...], down_t[...]), kept, sent)


def back_body(gain_at, base, chip, far, resid, rows, grad, low, dgain):
    for k in range(2):
        g = chip[k].astype(f32) + far[1 - k].astype(f32)
        back, sums = norm_back(g, resid[k], rows[gain_at : gain_at + 1, :])
        v = base[k].astype(f32) + back
        grad[k] = v
        low[k] = v.astype(bf16)
        if k == 0:
            dgain[...] = sums


def inner_rows(grad, out):
    return (grad.astype(f32) * out.astype(f32)).T


def cross_back_body(heads, g_own, g_other, q, kv, low_in, lse, w, grad_q, kept, sent, *grad_encs):
    top = both_halves(g_own, g_other)
    cols = q.shape[1]
    hd = cols // heads
    grad_mixed = mm(top, w[:, 3 * cols : 4 * cols]).astype(bf16)
    inner = inner_rows(grad_mixed, low_in[...])
    enc_rows = grad_encs[0].shape[0]
    for h in range(heads):
        sl = slice(h * hd, (h + 1) * hd)
        vl = slice(cols + h * hd, cols + (h + 1) * hd)
        qh = q[:, sl] * jnp.asarray(hd**-0.5, bf16)
        gh = grad_mixed[:, sl]
        probs = jnp.exp(mm_nt(kv[:, sl], qh) - lse[h : h + 1, :])
        grad_v = mm(probs.astype(bf16), gh).astype(bf16)
        delta = jnp.sum(inner[sl], axis=0, keepdims=True)
        ds = (probs * (mm_nt(kv[:, vl], gh) - delta)).astype(bf16)
        grad_k = mm(ds, qh).astype(bf16)
        for i, one in enumerate(grad_encs):
            one[:, sl] = grad_k[i * enc_rows : (i + 1) * enc_rows]
            one[:, vl] = grad_v[i * enc_rows : (i + 1) * enc_rows]
        grad_q[:, sl] = (mm_tn(ds, kv[:, sl]) * hd**-0.5).astype(bf16)
    split_store(mm_nt(grad_q[...], w[:, :cols]), kept, sent)


def enc_body(n_enc, w, *refs):
    parts, out = refs[:n_enc], refs[n_enc]
    total = parts[0][...].astype(f32)
    for one in parts[1:]:
        total = total + one[...].astype(f32)
    cols = total.shape[1] // 2
    out[...] = mm_nt(total.astype(bf16), w[:, cols : 3 * cols]).astype(bf16)


def self_back_body(block, heads, n_parts, sc, g_own, g_other, q, attn, lse, *refs):
    parts = refs[:n_parts]
    w = refs[n_parts]
    outs = refs[n_parts + 1 :]
    top, ds_trunk, ds_near, grad_own = outs[:4]
    remote = outs[4 : 4 + n_parts - 1]
    buffer, sums = outs[4 + n_parts - 1 :]
    own = parts[-1]
    fill_kv(buffer, parts)
    sums[...] = jnp.zeros(sums.shape, f32)
    own_rows = g_own.shape[1]
    for k in range(4):
        src = g_own[k] if k < 2 else g_other[k - 2]
        top[pl.ds(pl.multiple_of(sc[k], 16), own_rows), :] = src
    cols = q.shape[1]
    hd = cols // heads
    count = q.shape[0] // block
    trunk_rows = TRUNK_BLKS * block
    start = pl.multiple_of(sc[5], block)
    grad_attn = mm(top[...], w[...]).astype(bf16)
    inner = inner_rows(grad_attn, attn[...])
    rows_all = own.shape[0]
    base = (n_parts - 1) * rows_all
    for h in range(heads):
        col = h * hd
        sl, vl = slice(col, col + hd), slice(cols + col, cols + col + hd)
        qh = q[:, sl] * jnp.asarray(hd**-0.5, bf16)
        gh = grad_attn[:, sl]
        pieces, keys = self_scores(sc, buffer, own, qh, h, hd, block)
        delta = jnp.sum(inner[sl], axis=0, keepdims=True)
        level = lse[h : h + 1, :]
        vals = buffer[pl.ds(start, trunk_rows), vl]
        probs = jnp.exp(jnp.concatenate(pieces[:TRUNK_BLKS], axis=0) - level)
        ds = (probs * (mm_nt(vals, gh) - delta)).astype(bf16)
        ds_trunk[h] = ds
        sums[pl.ds(start, trunk_rows), sl] += mm(ds, qh)
        sums[pl.ds(start, trunk_rows), vl] += mm(probs.astype(bf16), gh)
        for i in range(count):
            rows = slice(i * block, (i + 1) * block)
            par_at = pl.ds(pl.multiple_of(sc[8 + i], block), block)
            own_at = slice(base + i * block, base + (i + 1) * block)
            q_i, g_i = qh[rows], gh[rows]
            near = ((pieces[TRUNK_BLKS], own_at), (pieces[TRUNK_BLKS + 1], par_at))
            for j, (piece, at) in enumerate(near):
                p = jnp.exp(piece[:, rows] - level[:, rows])
                d = (p * (mm_nt(buffer[at, vl], g_i) - delta[:, rows])).astype(bf16)
                ds_near[h, j, :, rows] = d
                sums[at, sl] += mm(d, q_i)
                sums[at, vl] += mm(p.astype(bf16), g_i)
    for index, one in enumerate(remote):
        one[...] = sums[index * rows_all : (index + 1) * rows_all, :].astype(bf16)
    grad_own[...] = sums[base : base + rows_all, :]


def self_rest_body(block, heads, n_parts, sc, act, top, attn, ds_trunk, ds_near, *refs):
    parts = refs[:n_parts]
    wq, sum_q, sum_o, grad_act, grad_q, buffer = refs[n_parts:]
    fill_kv(buffer, parts)
    own = parts[-1]
    cols = grad_q.shape[1]
    hd = cols // heads
    trunk_rows = TRUNK_BLKS * block
    start = pl.multiple_of(sc[5], block)
    for h in range(heads):
        sl = slice(h * hd, (h + 1) * hd)
        trunk = mm_tn(ds_trunk[h], buffer[pl.ds(start, trunk_rows), sl])
        for i in range(grad_q.shape[0] // block):
            rows = slice(i * block, (i + 1) * block)
            par = buffer[pl.ds(pl.multiple_of(sc[8 + i], block), block), sl]
            both = jnp.concatenate([ds_near[h, 0, :, rows], ds_near[h, 1, :, rows]], axis=0)
            near = mm_tn(both, jnp.concatenate([own[rows, sl], par], axis=0))
            grad_q[rows, sl] = ((trunk[rows] + near) * hd**-0.5).astype(bf16)
    sum_q[...] = mm_tn(act[...], grad_q[...])
    sum_o[...] = mm_tn(top[...], attn[...])
    grad_act[...] = mm_nt(grad_q[...], wq[...])


def self_end_body(n_parts, sc, slots, act, grad_own, *refs):
    remote = refs[: n_parts - 1]
    wk, wv, sum_q, sum_o, grad_act, near, far, kept, sent, total, scratch = refs[n_parts - 1 :]
    t = grad_own[...]
    for one in remote:
        t = t + one[...].astype(f32)
    total[...] = t.astype(bf16)
    cols = sum_q.shape[1]
    own_rows = kept.shape[1]
    for k in range(4):
        at = pl.ds(pl.multiple_of(sc[k], 16), own_rows)
        p = grad_act[at, :] + mm_nt(total[at, :cols], wk[...]) + mm_nt(total[at, cols:], wv[...])
        if k < 2:
            kept[k] = p
        else:
            sent[k - 2] = p.astype(bf16)
    weights = jnp.concatenate([sum_q[...], mm_tn(act[...], total[...]), sum_o[...]], axis=1)
    relative(slots, 2 * near.shape[0], scratch, weights, near, far)


def vector_body(tensor, trees, sc, kept, sent, half, other, grad_mid, rows, dgain_cross, dgain_ffn, out):
    gain = rows[0:1, :]
    dgain = jnp.zeros(gain.shape, f32)
    column = jnp.sum(grad_mid[0], axis=0, keepdims=True)
    for k in range(4):
        g = kept[k] if k < 2 else sent[k - 2].astype(f32)
        src = half[k] if k < 2 else other[k - 2]
        back, one = norm_back(g, src.astype(f32) + rows[3:4, :], gain)
        dgain = dgain + one
        column = column + jnp.sum(back, axis=0, keepdims=True)
    lines = lax.broadcasted_iota(i32, (out.shape[1], gain.shape[1]), 0)
    block = jnp.where(lines == 3 + sc[4], column, 0.0)
    for i, one in enumerate((dgain, dgain_cross[...], dgain_ffn[...])):
        block = jnp.where(lines == i, one, block)
    shard = out.shape[2]
    for d in range(out.shape[0] // tensor):
        for t in range(tensor):
            out[d * tensor + t] = block[:, d * shard : (d + 1) * shard]


def last_body(chip, far, tokens, grad_mid, rows, grad_in):
    g = chip[0] + far[...].astype(f32)
    back, _ = norm_back(g, tokens[...].astype(f32) + rows[3:4, :], rows[0:1, :])
    grad_in[...] = grad_mid[0] + back


def small_body(trees, steps, received, gains, table):
    total = received[0]
    for k in range(1, received.shape[0]):
        total = total + received[k]
    gains[...] = total[:8]
    lines = lax.broadcasted_iota(i32, table.shape, 0)
    sums = jnp.zeros(table.shape, f32)
    for i in range(trees):
        sums = sums + jnp.where(lines == steps[i], total[3 + i : 4 + i], 0.0)
    table[...] = sums


def finish_pair_body(near, far, *outs):
    total = near[0].astype(f32) + far[0].astype(f32)
    at = 0
    for one in outs:
        one[...] = total[:, at : at + one.shape[1]]
        at += one.shape[1]


def xor_route(axis, bit):
    return [(i, i ^ bit) for i in range(lax.axis_size(axis))]


def sibling(x):
    return lax.ppermute(x, "tensor", xor_route("tensor", 1))


def across(x):
    return lax.ppermute(x, "tensor", xor_route("tensor", 2))


def chip_sum(kept, sent):
    return kept + sibling(sent).astype(f32)


def tie(x, *others):
    return lax.optimization_barrier((x, *others))[0]


class Doubling:
    def __init__(self, x):
        self.held = x[None]
        self.bit = lax.axis_size("dp") // 2
        self.received = None
        self.send()

    def send(self):
        if self.bit > 1:
            self.received = lax.ppermute(self.held, "dp", xor_route("dp", self.bit))

    def step(self, *dues):
        if self.bit > 1:
            self.held = jnp.concatenate([self.held, tie(self.received, *dues)], axis=0)
            self.bit //= 2
            self.send()
        return self.held

    def end(self, *dues):
        while self.bit > 1:
            self.step(*dues)
        return self.held


def neighbour(x):
    return lax.ppermute(x, "dp", xor_route("dp", 1))


class Halving:
    def __init__(self, near, far):
        self.bit = 2
        self.near, self.received = near, neighbour(far)

    def step(self, *dues):
        self.received = tie(self.received, *dues)
        if self.bit >= lax.axis_size("dp"):
            return self.received
        total = (self.near.astype(f32) + self.received.astype(f32)).astype(bf16)
        middle = total.shape[0] // 2
        self.near = total[:middle]
        self.received = lax.ppermute(total[middle:], "dp", xor_route("dp", self.bit))
        self.bit *= 2
        return self.near

    def end(self, *dues):
        while self.bit < lax.axis_size("dp"):
            self.step(*dues)
        return self.near, tie(self.received, *dues)


def on_device(
    tokens_in, grad_out, enc_states, parents, tree_ids, timesteps, time_table, norm_self,
    w_query, w_key, w_value, w_out, norm_cross, c_query, c_key, c_value, c_out, norm_ffn,
    w_hidden, w_back,
):
    count = lax.axis_size("dp")
    tensor = lax.axis_size("tensor")
    heads = HEADS // tensor
    blocks_dev = parents.shape[0]
    tree_blocks = TRUNK_BLKS + BRANCHES * (1 + LEAVES)
    group = tree_blocks // blocks_dev
    hops_back = group - 1
    me = lax.axis_index("tensor")
    dp_index = lax.axis_index("dp")
    logical_dev = (dp_index - group // 2) % count
    trees = timesteps.shape[0]
    width = tokens_in.shape[1]
    own_rows = tokens_in.shape[0]
    token_rows = own_rows * tensor
    block = token_rows // blocks_dev
    shard = norm_self.shape[0]
    cols = w_query.shape[1]
    hidden_cols = w_hidden.shape[1]
    (packed,) = run(
        lambda *refs: pack_body(trees, *refs),
        [shaped((count, shard + 8, 3 * cols), bf16)],
        [timesteps, time_table, norm_self[None], norm_cross[None], norm_ffn[None], w_query, w_key, w_value],
        load=True,
        limit=60,
    )
    cross_pack, ffn_pack = run(
        lambda *refs: side_body(5, *refs),
        [shaped((shard, 5 * cols), bf16), shaped((shard, 2 * hidden_cols), bf16)],
        [tie(c_query, packed), c_key, c_value, c_out.T, w_out.T, w_hidden, w_back.T],
        load=True,
        limit=60,
    )
    first = lax.all_to_all(packed, "dp", 0, 0)
    tokens_half = jnp.stack([tokens_in, across(tie(tokens_in, packed))])
    tokens_other = sibling(tokens_half)
    grad_half = jnp.stack([grad_out, across(tie(grad_out, packed))])
    grad_other = sibling(grad_half)
    cross_chain = Doubling(cross_pack)

    def turn(distance):
        return [
            ((l + group // 2) % count, (l - l % group + (l + distance) % group + group // 2) % count)
            for l in range(count)
        ]

    position = logical_dev % group
    lead_blocks = group // 2 * blocks_dev
    parent_log = (parents - lead_blocks) % (count * blocks_dev)
    parent_rel = parent_log - logical_dev // group * tree_blocks
    query_block = position * blocks_dev + jnp.arange(blocks_dev, dtype=i32)
    is_leaf = query_block >= TRUNK_BLKS + BRANCHES
    shift = (hops_back - position) * blocks_dev
    parent_at = jnp.where(is_leaf, parent_rel, query_block) + shift
    step_id = jnp.sum(jnp.where(jnp.arange(trees, dtype=i32) == tree_ids[0], timesteps, 0))
    scalars = jnp.concatenate(
        [
            (me ^ jnp.array([0, 2, 1, 3], i32)) * own_rows,
            jnp.stack([tree_ids[0], shift * block, position * blocks_dev, step_id]),
            parent_at * block,
            is_leaf.astype(i32),
        ]
    ).astype(i32)
    bits = count.bit_length() - 1
    near_masks = [sum(((k >> j) & 1) * (count >> (j + 1)) for j in range(bits - 1)) for k in range(count // 2)]
    half_masks = [sum(((k >> j) & 1) * (count >> (j + 1)) for j in range(bits - 1)) for k in range(count // 2)]
    masks = near_masks + [m | 1 for m in near_masks] + half_masks + [m | 1 for m in half_masks] + [0]
    slots = (dp_index ^ jnp.array(masks, i32)).astype(i32)

    def assemble(near, far):
        far = far if far is not None else neighbour(near)
        (full,) = run(
            lambda *refs: assemble_body(refs[0], 0, *refs[1:]),
            [shaped((count,) + near.shape[1:], bf16)],
            [slots, near, far],
            us=1,
        )
        return full.reshape(width, near.shape[2])

    half = (2, own_rows, width)
    act_self, q, kv, rows, qkv_w = run(
        project_body,
        [
            shaped((token_rows, width), bf16), shaped((token_rows, cols), bf16),
            shaped((token_rows, 2 * cols), bf16), shaped((4 + trees, width), f32),
            shaped((width, 3 * cols), bf16),
        ],
        [scalars, tokens_half, tokens_other, first],
    )
    cross_chain.step(kv)
    ffn_chain = Doubling(tie(ffn_pack, kv))
    cross_near = cross_chain.end()
    rest_w = assemble(cross_near, neighbour(cross_near))
    w_o = part(rest_w, cols, 4)

    def later(distance):
        return [
            ((l + group // 2) % count, (l + distance + group // 2) % count)
            for l in range(count)
            if l % group + distance < group
        ]

    parts = [lax.ppermute(kv, "dp", later(d)) for d in range(hops_back, 0, -1)] + [kv]
    buffer_rows = group * token_rows + max(0, TRUNK_BLKS - blocks_dev) * block
    ffn_chain.step(kv)
    ffn_near = ffn_chain.end()
    q = tie(q, grad_other)
    attn, lse, kept, sent = run(
        lambda *refs: self_body(block, heads, group, *refs),
        [shaped((token_rows, cols), bf16), shaped((8, token_rows), f32), shaped(half, f32), shaped(half, bf16)],
        [scalars, q, *parts, w_o],
        [pltpu.VMEM((buffer_rows, 2 * cols), bf16)],
        us=5,
    )
    enc_rows = enc_states.shape[0]
    enc_sent = tie(enc_states, attn)
    enc_parts = [enc_states] + [lax.ppermute(enc_sent, "dp", turn(d)) for d in range(1, group)]
    chip = chip_sum(kept, sent).astype(bf16)
    ffn_far = neighbour(tie(ffn_near, attn))
    resid_mid, act_own = run(
        lambda *refs: norm_body(True, 3, 1, *refs),
        [shaped(half, f32), shaped(half, bf16)],
        [tokens_half, chip, tie(across(chip), ffn_far, *enc_parts), rows],
        us=1,
    )
    act_other = sibling(act_own)
    ffn_w = assemble(ffn_near, ffn_far)
    up_w, down_w = part(ffn_w, hidden_cols, 0), part(ffn_w, hidden_cols, 1)
    cross_q, cross_kv, cross_low, cross_lse, kept, sent = run(
        lambda *refs: cross_body(heads, group, *refs),
        [
            shaped((token_rows, cols), bf16), shaped((group * enc_rows, 2 * cols), bf16),
            shaped((token_rows, cols), bf16), shaped((8, token_rows), f32), shaped(half, f32), shaped(half, bf16),
        ],
        [act_own, act_other, *enc_parts, rest_w],
    )
    chip = chip_sum(kept, sent).astype(bf16)
    resid_ffn, ffn_own = run(
        lambda *refs: norm_body(False, 3, 2, *refs),
        [shaped(half, f32), shaped(half, bf16)],
        [resid_mid, chip, tie(across(chip)), rows],
        us=1,
    )
    ffn_other = sibling(ffn_own)
    hidden, grad_pre, kept, sent = run(
        ffn_body,
        [
            shaped((token_rows, hidden_cols), bf16), shaped((token_rows, hidden_cols), bf16),
            shaped(half, f32), shaped(half, bf16),
        ],
        [ffn_own, ffn_other, grad_half, grad_other, up_w, down_w],
        us=3,
    )
    chip = chip_sum(kept, sent).astype(bf16)
    out_kept, out_sent = run(
        out_body, [shaped(half, f32), shaped(half, bf16)], [hidden, down_w]
    )
    grad_resid_ffn, top_own, dgain_ffn = run(
        lambda *refs: back_body(2, *refs),
        [shaped(half, f32), shaped(half, bf16), shaped((1, width), f32)],
        [grad_half, chip, tie(across(chip), out_sent), resid_ffn, rows],
        us=1,
    )
    top_other = sibling(top_own)
    grad_cq, kept, sent, *grad_encs = run(
        lambda *refs: cross_back_body(heads, *refs),
        [shaped((token_rows, cols), bf16), shaped(half, f32), shaped(half, bf16)]
        + [shaped((enc_rows, 2 * cols), bf16)] * group,
        [top_own, top_other, cross_q, cross_kv, cross_low, cross_lse, rest_w],
        us=3,
    )
    chip = chip_sum(kept, sent).astype(bf16)
    split = (count // 2, shard, 4 * cols + 2 * hidden_cols)
    rest_kept, rest_sent = run(
        lambda *refs: grads_body(group, *refs),
        [shaped(split, bf16), shaped(split, bf16)],
        [
            slots, tie(act_own, chip), act_other, top_own, top_other, grad_cq, cross_low, *enc_parts, *grad_encs,
            ffn_own, ffn_other, grad_half, grad_other, hidden, grad_pre,
        ],
        [pltpu.VMEM((count, shard, split[2]), bf16)],
        us=4,
    )
    rest_chain = Halving(rest_kept, rest_sent)
    out_chip = out_kept + sibling(tie(out_sent, chip)).astype(f32)
    grad_encs = [grad_encs[0]] + [
        lax.ppermute(tie(grad_encs[d], rest_sent), "dp", [(b, a) for a, b in turn(d)]) for d in range(1, group)
    ]
    grad_resid_mid, self_own, dgain_cross = run(
        lambda *refs: back_body(1, *refs),
        [shaped(half, f32), shaped(half, bf16), shaped((1, width), f32)],
        [grad_resid_ffn, chip, tie(across(chip), rest_sent, out_chip), resid_mid, rows],
        us=1,
    )
    (enc_part,) = run(
        lambda *refs: enc_body(group, *refs),
        [shaped((enc_rows, width), bf16)],
        [rest_w, grad_encs[0], *grad_encs[1:]],
        us=1,
    )
    enc_chip = (enc_part.astype(f32) + sibling(enc_part).astype(f32)).astype(bf16)
    enc_far = across(enc_chip)
    self_other = sibling(self_own)
    out_far = across(tie(out_chip[1].astype(bf16), self_own))
    kv_shape = (token_rows, 2 * cols)
    top, ds_trunk, ds_near, grad_own, *remote = run(
        lambda *refs: self_back_body(block, heads, group, *refs),
        [
            shaped((token_rows, width), bf16), shaped((heads, TRUNK_BLKS * block, token_rows), bf16),
            shaped((heads, 2, block, token_rows), bf16), shaped(kv_shape, f32),
        ]
        + [shaped(kv_shape, bf16)] * hops_back,
        [scalars, self_own, self_other, q, attn, lse, *parts, w_o],
        [pltpu.VMEM((buffer_rows, 2 * cols), bf16), pltpu.VMEM((buffer_rows, 2 * cols), f32)],
        us=8,
    )
    back = [
        lax.ppermute(one, "dp", [(b, a) for a, b in later(d)]) for one, d in zip(remote, range(hops_back, 0, -1))
    ]
    sum_q, sum_o, grad_act = run(
        lambda *refs: self_rest_body(block, heads, group, *refs),
        [shaped((width, cols), f32), shaped((width, cols), f32), shaped((token_rows, width), f32)],
        [scalars, act_self, top, attn, ds_trunk, ds_near, *parts, part(qkv_w, cols, 0)],
        [pltpu.VMEM((token_rows, cols), bf16), pltpu.VMEM((buffer_rows, 2 * cols), bf16)],
        us=4,
    )
    held = rest_chain.step(grad_act)
    grad_own = tie(grad_own, held)
    split = (count // 2, shard, 4 * cols)
    self_kept, self_sent, kept, sent = run(
        lambda *refs: self_end_body(group, *refs),
        [shaped(split, bf16), shaped(split, bf16), shaped(half, f32), shaped(half, bf16)],
        [
            scalars, slots, act_self, grad_own, *back, part(qkv_w, cols, 1), part(qkv_w, cols, 2), sum_q, sum_o, grad_act,
        ],
        [pltpu.VMEM(kv_shape, bf16), pltpu.VMEM((count, shard, 4 * cols), bf16)],
        us=3,
    )
    self_chain = Halving(self_kept, self_sent)
    chip = chip_sum(kept, sent)
    (vectors,) = run(
        lambda *refs: vector_body(tensor, trees, *refs),
        [shaped((count * tensor, -(-(3 + trees) // 8) * 8, shard), f32)],
        [scalars, tie(kept, chip), sent, tokens_half, tokens_other, grad_resid_mid, rows, dgain_cross, dgain_ffn],
    )
    received = lax.all_to_all(vectors, ("dp", "tensor"), 0, 0)
    (grad_in,) = run(
        last_body,
        [shaped((own_rows, width), f32)],
        [chip, across(chip[1].astype(bf16)), tokens_in, grad_resid_mid, rows],
        us=1,
    )
    self_chain.step()
    rest_chain.step(sent)
    output = (resid_ffn[0] + (out_chip[0] + out_far.astype(f32))).astype(bf16)
    grad_enc = enc_chip.astype(f32) + enc_far.astype(f32)
    self_sums, rest_sums = self_chain.end(), rest_chain.end()
    gains, grad_table = run(
        lambda *refs: small_body(trees, *refs),
        [shaped((8, shard), f32), shaped((time_table.shape[0], shard), f32)],
        [timesteps, received],
        us=1,
    )
    square = shaped((shard, cols), f32)
    gq, gk, gv, go = run(finish_pair_body, [square] * 4, [*self_sums], us=1)
    wide = shaped((shard, hidden_cols), f32)
    gcq, gck, gcv, gco, gup, gdown = run(finish_pair_body, [square] * 4 + [wide] * 2, [*rest_sums], us=1)
    return (
        output, grad_in, grad_enc, grad_table, gains[0], gq, gk, gv, go.T, gains[1],
        gcq, gck, gcv, gco.T, gains[2], gup, gdown.T,
    )


def solution(mesh):
    rows, cols, repl = P(("dp", "tensor"), None), P("dp", "tensor"), P("tensor", "dp")
    in_specs = (
        rows, rows, P("dp", None), P("dp"), P("dp"), P(), P(None, "dp"), P("dp"), cols, cols, cols, repl,
        P("dp"), cols, cols, cols, repl, P("dp"), cols, repl,
    )
    out_specs = (
        rows, rows, P("dp", None), P(None, "dp"), P("dp"), cols, cols, cols, repl, P("dp"), cols, cols, cols,
        repl, P("dp"), cols, repl,
    )
    return jax.shard_map(on_device, mesh=mesh, in_specs=in_specs, out_specs=out_specs, check_vma=False)
```

```python
import jax
import jax.numpy as jnp
from jax import lax
from jax.experimental import pallas as pl
from jax.experimental.pallas import tpu as pltpu
from jax.sharding import PartitionSpec as P

HEADS = 8
TRUNK_BLKS = 8
BRANCHES = 4
LEAVES = 2
eps = 1e-05
bf16 = jnp.bfloat16
f32 = jnp.float32
i32 = jnp.int32
NEG = -1e30


def mm(a, b):
    return lax.dot_general(a, b, (((1,), (0,)), ((), ())), preferred_element_type=f32)


def mm_tn(a, b):
    return lax.dot_general(a, b, (((0,), (0,)), ((), ())), preferred_element_type=f32)


def mm_nt(a, b):
    return lax.dot_general(a, b, (((1,), (1,)), ((), ())), preferred_element_type=f32)


def normalize(v):
    centered = v - jnp.mean(v, axis=-1, keepdims=True)
    inv = lax.rsqrt(jnp.mean(centered * centered, axis=-1, keepdims=True) + eps)
    return centered * inv, inv


def norm_back(grad_act, resid, gain):
    normed, inv = normalize(resid)
    scaled = grad_act * gain
    mean_g = jnp.mean(scaled, axis=-1, keepdims=True)
    mean_gx = jnp.mean(scaled * normed, axis=-1, keepdims=True)
    return inv * (scaled - mean_g - normed * mean_gx), jnp.sum(grad_act * normed, axis=0, keepdims=True)


def shaped(shape, dtype):
    return jax.ShapeDtypeStruct(shape, dtype)


class Cols:
    def __init__(self, ref, start, width):
        self.ref, self.cols, self.dtype = ref, slice(start, start + width), ref.dtype
        self.shape = (ref.shape[0], width)

    def __getitem__(self, key):
        return self.ref[:, self.cols]


def part(array, width, index):
    return (array, width * index, width)


def loading(body, n_scalars, n_loads, n_ins):
    def wrapped(*refs):
        sources = refs[n_scalars : n_scalars + n_loads]
        held = refs[len(refs) - n_loads - 1 : len(refs) - 1]
        sems = refs[-1]
        copies = [pltpu.make_async_copy(src, dst, sems.at[i]) for i, (src, dst) in enumerate(zip(sources, held))]
        for one in copies:
            one.start()
        for one in copies:
            one.wait()
        body(*refs[:n_scalars], *held, *refs[n_ins : len(refs) - n_loads - 1])

    return wrapped


def run(body, outs, ins, scratch=(), us=2, load=False, limit=24):
    arrays = [item[0] if isinstance(item, tuple) else item for item in ins]
    spaces = [pltpu.SMEM if array.dtype == i32 else (pltpu.HBM if load else pltpu.VMEM) for array in arrays]
    scratch = list(scratch)

    def wrapped(*refs):
        seen = [Cols(ref, item[1], item[2]) if isinstance(item, tuple) else ref for ref, item in zip(refs, ins)]
        body(*seen, *refs[len(ins) :])

    if load:
        loads = [array for array in arrays if array.dtype != i32]
        wrapped = loading(body, len(arrays) - len(loads), len(loads), len(arrays))
        scratch += [pltpu.VMEM(array.shape, array.dtype) for array in loads]
        scratch.append(pltpu.SemaphoreType.DMA((len(loads),)))
    return pl.pallas_call(
        wrapped,
        out_shape=outs,
        in_specs=[pl.BlockSpec(memory_space=space) for space in spaces],
        out_specs=[pl.BlockSpec(memory_space=pltpu.VMEM) for _ in outs],
        scratch_shapes=scratch,
        cost_estimate=pl.CostEstimate(flops=us * 100 * 10**6, bytes_accessed=10**6, transcendentals=0),
        compiler_params=pltpu.CompilerParams(vmem_limit_bytes=limit * 1024 * 1024),
    )(*arrays)


def side_body(n_first, *refs):
    ins, outs = refs[:-2], refs[-2:]
    for group, one in ((ins[:n_first], outs[0]), (ins[n_first:], outs[1])):
        at = 0
        for piece in group:
            one[:, at : at + piece.shape[1]] = piece[...]
            at += piece.shape[1]


def pack_body(trees, steps, table, n_self, n_cross, n_ffn, *refs):
    weights, out = refs[:-1], refs[-1]
    lines = lax.broadcasted_iota(i32, table.shape, 0)
    full = table[...].astype(f32)
    small = [n_self[...].astype(f32), n_cross[...].astype(f32), n_ffn[...].astype(f32)]
    for i in range(trees):
        small.append(jnp.sum(jnp.where(lines == steps[i], full, 0.0), axis=0, keepdims=True))
    shard = table.shape[1]
    small.append(jnp.zeros((1, out.shape[2] - len(small) * shard), f32))
    tail = jnp.broadcast_to(jnp.concatenate(small, axis=1), (8, out.shape[2])).astype(bf16)
    for d in range(out.shape[0]):
        at = 0
        for one in weights:
            out[d, :shard, at : at + one.shape[1]] = one[...]
            at += one.shape[1]
        out[d, shard:, :] = tail


def assemble_body(slots, base, near, far, out):
    for i, ref in enumerate((near, far)):
        for k in range(ref.shape[0]):
            out[slots[base + i * ref.shape[0] + k]] = ref[k]


def project_body(sc, half, other, first, act, q, kv, rows, w):
    shard = first.shape[1] - 8
    count = first.shape[0]
    for d in range(count):
        w[d * shard : (d + 1) * shard, :] = first[d, :shard, :]
    tails = [first[d, shard:, :].astype(f32)[0:1] for d in range(count)]

    def line(k):
        return jnp.concatenate([one[:, k * shard : (k + 1) * shard] for one in tails], axis=1)

    trees = (first.shape[2] // shard) - 3
    time_row = jnp.zeros((1, count * shard), f32)
    for i in range(min(trees, rows.shape[0] - 4)):
        time_row = time_row + jnp.where(sc[4] == i, line(3 + i), 0.0)
    gain = line(0)
    rows[0:1, :] = gain
    rows[1:2, :] = line(1)
    rows[2:3, :] = line(2)
    rows[3:4, :] = time_row
    own_rows = half.shape[1]
    for k in range(4):
        src = half[k] if k < 2 else other[k - 2]
        normed, _ = normalize(src.astype(f32) + time_row)
        act[pl.ds(pl.multiple_of(sc[k], 16), own_rows), :] = (normed * gain).astype(bf16)
    cols = q.shape[1]
    result = mm(act[...], w[...]).astype(bf16)
    q[...] = result[:, :cols]
    kv[...] = result[:, cols:]


def fill_kv(buffer, parts):
    rows = parts[0].shape[0]
    for index, one in enumerate(parts):
        buffer[index * rows : (index + 1) * rows, :] = one[...]
    done = len(parts) * rows
    if buffer.shape[0] > done:
        buffer[done:, :] = jnp.zeros((buffer.shape[0] - done, buffer.shape[1]), buffer.dtype)


def self_scores(sc, buffer, own, qh, h, hd, block):
    count = qh.shape[0] // block
    col = h * hd
    start = pl.multiple_of(sc[5], block)
    trunk_rows = TRUNK_BLKS * block
    keys = buffer[pl.ds(start, trunk_rows), col : col + hd]
    trunk = mm_nt(keys, qh)
    query_block = lax.broadcasted_iota(i32, (1, qh.shape[0]), 1) // block + sc[6]
    pieces = []
    for j in range(TRUNK_BLKS):
        bias = jnp.where(query_block > j, 0.0, NEG)
        pieces.append(trunk[j * block : (j + 1) * block] + bias)
    key_pos = lax.broadcasted_iota(i32, (block, block), 0)
    query_pos = lax.broadcasted_iota(i32, (block, block), 1)
    own_s, par_s = [], []
    for i in range(count):
        q_i = qh[i * block : (i + 1) * block]
        o = mm_nt(own[i * block : (i + 1) * block, col : col + hd], q_i)
        own_s.append(jnp.where(key_pos <= query_pos, o, NEG))
        par = buffer[pl.ds(pl.multiple_of(sc[8 + i], block), block), col : col + hd]
        leaf = (lax.broadcasted_iota(i32, (1, block), 1) * 0 + sc[8 + count + i]) > 0
        par_s.append(mm_nt(par, q_i) + jnp.where(leaf, 0.0, NEG))
    pieces.append(jnp.concatenate(own_s, axis=1))
    pieces.append(jnp.concatenate(par_s, axis=1))
    return pieces, keys


def out_partial(sc, source, w, kept, sent):
    own_rows = kept.shape[1]
    for k in range(4):
        p = mm_nt(source[pl.ds(pl.multiple_of(sc[k], 16), own_rows), :], w[...])
        if k < 2:
            kept[k] = p
        else:
            sent[k - 2] = p.astype(bf16)


def self_body(block, heads, n_parts, sc, q, *refs):
    parts = refs[:n_parts]
    w = refs[n_parts]
    attn, lse, kept, sent, buffer = refs[n_parts + 1 :]
    own = parts[-1]
    fill_kv(buffer, parts)
    cols = q.shape[1]
    hd = cols // heads
    count = q.shape[0] // block
    trunk_rows = TRUNK_BLKS * block
    start = pl.multiple_of(sc[5], block)
    for h in range(heads):
        col = h * hd
        qh = q[:, col : col + hd] * jnp.asarray(hd**-0.5, bf16)
        pieces, _ = self_scores(sc, buffer, own, qh, h, hd, block)
        peak = pieces[0]
        for s in pieces[1:]:
            peak = jnp.maximum(peak, s)
        peak = jnp.max(peak, axis=0, keepdims=True)
        exps = [jnp.exp(s - peak) for s in pieces]
        total = exps[0]
        for e in exps[1:]:
            total = total + e
        total = jnp.sum(total, axis=0, keepdims=True)
        inv = 1.0 / total
        lse[h : h + 1, :] = peak + jnp.log(total)
        low = [(e * inv).astype(bf16) for e in exps]
        vals = buffer[pl.ds(start, trunk_rows), cols + col : cols + col + hd]
        mixed = mm_tn(jnp.concatenate(low[:TRUNK_BLKS], axis=0), vals)
        for i in range(count):
            rows = slice(i * block, (i + 1) * block)
            par = buffer[pl.ds(pl.multiple_of(sc[8 + i], block), block), cols + col : cols + col + hd]
            both = jnp.concatenate([low[TRUNK_BLKS][:, rows], low[TRUNK_BLKS + 1][:, rows]], axis=0)
            two = jnp.concatenate([own[rows, cols + col : cols + col + hd], par], axis=0)
            attn[rows, col : col + hd] = (mixed[rows] + mm_tn(both, two)).astype(bf16)
    out_partial(sc, attn, w, kept, sent)


def norm_body(first, time_at, gain_at, resid, chip, far, rows, resid_out, act):
    for k in range(2):
        base = resid[k].astype(f32)
        if first:
            base = base + rows[time_at : time_at + 1, :]
        v = base + (chip[k].astype(f32) + far[1 - k].astype(f32))
        resid_out[k] = v
        normed, _ = normalize(v)
        act[k] = (normed * rows[gain_at : gain_at + 1, :]).astype(bf16)


def both_halves(own, other):
    r, d = own.shape[1], own.shape[2]
    return jnp.concatenate([own[...].reshape(2 * r, d), other[...].reshape(2 * r, d)], axis=0)


def split_store(p, kept, sent):
    r = kept.shape[1]
    for k in range(2):
        kept[k] = p[k * r : (k + 1) * r]
        sent[k] = p[(2 + k) * r : (3 + k) * r].astype(bf16)


def cross_body(heads, n_enc, own, other, *refs):
    encs = refs[:n_enc]
    w, q, kv, low_out, lse, kept, sent = refs[n_enc:]
    act = both_halves(own, other)
    cols = q.shape[1]
    hd = cols // heads
    queries = mm(act, w[:, :cols]).astype(bf16)
    q[...] = queries
    pairs = mm(jnp.concatenate([enc[...] for enc in encs], axis=0), w[:, cols : 3 * cols]).astype(bf16)
    kv[...] = pairs
    for h in range(heads):
        sl = slice(h * hd, (h + 1) * hd)
        s = mm_nt(pairs[:, sl], queries[:, sl] * jnp.asarray(hd**-0.5, bf16))
        peak = jnp.max(s, axis=0, keepdims=True)
        e = jnp.exp(s - peak)
        total = jnp.sum(e, axis=0, keepdims=True)
        lse[h : h + 1, :] = peak + jnp.log(total)
        vals = pairs[:, cols + h * hd : cols + (h + 1) * hd]
        low_out[:, sl] = mm_tn((e * (1.0 / total)).astype(bf16), vals).astype(bf16)
    split_store(mm_nt(low_out[...], w[:, 3 * cols : 4 * cols]), kept, sent)


def ffn_body(own, other, g_own, g_other, up, down_t, hidden, grad_pre, kept, sent):
    r = own.shape[1]
    for k in range(4):
        act = own[k] if k < 2 else other[k - 2]
        top = g_own[k] if k < 2 else g_other[k - 2]
        pre = mm(act, up[...])
        cdf = 0.5 * (1.0 + lax.erf(pre * 0.7071067811865476))
        hidden[k * r : (k + 1) * r, :] = (pre * cdf).astype(bf16)
        slope = cdf + pre * (jnp.exp(-0.5 * pre * pre) * 0.3989422804014327)
        gp = (mm(top, down_t[...]) * slope).astype(bf16)
        grad_pre[k * r : (k + 1) * r, :] = gp
        p = mm_nt(gp, up[...])
        if k < 2:
            kept[k] = p
        else:
            sent[k - 2] = p.astype(bf16)


def relative(slots, base, scratch, value, kept, sent):
    scratch[...] = value.reshape(scratch.shape).astype(bf16)
    for i, ref in enumerate((kept, sent)):
        for k in range(ref.shape[0]):
            ref[k] = scratch[slots[base + i * ref.shape[0] + k]]


def grads_body(n_enc, slots, *refs):
    own, other, top_own, top_other, grad_q, low_in = refs[:6]
    encs, grad_encs = refs[6 : 6 + n_enc], refs[6 + n_enc : 6 + 2 * n_enc]
    ffn_own, ffn_other, g_own, g_other, hidden, grad_pre, near, far, scratch = refs[6 + 2 * n_enc :]
    sums = [
        mm_tn(both_halves(own, other), grad_q[...]),
        mm_tn(
            jnp.concatenate([one[...] for one in encs], axis=0), jnp.concatenate([one[...] for one in grad_encs], axis=0)
        ),
        mm_tn(both_halves(top_own, top_other), low_in[...]),
        mm_tn(both_halves(ffn_own, ffn_other), grad_pre[...]),
        mm_tn(both_halves(g_own, g_other), hidden[...]),
    ]
    relative(slots, 2 * near.shape[0], scratch, jnp.concatenate(sums, axis=1), near, far)


def out_body(hidden, down_t, kept, sent):
    split_store(mm_nt(hidden[...], down_t[...]), kept, sent)


def back_body(gain_at, base, chip, far, resid, rows, grad, low, dgain):
    for k in range(2):
        g = chip[k].astype(f32) + far[1 - k].astype(f32)
        back, sums = norm_back(g, resid[k], rows[gain_at : gain_at + 1, :])
        v = base[k].astype(f32) + back
        grad[k] = v
        low[k] = v.astype(bf16)
        if k == 0:
            dgain[...] = sums


def inner_rows(grad, out):
    return (grad.astype(f32) * out.astype(f32)).T


def cross_back_body(heads, g_own, g_other, q, kv, low_in, lse, w, grad_q, kept, sent, *grad_encs):
    top = both_halves(g_own, g_other)
    cols = q.shape[1]
    hd = cols // heads
    grad_mixed = mm(top, w[:, 3 * cols : 4 * cols]).astype(bf16)
    inner = inner_rows(grad_mixed, low_in[...])
    enc_rows = grad_encs[0].shape[0]
    for h in range(heads):
        sl = slice(h * hd, (h + 1) * hd)
        vl = slice(cols + h * hd, cols + (h + 1) * hd)
        qh = q[:, sl] * jnp.asarray(hd**-0.5, bf16)
        gh = grad_mixed[:, sl]
        probs = jnp.exp(mm_nt(kv[:, sl], qh) - lse[h : h + 1, :])
        grad_v = mm(probs.astype(bf16), gh).astype(bf16)
        delta = jnp.sum(inner[sl], axis=0, keepdims=True)
        ds = (probs * (mm_nt(kv[:, vl], gh) - delta)).astype(bf16)
        grad_k = mm(ds, qh).astype(bf16)
        for i, one in enumerate(grad_encs):
            one[:, sl] = grad_k[i * enc_rows : (i + 1) * enc_rows]
            one[:, vl] = grad_v[i * enc_rows : (i + 1) * enc_rows]
        grad_q[:, sl] = (mm_tn(ds, kv[:, sl]) * hd**-0.5).astype(bf16)
    split_store(mm_nt(grad_q[...], w[:, :cols]), kept, sent)


def enc_body(n_enc, w, *refs):
    parts, out = refs[:n_enc], refs[n_enc]
    total = parts[0][...].astype(f32)
    for one in parts[1:]:
        total = total + one[...].astype(f32)
    cols = total.shape[1] // 2
    out[...] = mm_nt(total.astype(bf16), w[:, cols : 3 * cols]).astype(bf16)


def self_back_body(block, heads, n_parts, sc, g_own, g_other, q, attn, lse, *refs):
    parts = refs[:n_parts]
    w = refs[n_parts]
    outs = refs[n_parts + 1 :]
    top, ds_trunk, ds_near, grad_own = outs[:4]
    remote = outs[4 : 4 + n_parts - 1]
    buffer, sums = outs[4 + n_parts - 1 :]
    own = parts[-1]
    fill_kv(buffer, parts)
    sums[...] = jnp.zeros(sums.shape, f32)
    own_rows = g_own.shape[1]
    for k in range(4):
        src = g_own[k] if k < 2 else g_other[k - 2]
        top[pl.ds(pl.multiple_of(sc[k], 16), own_rows), :] = src
    cols = q.shape[1]
    hd = cols // heads
    count = q.shape[0] // block
    trunk_rows = TRUNK_BLKS * block
    start = pl.multiple_of(sc[5], block)
    grad_attn = mm(top[...], w[...]).astype(bf16)
    inner = inner_rows(grad_attn, attn[...])
    rows_all = own.shape[0]
    base = (n_parts - 1) * rows_all
    for h in range(heads):
        col = h * hd
        sl, vl = slice(col, col + hd), slice(cols + col, cols + col + hd)
        qh = q[:, sl] * jnp.asarray(hd**-0.5, bf16)
        gh = grad_attn[:, sl]
        pieces, keys = self_scores(sc, buffer, own, qh, h, hd, block)
        delta = jnp.sum(inner[sl], axis=0, keepdims=True)
        level = lse[h : h + 1, :]
        vals = buffer[pl.ds(start, trunk_rows), vl]
        probs = jnp.exp(jnp.concatenate(pieces[:TRUNK_BLKS], axis=0) - level)
        ds = (probs * (mm_nt(vals, gh) - delta)).astype(bf16)
        ds_trunk[h] = ds
        sums[pl.ds(start, trunk_rows), sl] += mm(ds, qh)
        sums[pl.ds(start, trunk_rows), vl] += mm(probs.astype(bf16), gh)
        for i in range(count):
            rows = slice(i * block, (i + 1) * block)
            par_at = pl.ds(pl.multiple_of(sc[8 + i], block), block)
            own_at = slice(base + i * block, base + (i + 1) * block)
            q_i, g_i = qh[rows], gh[rows]
            near = ((pieces[TRUNK_BLKS], own_at), (pieces[TRUNK_BLKS + 1], par_at))
            for j, (piece, at) in enumerate(near):
                p = jnp.exp(piece[:, rows] - level[:, rows])
                d = (p * (mm_nt(buffer[at, vl], g_i) - delta[:, rows])).astype(bf16)
                ds_near[h, j, :, rows] = d
                sums[at, sl] += mm(d, q_i)
                sums[at, vl] += mm(p.astype(bf16), g_i)
    for index, one in enumerate(remote):
        one[...] = sums[index * rows_all : (index + 1) * rows_all, :].astype(bf16)
    grad_own[...] = sums[base : base + rows_all, :]


def self_rest_body(block, heads, n_parts, sc, act, top, attn, ds_trunk, ds_near, *refs):
    parts = refs[:n_parts]
    wq, sum_q, sum_o, grad_act, grad_q, buffer = refs[n_parts:]
    fill_kv(buffer, parts)
    own = parts[-1]
    cols = grad_q.shape[1]
    hd = cols // heads
    trunk_rows = TRUNK_BLKS * block
    start = pl.multiple_of(sc[5], block)
    for h in range(heads):
        sl = slice(h * hd, (h + 1) * hd)
        trunk = mm_tn(ds_trunk[h], buffer[pl.ds(start, trunk_rows), sl])
        for i in range(grad_q.shape[0] // block):
            rows = slice(i * block, (i + 1) * block)
            par = buffer[pl.ds(pl.multiple_of(sc[8 + i], block), block), sl]
            both = jnp.concatenate([ds_near[h, 0, :, rows], ds_near[h, 1, :, rows]], axis=0)
            near = mm_tn(both, jnp.concatenate([own[rows, sl], par], axis=0))
            grad_q[rows, sl] = ((trunk[rows] + near) * hd**-0.5).astype(bf16)
    sum_q[...] = mm_tn(act[...], grad_q[...])
    sum_o[...] = mm_tn(top[...], attn[...])
    grad_act[...] = mm_nt(grad_q[...], wq[...])


def self_end_body(n_parts, sc, slots, act, grad_own, *refs):
    remote = refs[: n_parts - 1]
    wk, wv, sum_q, sum_o, grad_act, near, far, kept, sent, total, scratch = refs[n_parts - 1 :]
    t = grad_own[...]
    for one in remote:
        t = t + one[...].astype(f32)
    total[...] = t.astype(bf16)
    cols = sum_q.shape[1]
    own_rows = kept.shape[1]
    for k in range(4):
        at = pl.ds(pl.multiple_of(sc[k], 16), own_rows)
        p = grad_act[at, :] + mm_nt(total[at, :cols], wk[...]) + mm_nt(total[at, cols:], wv[...])
        if k < 2:
            kept[k] = p
        else:
            sent[k - 2] = p.astype(bf16)
    weights = jnp.concatenate([sum_q[...], mm_tn(act[...], total[...]), sum_o[...]], axis=1)
    relative(slots, 2 * near.shape[0], scratch, weights, near, far)


def vector_body(tensor, trees, sc, kept, sent, half, other, grad_mid, rows, dgain_cross, dgain_ffn, out):
    gain = rows[0:1, :]
    dgain = jnp.zeros(gain.shape, f32)
    column = jnp.sum(grad_mid[0], axis=0, keepdims=True)
    for k in range(4):
        g = kept[k] if k < 2 else sent[k - 2].astype(f32)
        src = half[k] if k < 2 else other[k - 2]
        back, one = norm_back(g, src.astype(f32) + rows[3:4, :], gain)
        dgain = dgain + one
        column = column + jnp.sum(back, axis=0, keepdims=True)
    lines = lax.broadcasted_iota(i32, (out.shape[1], gain.shape[1]), 0)
    block = jnp.where(lines == 3 + sc[4], column, 0.0)
    for i, one in enumerate((dgain, dgain_cross[...], dgain_ffn[...])):
        block = jnp.where(lines == i, one, block)
    shard = out.shape[2]
    for d in range(out.shape[0] // tensor):
        for t in range(tensor):
            out[d * tensor + t] = block[:, d * shard : (d + 1) * shard]


def last_body(chip, far, tokens, grad_mid, rows, grad_in):
    g = chip[0] + far[...].astype(f32)
    back, _ = norm_back(g, tokens[...].astype(f32) + rows[3:4, :], rows[0:1, :])
    grad_in[...] = grad_mid[0] + back


def small_body(trees, steps, received, gains, table):
    total = received[0]
    for k in range(1, received.shape[0]):
        total = total + received[k]
    gains[...] = total[:8]
    lines = lax.broadcasted_iota(i32, table.shape, 0)
    sums = jnp.zeros(table.shape, f32)
    for i in range(trees):
        sums = sums + jnp.where(lines == steps[i], total[3 + i : 4 + i], 0.0)
    table[...] = sums


def finish_pair_body(near, far, *outs):
    total = near[0].astype(f32) + far[0].astype(f32)
    at = 0
    for one in outs:
        one[...] = total[:, at : at + one.shape[1]]
        at += one.shape[1]


def xor_route(axis, bit):
    return [(i, i ^ bit) for i in range(lax.axis_size(axis))]


def sibling(x):
    return lax.ppermute(x, "tensor", xor_route("tensor", 1))


def across(x):
    return lax.ppermute(x, "tensor", xor_route("tensor", 2))


def chip_sum(kept, sent):
    return kept + sibling(sent).astype(f32)


def tie(x, *others):
    return lax.optimization_barrier((x, *others))[0]


class Doubling:
    def __init__(self, x):
        self.held = x[None]
        self.bit = lax.axis_size("dp") // 2
        self.received = None
        self.send()

    def send(self):
        if self.bit > 1:
            self.received = lax.ppermute(self.held, "dp", xor_route("dp", self.bit))

    def step(self, *dues):
        if self.bit > 1:
            self.held = jnp.concatenate([self.held, tie(self.received, *dues)], axis=0)
            self.bit //= 2
            self.send()
        return self.held

    def end(self, *dues):
        while self.bit > 1:
            self.step(*dues)
        return self.held


def neighbour(x):
    return lax.ppermute(x, "dp", xor_route("dp", 1))


class Halving:
    def __init__(self, near, far):
        self.bit = 2
        self.near, self.received = near, neighbour(far)

    def step(self, *dues):
        self.received = tie(self.received, *dues)
        if self.bit >= lax.axis_size("dp"):
            return self.received
        total = (self.near.astype(f32) + self.received.astype(f32)).astype(bf16)
        middle = total.shape[0] // 2
        self.near = total[:middle]
        self.received = lax.ppermute(total[middle:], "dp", xor_route("dp", self.bit))
        self.bit *= 2
        return self.near

    def end(self, *dues):
        while self.bit < lax.axis_size("dp"):
            self.step(*dues)
        return self.near, tie(self.received, *dues)


def on_device(
    tokens_in, grad_out, enc_states, parents, tree_ids, timesteps, time_table, norm_self,
    w_query, w_key, w_value, w_out, norm_cross, c_query, c_key, c_value, c_out, norm_ffn,
    w_hidden, w_back,
):
    count = lax.axis_size("dp")
    tensor = lax.axis_size("tensor")
    heads = HEADS // tensor
    blocks_dev = parents.shape[0]
    tree_blocks = TRUNK_BLKS + BRANCHES * (1 + LEAVES)
    group = tree_blocks // blocks_dev
    hops_back = group - 1
    me = lax.axis_index("tensor")
    dp_index = lax.axis_index("dp")
    logical_dev = (dp_index - group // 2) % count
    trees = timesteps.shape[0]
    width = tokens_in.shape[1]
    own_rows = tokens_in.shape[0]
    token_rows = own_rows * tensor
    block = token_rows // blocks_dev
    shard = norm_self.shape[0]
    cols = w_query.shape[1]
    hidden_cols = w_hidden.shape[1]
    (packed,) = run(
        lambda *refs: pack_body(trees, *refs),
        [shaped((count, shard + 8, 3 * cols), bf16)],
        [timesteps, time_table, norm_self[None], norm_cross[None], norm_ffn[None], w_query, w_key, w_value],
        load=True,
        limit=60,
    )
    cross_pack, ffn_pack = run(
        lambda *refs: side_body(5, *refs),
        [shaped((shard, 5 * cols), bf16), shaped((shard, 2 * hidden_cols), bf16)],
        [tie(c_query, packed), c_key, c_value, c_out.T, w_out.T, w_hidden, w_back.T],
        load=True,
        limit=60,
    )
    first = lax.all_to_all(packed, "dp", 0, 0)
    tokens_half = jnp.stack([tokens_in, across(tie(tokens_in, packed))])
    tokens_other = sibling(tokens_half)
    grad_half = jnp.stack([grad_out, across(tie(grad_out, packed))])
    grad_other = sibling(grad_half)
    cross_chain = Doubling(cross_pack)

    def turn(distance):
        return [
            ((l + group // 2) % count, (l - l % group + (l + distance) % group + group // 2) % count)
            for l in range(count)
        ]

    position = logical_dev % group
    lead_blocks = group // 2 * blocks_dev
    parent_log = (parents - lead_blocks) % (count * blocks_dev)
    parent_rel = parent_log - logical_dev // group * tree_blocks
    query_block = position * blocks_dev + jnp.arange(blocks_dev, dtype=i32)
    is_leaf = query_block >= TRUNK_BLKS + BRANCHES
    shift = (hops_back - position) * blocks_dev
    parent_at = jnp.where(is_leaf, parent_rel, query_block) + shift
    step_id = jnp.sum(jnp.where(jnp.arange(trees, dtype=i32) == tree_ids[0], timesteps, 0))
    scalars = jnp.concatenate(
        [
            (me ^ jnp.array([0, 2, 1, 3], i32)) * own_rows,
            jnp.stack([tree_ids[0], shift * block, position * blocks_dev, step_id]),
            parent_at * block,
            is_leaf.astype(i32),
        ]
    ).astype(i32)
    bits = count.bit_length() - 1
    near_masks = [sum(((k >> j) & 1) * (count >> (j + 1)) for j in range(bits - 1)) for k in range(count // 2)]
    half_masks = [sum(((k >> j) & 1) * (count >> (j + 1)) for j in range(bits - 1)) for k in range(count // 2)]
    masks = near_masks + [m | 1 for m in near_masks] + half_masks + [m | 1 for m in half_masks] + [0]
    slots = (dp_index ^ jnp.array(masks, i32)).astype(i32)

    def assemble(near, far):
        far = far if far is not None else neighbour(near)
        (full,) = run(
            lambda *refs: assemble_body(refs[0], 0, *refs[1:]),
            [shaped((count,) + near.shape[1:], bf16)],
            [slots, near, far],
            us=1,
        )
        return full.reshape(width, near.shape[2])

    half = (2, own_rows, width)
    act_self, q, kv, rows, qkv_w = run(
        project_body,
        [
            shaped((token_rows, width), bf16), shaped((token_rows, cols), bf16),
            shaped((token_rows, 2 * cols), bf16), shaped((4 + trees, width), f32),
            shaped((width, 3 * cols), bf16),
        ],
        [scalars, tokens_half, tokens_other, first],
    )
    cross_chain.step(kv)
    ffn_chain = Doubling(tie(ffn_pack, kv))
    cross_near = cross_chain.end()
    rest_w = assemble(cross_near, neighbour(cross_near))
    w_o = part(rest_w, cols, 4)

    def later(distance):
        return [
            ((l + group // 2) % count, (l + distance + group // 2) % count)
            for l in range(count)
            if l % group + distance < group
        ]

    parts = [lax.ppermute(kv, "dp", later(d)) for d in range(hops_back, 0, -1)] + [kv]
    buffer_rows = group * token_rows + max(0, TRUNK_BLKS - blocks_dev) * block
    ffn_chain.step(kv)
    ffn_near = ffn_chain.end()
    q = tie(q, grad_other)
    attn, lse, kept, sent = run(
        lambda *refs: self_body(block, heads, group, *refs),
        [shaped((token_rows, cols), bf16), shaped((8, token_rows), f32), shaped(half, f32), shaped(half, bf16)],
        [scalars, q, *parts, w_o],
        [pltpu.VMEM((buffer_rows, 2 * cols), bf16)],
        us=5,
    )
    enc_rows = enc_states.shape[0]
    enc_sent = tie(enc_states, attn)
    enc_parts = [enc_states] + [lax.ppermute(enc_sent, "dp", turn(d)) for d in range(1, group)]
    chip = chip_sum(kept, sent).astype(bf16)
    ffn_far = neighbour(tie(ffn_near, rest_w))
    resid_mid, act_own = run(
        lambda *refs: norm_body(True, 3, 1, *refs),
        [shaped(half, f32), shaped(half, bf16)],
        [tokens_half, chip, tie(across(chip), ffn_far, *enc_parts), rows],
        us=1,
    )
    act_other = sibling(act_own)
    ffn_w = assemble(ffn_near, ffn_far)
    up_w, down_w = part(ffn_w, hidden_cols, 0), part(ffn_w, hidden_cols, 1)
    cross_q, cross_kv, cross_low, cross_lse, kept, sent = run(
        lambda *refs: cross_body(heads, group, *refs),
        [
            shaped((token_rows, cols), bf16), shaped((group * enc_rows, 2 * cols), bf16),
            shaped((token_rows, cols), bf16), shaped((8, token_rows), f32), shaped(half, f32), shaped(half, bf16),
        ],
        [act_own, act_other, *enc_parts, rest_w],
    )
    chip = chip_sum(kept, sent).astype(bf16)
    resid_ffn, ffn_own = run(
        lambda *refs: norm_body(False, 3, 2, *refs),
        [shaped(half, f32), shaped(half, bf16)],
        [resid_mid, chip, tie(across(chip)), rows],
        us=1,
    )
    ffn_other = sibling(ffn_own)
    hidden, grad_pre, kept, sent = run(
        ffn_body,
        [
            shaped((token_rows, hidden_cols), bf16), shaped((token_rows, hidden_cols), bf16),
            shaped(half, f32), shaped(half, bf16),
        ],
        [ffn_own, ffn_other, grad_half, grad_other, up_w, down_w],
        us=3,
    )
    chip = chip_sum(kept, sent).astype(bf16)
    out_kept, out_sent = run(
        out_body, [shaped(half, f32), shaped(half, bf16)], [hidden, down_w]
    )
    grad_resid_ffn, top_own, dgain_ffn = run(
        lambda *refs: back_body(2, *refs),
        [shaped(half, f32), shaped(half, bf16), shaped((1, width), f32)],
        [grad_half, chip, tie(across(chip), out_sent), resid_ffn, rows],
        us=1,
    )
    top_other = sibling(top_own)
    grad_cq, kept, sent, *grad_encs = run(
        lambda *refs: cross_back_body(heads, *refs),
        [shaped((token_rows, cols), bf16), shaped(half, f32), shaped(half, bf16)]
        + [shaped((enc_rows, 2 * cols), bf16)] * group,
        [top_own, top_other, cross_q, cross_kv, cross_low, cross_lse, rest_w],
        us=3,
    )
    chip = chip_sum(kept, sent).astype(bf16)
    split = (count // 2, shard, 4 * cols + 2 * hidden_cols)
    rest_kept, rest_sent = run(
        lambda *refs: grads_body(group, *refs),
        [shaped(split, bf16), shaped(split, bf16)],
        [
            slots, tie(act_own, chip), act_other, top_own, top_other, grad_cq, cross_low, *enc_parts, *grad_encs,
            ffn_own, ffn_other, grad_half, grad_other, hidden, grad_pre,
        ],
        [pltpu.VMEM((count, shard, split[2]), bf16)],
        us=4,
    )
    rest_chain = Halving(rest_kept, rest_sent)
    out_chip = out_kept + sibling(tie(out_sent, chip)).astype(f32)
    grad_encs = [grad_encs[0]] + [
        lax.ppermute(tie(grad_encs[d], rest_sent), "dp", [(b, a) for a, b in turn(d)]) for d in range(1, group)
    ]
    grad_resid_mid, self_own, dgain_cross = run(
        lambda *refs: back_body(1, *refs),
        [shaped(half, f32), shaped(half, bf16), shaped((1, width), f32)],
        [grad_resid_ffn, chip, tie(across(chip), rest_sent, out_chip), resid_mid, rows],
        us=1,
    )
    (enc_part,) = run(
        lambda *refs: enc_body(group, *refs),
        [shaped((enc_rows, width), bf16)],
        [rest_w, grad_encs[0], *grad_encs[1:]],
        us=1,
    )
    enc_chip = (enc_part.astype(f32) + sibling(enc_part).astype(f32)).astype(bf16)
    enc_far = across(enc_chip)
    self_other = sibling(self_own)
    out_far = across(tie(out_chip[1].astype(bf16), self_own))
    kv_shape = (token_rows, 2 * cols)
    top, ds_trunk, ds_near, grad_own, *remote = run(
        lambda *refs: self_back_body(block, heads, group, *refs),
        [
            shaped((token_rows, width), bf16), shaped((heads, TRUNK_BLKS * block, token_rows), bf16),
            shaped((heads, 2, block, token_rows), bf16), shaped(kv_shape, f32),
        ]
        + [shaped(kv_shape, bf16)] * hops_back,
        [scalars, self_own, self_other, q, attn, lse, *parts, w_o],
        [pltpu.VMEM((buffer_rows, 2 * cols), bf16), pltpu.VMEM((buffer_rows, 2 * cols), f32)],
        us=8,
    )
    back = [
        lax.ppermute(one, "dp", [(b, a) for a, b in later(d)]) for one, d in zip(remote, range(hops_back, 0, -1))
    ]
    sum_q, sum_o, grad_act = run(
        lambda *refs: self_rest_body(block, heads, group, *refs),
        [shaped((width, cols), f32), shaped((width, cols), f32), shaped((token_rows, width), f32)],
        [scalars, act_self, top, attn, ds_trunk, ds_near, *parts, part(qkv_w, cols, 0)],
        [pltpu.VMEM((token_rows, cols), bf16), pltpu.VMEM((buffer_rows, 2 * cols), bf16)],
        us=4,
    )
    held = rest_chain.step(grad_act)
    grad_own = tie(grad_own, held)
    split = (count // 2, shard, 4 * cols)
    self_kept, self_sent, kept, sent = run(
        lambda *refs: self_end_body(group, *refs),
        [shaped(split, bf16), shaped(split, bf16), shaped(half, f32), shaped(half, bf16)],
        [
            scalars, slots, act_self, grad_own, *back, part(qkv_w, cols, 1), part(qkv_w, cols, 2), sum_q, sum_o, grad_act,
        ],
        [pltpu.VMEM(kv_shape, bf16), pltpu.VMEM((count, shard, 4 * cols), bf16)],
        us=3,
    )
    self_chain = Halving(self_kept, self_sent)
    chip = chip_sum(kept, sent)
    (vectors,) = run(
        lambda *refs: vector_body(tensor, trees, *refs),
        [shaped((count * tensor, -(-(3 + trees) // 8) * 8, shard), f32)],
        [scalars, tie(kept, chip), sent, tokens_half, tokens_other, grad_resid_mid, rows, dgain_cross, dgain_ffn],
    )
    received = lax.all_to_all(vectors, ("dp", "tensor"), 0, 0)
    (grad_in,) = run(
        last_body,
        [shaped((own_rows, width), f32)],
        [chip, across(chip[1].astype(bf16)), tokens_in, grad_resid_mid, rows],
        us=1,
    )
    self_chain.step()
    rest_chain.step(sent)
    output = (resid_ffn[0] + (out_chip[0] + out_far.astype(f32))).astype(bf16)
    grad_enc = enc_chip.astype(f32) + enc_far.astype(f32)
    self_sums, rest_sums = self_chain.end(), rest_chain.end()
    gains, grad_table = run(
        lambda *refs: small_body(trees, *refs),
        [shaped((8, shard), f32), shaped((time_table.shape[0], shard), f32)],
        [timesteps, received],
        us=1,
    )
    square = shaped((shard, cols), f32)
    gq, gk, gv, go = run(finish_pair_body, [square] * 4, [*self_sums], us=1)
    wide = shaped((shard, hidden_cols), f32)
    gcq, gck, gcv, gco, gup, gdown = run(finish_pair_body, [square] * 4 + [wide] * 2, [*rest_sums], us=1)
    return (
        output, grad_in, grad_enc, grad_table, gains[0], gq, gk, gv, go.T, gains[1],
        gcq, gck, gcv, gco.T, gains[2], gup, gdown.T,
    )


def solution(mesh):
    rows, cols, repl = P(("dp", "tensor"), None), P("dp", "tensor"), P("tensor", "dp")
    in_specs = (
        rows, rows, P("dp", None), P("dp"), P("dp"), P(), P(None, "dp"), P("dp"), cols, cols, cols, repl,
        P("dp"), cols, cols, cols, repl, P("dp"), cols, repl,
    )
    out_specs = (
        rows, rows, P("dp", None), P(None, "dp"), P("dp"), cols, cols, cols, repl, P("dp"), cols, cols, cols,
        repl, P("dp"), cols, repl,
    )
    return jax.shard_map(on_device, mesh=mesh, in_specs=in_specs, out_specs=out_specs, check_vma=False)
```
